32 devices in a mesh: frm: 4 (over z), pat: 8 (over y, x, core).
Axes of the slice: x: 2, y: 2, z: 4, core: 2. Of those that a mesh axis runs over, the one named last changes fastest.
Arguments:
- frames: float32 [4, 1024, 2048], P('frm', 'pat'), may hold values from -6 to 6
- shifts: float32 [4, 2], P('frm'), may hold values from -0.5 to 0.5
- coefficients: float32 [4, 256, 40], P('frm', 'pat'), may hold values from -0.9 to 0.9
- anchors: int32 [256, 2], P('pat'), may hold values from 0 to 1960, as said below
- assign: int32 [256], P('pat'), may hold values from 0 to 7, as said below
Outputs:
- new_coefficients: float32 [4, 256, 40], P('frm', 'pat')
- object_spectra: float32 [256, 2, 7744], P(('pat', 'frm'))
The draws below stay inside these ranges and needn't reach their ends.
Inputs may be any that keep to these rules, and one draw needn't show every extreme that they name: `anchors`: the anchor row of patch p lies in p // 32 * 128 to p // 32 * 128 + 127 and is at most 936; the anchor column is at most 1960. `assign`: among the 32 patches p of one value of p // 32, exactly 4 carry each group number.
All inputs are finite; a program needn't handle non-finite values.
Results may differ from the reference program's by a relative error of at most 0.0003.
Values sent between devices are 32-bit elements; how exact they have to be, the bound alone decides.
No kernel may reach another device: no remote copies, remote signals or barrier semaphores. Data moves between devices by JAX's collectives and lax.ppermute only.
A program may use at most 128 MiB of HBM per device.

```python
import math
import jax
import jax.numpy as jnp
from jax import lax

PATCH = 88
MODES = 40
ITERS = 2
COLS = 2048
SH = 128
PPS = 32
FRAMES = 4
ROWS = 1024
PATCHES = 256
N_PAT = 8


def draw_anchors(key, part):
    row_key, col_key = jax.random.split(jax.random.fold_in(key, 11))
    strip_index = jnp.arange(PATCHES, dtype=jnp.int32) // PPS
    lowest = strip_index * SH
    highest = jnp.minimum(lowest + SH, ROWS - PATCH + 1)
    offsets = jax.random.randint(row_key, (PATCHES,), 0, 1 << 20, dtype=jnp.int32)
    row_start = lowest + offsets % (highest - lowest)
    col_start = jax.random.randint(col_key, (PATCHES,), 0, COLS - PATCH + 1, dtype=jnp.int32)
    return jnp.stack([row_start, col_start], axis=1).astype(jnp.int32)


def draw_assign(key, part):
    per_group = PPS // N_PAT
    strip_keys = jax.random.split(jax.random.fold_in(key, 23), N_PAT)
    targets = jnp.arange(PPS, dtype=jnp.int32) // per_group

    def shuffle_strip(strip_key):
        return jax.random.permutation(strip_key, targets)
    return jax.vmap(shuffle_strip)(strip_keys).reshape(PATCHES).astype(jnp.int32)


def shard_levels(key, dims, cuts, least, top_value):
    gain, own = 1.0, jax.random.fold_in(key, 6)
    for axis_at, blocks in cuts:
        draws = jnp.exp(jax.random.uniform(jax.random.fold_in(own, axis_at), (blocks,), jnp.float32, least / len(cuts), top_value / len(cuts)))
        gain = gain * jnp.repeat(draws, dims[axis_at] // blocks).reshape([-1 if axis == axis_at else 1 for axis in range(len(dims))])
    return gain


def normal_values(rng, dims, width, most, shards=(), kind=jnp.bfloat16):
    drawn = jax.random.normal(rng, dims, jnp.float32) * width
    if len(shards) > 0:
        drawn = shard_levels(rng, dims, shards, -0.22, 0.18) * drawn
    return jnp.clip(drawn, min=-most, max=most).astype(kind)


def setup_inputs(seed: int = 0) -> dict:
    seeds = jax.random.split(jax.random.key(seed), 6)
    return {
        "frames": normal_values(seeds[0], (FRAMES, ROWS, COLS), 1.0, 6.0, ((0, 4), (1, 8)), jnp.float32),
        "shifts": jnp.clip(jax.random.uniform(seeds[1], (FRAMES, 2), jnp.float32, -0.5, 0.5) * shard_levels(seeds[1], (FRAMES, 2), ((0, 4),), -0.4, 0.0), -0.5, 0.5),
        "coefficients": normal_values(seeds[2], (FRAMES, PATCHES, MODES), 0.15, 0.9, ((0, 4), (1, 8)), jnp.float32),
        "anchors": draw_anchors(jax.random.fold_in(seeds[5], 71), 0),
        "assign": draw_assign(jax.random.fold_in(seeds[5], 71), 0),
    }


damping = 0.05
step_size = 64.0

def noll_index(j):
    n = 0
    remaining = j - 1
    while remaining > n:
        n += 1
        remaining -= n
    m = (-1) ** j * (n % 2 + 2 * ((remaining + (n + 1) % 2) // 2))
    return (n, m)

def zernike_table(length, number):
    centre = length / 2.0
    coords = (jnp.arange(length, dtype=jnp.float32) - centre) / (length / 4.0)
    row_grid = jnp.broadcast_to(coords[:, None], (length, length))
    col_grid = jnp.broadcast_to(coords[None, :], (length, length))
    radius = jnp.sqrt(row_grid * row_grid + col_grid * col_grid)
    angle_grid = jnp.arctan2(row_grid, col_grid)
    inside = (radius <= 1.0).astype(jnp.float32)
    surfaces = []
    for j in range(2, number + 2):
        n, m = noll_index(j)
        order_abs = abs(m)
        radial = jnp.zeros((length, length), jnp.float32)
        for k in range((n - order_abs) // 2 + 1):
            factor = (-1) ** k * math.factorial(n - k) / (math.factorial(k) * math.factorial((n + order_abs) // 2 - k) * math.factorial((n - order_abs) // 2 - k))
            radial = radial + factor * radius ** (n - 2 * k)
        if m == 0:
            surface = math.sqrt(n + 1) * radial
        elif m > 0:
            surface = math.sqrt(2 * (n + 1)) * radial * jnp.cos(order_abs * angle_grid)
        else:
            surface = math.sqrt(2 * (n + 1)) * radial * jnp.sin(order_abs * angle_grid)
        surfaces.append(surface * inside)
    return (jnp.stack(surfaces), inside)

def window_table(length):
    ramp_index = jnp.arange(length, dtype=jnp.float32)
    profile = 0.5 - 0.5 * jnp.cos(2.0 * jnp.pi * (ramp_index + 0.5) / length)
    return profile[:, None] * profile[None, :]

def signed_frequencies(length):
    ramp_index = jnp.arange(length, dtype=jnp.int32)
    return ((ramp_index + length // 2) % length - length // 2).astype(jnp.float32)

def squared_modulus(values):
    return jnp.real(values) ** 2 + jnp.imag(values) ** 2

def solve_block(frames, shifts, zernike_modes, aperture, spread_scale, anchors_block, start_block):

    def cut_patch(anchor):
        return lax.dynamic_slice(frames, (anchor[0] * 0, anchor[0], anchor[1]), (FRAMES, PATCH, PATCH))
    blocks = jax.vmap(cut_patch)(anchors_block)
    spectra = jnp.fft.fft2(blocks * window_table(PATCH))
    frequencies = signed_frequencies(PATCH)
    ramp_angle = -2.0 * jnp.pi / PATCH * (frequencies[None, :, None] * shifts[:, 0, None, None] + frequencies[None, None, :] * shifts[:, 1, None, None])
    data_spectrum = spectra * jnp.exp(1j * ramp_angle)[None]
    energy = lax.optimization_barrier(jnp.sum(squared_modulus(data_spectrum), axis=(1, 2, 3)))
    current = start_block
    estimate = data_spectrum[:, 0]
    for iteration in range(ITERS):
        phases = jnp.einsum('pfm,mxy->pfxy', current, zernike_modes, precision=lax.Precision.HIGHEST)
        pupil_field = aperture * jnp.exp(1j * phases)
        focal_field = jnp.fft.fft2(pupil_field)
        spread = spread_scale * squared_modulus(focal_field)
        transfer = jnp.fft.fft2(spread)
        numerator = lax.optimization_barrier(jnp.sum(data_spectrum * jnp.conj(transfer), axis=1))
        denominator = lax.optimization_barrier(jnp.sum(squared_modulus(transfer), axis=1)) + damping
        estimate = numerator / denominator
        misfit = data_spectrum - estimate[:, None] * transfer
        grad_transfer = -2.0 * jnp.conj(estimate)[:, None] * misfit
        grad_spread = jnp.real(jnp.fft.ifft2(grad_transfer)) * (PATCH * PATCH)
        grad_focal = 2.0 * spread_scale * grad_spread * focal_field
        grad_pupil = jnp.fft.ifft2(grad_focal) * (PATCH * PATCH)
        grad_phase = jnp.imag(grad_pupil * jnp.conj(pupil_field))
        grad_coef = jnp.einsum('pfxy,mxy->pfm', grad_phase, zernike_modes, precision=lax.Precision.HIGHEST)
        current = current - step_size * FRAMES * grad_coef / energy[:, None, None]
    return (current, jnp.real(estimate), jnp.imag(estimate))

def reference(frames, shifts, coefficients, anchors, assign):
    zernike_modes, aperture = zernike_table(PATCH, MODES)
    spread_scale = 1.0 / (PATCH * PATCH * jnp.sum(aperture))
    blocks_anchor = anchors.reshape(N_PAT, PPS, 2)
    blocks_start = jnp.transpose(coefficients, (1, 0, 2)).reshape(N_PAT, PPS, FRAMES, MODES)

    def per_strip(pieces):
        return solve_block(frames, shifts, zernike_modes, aperture, spread_scale, pieces[0], pieces[1])
    finals, estimate_real, estimate_imag = lax.map(per_strip, (blocks_anchor, blocks_start))
    new_coefficients = jnp.transpose(finals.reshape(PATCHES, FRAMES, MODES), (1, 0, 2))
    ordering = jnp.argsort(assign * PATCHES + jnp.arange(PATCHES, dtype=jnp.int32))
    estimates = jnp.stack([estimate_real.reshape(PATCHES, PATCH * PATCH), estimate_imag.reshape(PATCHES, PATCH * PATCH)], axis=1)
    object_spectra = estimates[ordering] / PATCH
    return (new_coefficients, object_spectra)
```

```python
import functools
import math

import jax
import jax.numpy as jnp
import ml_dtypes
import numpy as np
from jax import lax
from jax.experimental import pallas as pl
from jax.experimental.pallas import tpu as pltpu
from jax.sharding import PartitionSpec as P

PATCH = 88
MODES = 40
ITERS = 2

BOX = 48
HALF = 48
MPAD = 48
LANES = 128
PACK = 64
FULL = 96

damping = 0.05
step_size = 64.0
f32 = jnp.float32
bf16 = jnp.bfloat16


def noll_index(j):
    n = 0
    remaining = j - 1
    while remaining > n:
        n += 1
        remaining -= n
    m = (-1) ** j * (n % 2 + 2 * ((remaining + (n + 1) % 2) // 2))
    return (n, m)


def zernike_table(length, number):
    centre = length / 2.0
    coords = (np.arange(length) - centre) / (length / 4.0)
    rows, cols = np.meshgrid(coords, coords, indexing="ij")
    radius = np.sqrt(rows * rows + cols * cols)
    angle = np.arctan2(rows, cols)
    inside = (radius <= 1.0).astype(np.float64)
    surfaces = []
    for j in range(2, number + 2):
        n, m = noll_index(j)
        order = abs(m)
        radial = np.zeros((length, length))
        for k in range((n - order) // 2 + 1):
            factor = (
                (-1) ** k
                * math.factorial(n - k)
                / (
                    math.factorial(k)
                    * math.factorial((n + order) // 2 - k)
                    * math.factorial((n - order) // 2 - k)
                )
            )
            radial = radial + factor * radius ** (n - 2 * k)
        if m == 0:
            surface = math.sqrt(n + 1) * radial
        elif m > 0:
            surface = math.sqrt(2 * (n + 1)) * radial * np.cos(order * angle)
        else:
            surface = math.sqrt(2 * (n + 1)) * radial * np.sin(order * angle)
        surfaces.append(surface * inside)
    return (np.stack(surfaces), inside)


def split_table(table):
    table = np.asarray(table, np.float32)
    high = table.astype(ml_dtypes.bfloat16)
    low = (table - high.astype(np.float32)).astype(ml_dtypes.bfloat16)
    return np.stack([high, low])


@functools.lru_cache(None)
def tables():
    n = PATCH
    start = n // 2 - n // 4
    grid = np.arange(n)
    full = np.zeros(LANES, np.int64)
    full[:n] = grid
    full[n] = n // 2
    full_ok = np.zeros(LANES)
    full_ok[: n + 1] = 1.0
    box = start + np.arange(BOX)
    half = np.arange(HALF)
    half_ok = (half <= n // 2).astype(np.float64)
    ang = lambda a, b: 2.0 * np.pi * (np.multiply.outer(a, b) % n) / n
    t = ang(box, grid)
    ta = np.zeros((LANES, 2 * LANES))
    ta[:BOX, :n] = np.cos(t)
    ta[64 : 64 + BOX, :n] = np.sin(t)
    ta[:BOX, LANES : LANES + n] = -np.sin(t)
    ta[64 : 64 + BOX, LANES : LANES + n] = np.cos(t)
    t = ang(grid, box)
    tb = np.concatenate([np.cos(t), -np.sin(t)], axis=0)
    t = ang(half, grid)
    tc1 = np.zeros((2 * HALF, FULL))
    tc1[:HALF, :n] = np.cos(t) * half_ok[:, None]
    tc1[HALF:, :n] = -np.sin(t) * half_ok[:, None]
    t = ang(grid, full)
    tc2 = np.zeros((LANES, 2 * LANES))
    tc2[:n, :LANES] = np.cos(t) * full_ok
    tc2[:n, LANES:] = -np.sin(t) * full_ok
    tf1 = np.zeros((LANES, 2 * LANES))
    tf1[:, :n] = (np.cos(t) * full_ok).T
    tf1[:, LANES : LANES + n] = (np.sin(t) * full_ok).T
    t = ang(grid, half)
    tf2 = np.concatenate([np.cos(t) * half_ok, -np.sin(t) * half_ok], axis=1)
    t = ang(box, grid)
    tg1 = np.zeros((2 * BOX, FULL))
    tg1[:BOX, :n] = np.cos(t)
    tg1[BOX:, :n] = np.sin(t)
    t = ang(grid, box)
    tg2 = np.zeros((2 * LANES, LANES))
    tg2[:n, :BOX] = np.sin(t)
    tg2[LANES : LANES + n, :BOX] = np.cos(t)
    tg2[:n, 64 : 64 + BOX] = -np.cos(t)
    tg2[LANES : LANES + n, 64 : 64 + BOX] = np.sin(t)
    modes, inside = zernike_table(n, MODES)
    z = np.zeros((BOX, MPAD, LANES))
    mask = np.zeros((BOX, LANES))
    width = min(BOX, n - start)
    cut = slice(start, start + width)
    for off in (0, 64):
        z[:width, :MODES, off : off + width] = np.transpose(modes[:, cut, cut], (1, 0, 2))
        mask[:width, off : off + width] = inside[cut, cut]
    zs = split_table(z)
    ztab = np.concatenate([zs[0], zs[1]], axis=1)
    scale = 1.0 / (n * n * inside.sum())
    profile = 0.5 - 0.5 * np.cos(2.0 * np.pi * (grid + 0.5) / n)
    window = np.zeros((n, LANES), np.float32)
    window[:, :n] = profile[:, None] * profile[None, :]
    weight = np.zeros((HALF, LANES), np.float32)
    weight[0, :n] = 1.0
    weight[n // 2, :n] = 1.0
    weight[1 : n // 2, : n + 1] = 2.0
    weight[1 : n // 2, n // 2] = 1.0
    weight[1 : n // 2, n] = 1.0
    fu = np.where(half < n // 2, half, -half) * half_ok
    fv = np.where(full < n // 2, full, full - n) * full_ok
    fv[n] = n // 2
    freq = np.zeros((2, HALF, LANES), np.float32)
    freq[0] = fu[:, None] * (-2.0 * np.pi / n)
    freq[1] = fv[None, :] * (-2.0 * np.pi / n)
    return dict(
        ta=split_table(ta),
        tb=split_table(tb),
        tc1=split_table(tc1),
        tc2=split_table(tc2),
        tf1=split_table(tf1),
        tf2=split_table(tf2),
        tg1=split_table(tg1),
        tg2=split_table(tg2),
        z=ztab,
        mask=mask.astype(np.float32),
        window=window,
        weight=weight,
        freq=freq,
        scale=float(scale),
    )


def split(x):
    high = x.astype(bf16)
    low = (x - high.astype(f32)).astype(bf16)
    return high, low


def mm(a, b):
    return jnp.dot(a, b, preferred_element_type=f32)


def left(table_ref, x):
    high, low = split(x)
    return mm(table_ref[0], high) + mm(table_ref[1], high) + mm(table_ref[0], low)


def right(x, table_ref):
    high, low = split(x)
    return mm(high, table_ref[0]) + mm(low, table_ref[0]) + mm(high, table_ref[1])


def quadrant_cos(x, offset):
    turns = jnp.floor(x * (2.0 / math.pi) + 0.5)
    r = x - turns * 1.5703125
    r = r - turns * 4.837512969970703125e-4
    r = r - turns * 7.54978995489188216e-8
    r2 = r * r
    s = r + r * r2 * (-1.6666654611e-1 + r2 * (8.3321608736e-3 + r2 * -1.9515295891e-4))
    c = (
        1.0
        - 0.5 * r2
        + r2 * r2 * (4.166664568298827e-2 + r2 * (-1.388731625493765e-3 + r2 * 2.443315711809948e-5))
    )
    k = turns.astype(jnp.int32) - offset
    value = jnp.where((k & 1) == 0, c, s)
    return jnp.where(((k + 1) & 2) == 0, value, -value)


def lane_offset(shape):
    return (lax.broadcasted_iota(jnp.int32, shape, len(shape) - 1) >= 64).astype(jnp.int32)


def pupil_and_columns(current, z_ref, mask_ref, ta_ref, pupil_ref, cols_ref):
    items = current.shape[0]
    doubled = current + pltpu.roll(current, MPAD, 1)
    high, low = split(doubled[:, : 2 * MPAD])
    stacked = jnp.concatenate([high, low], axis=0)
    offset = lane_offset((items, LANES))

    def one_row(row, carry):
        both = mm(stacked, z_ref[row])
        phase = both[:items] + both[items:]
        pupil = quadrant_cos(phase, offset) * mask_ref[pl.ds(row, 1), :]
        pupil_ref[pl.ds(pl.multiple_of(row * items, 8), items), :] = pupil
        return carry

    lax.fori_loop(0, BOX, one_row, 0, unroll=4)
    chunk = BOX * items // 6

    def one_chunk(i, carry):
        rows = pl.ds(pl.multiple_of(i * chunk, 8), chunk)
        wide = right(pupil_ref[rows, :], ta_ref)
        cols_ref[0, rows, :] = wide[:, :LANES]
        cols_ref[1, rows, :] = wide[:, LANES:]
        return carry

    lax.fori_loop(0, 6, one_chunk, 0)


def half_spectrum(planes, tc1_ref, tc2_ref):
    rows = []
    pad = jnp.zeros((FULL - PATCH, 2 * LANES), f32)
    for i in range(0, len(planes), 2):
        pair = planes[i : i + 2]
        if len(pair) == 1:
            pair = pair * 2
        both = left(tc1_ref, jnp.concatenate([jnp.concatenate(pair, axis=1), pad], axis=0))
        rows.append(both[:, :LANES])
        rows.append(both[:, LANES:])
    rows = rows[: len(planes)]
    spread = right(jnp.concatenate(rows, axis=0), tc2_ref)
    result = []
    for i in range(len(planes)):
        top = spread[2 * HALF * i : 2 * HALF * i + HALF]
        bottom = spread[2 * HALF * i + HALF : 2 * HALF * (i + 1)]
        result.append(
            (
                top[:, :LANES] - bottom[:, LANES:],
                top[:, LANES:] + bottom[:, :LANES],
            )
        )
    return result


def transfers(scale, frames, patches, p, tb_ref, tc1_ref, tc2_ref, cols_ref, focal_ref):
    items = frames * patches
    planes = []
    for f in range(frames):
        item = f * patches + p
        cols = jnp.concatenate(
            [
                cols_ref[0, pl.ds(item, BOX, stride=items), :],
                cols_ref[1, pl.ds(item, BOX, stride=items), :],
            ],
            axis=1,
        )
        both = left(tb_ref, cols)
        real = both[:PATCH, :LANES] - both[PATCH:, LANES:]
        imag = both[:PATCH, LANES:] + both[PATCH:, :LANES]
        focal_ref[item, :, :LANES] = real
        focal_ref[item, :, LANES:] = imag
        planes.append(scale * (real * real + imag * imag))
    return half_spectrum(planes, tc1_ref, tc2_ref)


def estimate_of(data, transfer):
    cross_real = sum(d[0] * t[0] + d[1] * t[1] for d, t in zip(data, transfer))
    cross_imag = sum(d[1] * t[0] - d[0] * t[1] for d, t in zip(data, transfer))
    power = sum(t[0] * t[0] + t[1] * t[1] for t in transfer) + damping
    return cross_real / power, cross_imag / power


def gradient_of(data, transfer, est, weight):
    er, ei = est
    grads = []
    for d, t in zip(data, transfer):
        mr = d[0] - (er * t[0] - ei * t[1])
        mi = d[1] - (er * t[1] + ei * t[0])
        grads.append((-2.0 * weight * (er * mr + ei * mi), -2.0 * weight * (er * mi - ei * mr)))
    return grads


def back_to_pupil(scale, frames, patches, p, grads, tf1_ref, tf2_ref, tg1_ref, tg2_ref, focal_ref, back_ref):
    items = frames * patches
    stacked = jnp.concatenate([plane for pair in grads for plane in pair], axis=0)
    wide = right(stacked, tf1_ref)
    columns = []
    for f in range(frames):
        top = wide[2 * HALF * f : 2 * HALF * f + HALF]
        bottom = wide[2 * HALF * f + HALF : 2 * HALF * (f + 1)]
        columns.append(
            jnp.concatenate(
                [top[:, :LANES] - bottom[:, LANES:], top[:, LANES:] + bottom[:, :LANES]], axis=0
            )
        )
    pad = jnp.zeros((FULL - PATCH, 2 * LANES), f32)
    halves = []
    for f in range(0, frames, 2):
        pair = columns[f : f + 2]
        if len(pair) == 1:
            pair = pair * 2
        both = left(tf2_ref, jnp.concatenate(pair, axis=1))
        for g in range(f, min(f + 2, frames)):
            spread = both[:, (g - f) * LANES : (g - f + 1) * LANES] * (2.0 * scale)
            item = g * patches + p
            field = focal_ref[item] * jnp.concatenate([spread, spread], axis=1)
            rows = left(tg1_ref, jnp.concatenate([field, pad], axis=0))
            halves.append(
                jnp.concatenate(
                    [
                        rows[:BOX, :LANES] - rows[BOX:, LANES:],
                        rows[:BOX, LANES:] + rows[BOX:, :LANES],
                    ],
                    axis=1,
                )
            )
    back = right(jnp.concatenate(halves, axis=0), tg2_ref)
    for f in range(frames):
        item = f * patches + p
        back_ref[pl.ds(item, BOX, stride=items), :] = back[f * BOX : (f + 1) * BOX]


def coefficient_gradient(items, z_ref, pupil_ref, back_ref):
    def one_row(row, total):
        rows = pl.ds(pl.multiple_of(row * items, 8), items)
        high, low = split(pupil_ref[rows, :] * back_ref[rows, :])
        stacked = jnp.concatenate([high, low], axis=0)
        return total + lax.dot_general(
            stacked, z_ref[row], (((1,), (1,)), ((), ())), preferred_element_type=f32
        )

    total = lax.fori_loop(
        0, BOX, one_row, jnp.zeros((2 * items, 2 * MPAD), f32), unroll=4
    )
    total = total[:items] + total[items:]
    total = jnp.concatenate([total, jnp.zeros((items, LANES - 2 * MPAD), f32)], axis=1)
    total = total + pltpu.roll(total, LANES - MPAD, 1)
    lane = lax.broadcasted_iota(jnp.int32, total.shape, 1)
    return jnp.where(lane < MPAD, total, 0.0)


def unpack_pixels(packed):
    lane = lax.broadcasted_iota(jnp.int32, (PACK - 40, LANES), 1)
    third = jnp.concatenate(
        [pltpu.roll(packed[48:56], LANES - 8 - 8 * t, 1) for t in range(3)], axis=0
    )
    rest = jnp.where(
        lane < 40,
        pltpu.roll(packed[:24], 40, 1),
        jnp.where(lane < 80, pltpu.roll(packed[24:48], 80, 1), third),
    )
    return jnp.concatenate([packed, rest], axis=0)


def first_kernel(scale, frames, patches, *refs):
    start = refs[:frames]
    z_ref, mask_ref, ta_ref, tb_ref, tc1_ref, tc2_ref = refs[frames : frames + 6]
    pupil_ref, focal_ref, transfer_ref, cols_ref = refs[frames + 6 :]
    lane = lax.broadcasted_iota(jnp.int32, (frames * patches, LANES), 1)
    current = jnp.concatenate([s[...] for s in start], axis=0)
    current = jnp.where(lane < MPAD, current, 0.0)
    pupil_and_columns(current, z_ref, mask_ref, ta_ref, pupil_ref, cols_ref)

    def one_patch(p, carry):
        result = transfers(
            scale, frames, patches, p, tb_ref, tc1_ref, tc2_ref, cols_ref, focal_ref
        )
        for f in range(frames):
            transfer_ref[f * patches + p, :HALF, :] = result[f][0]
            transfer_ref[f * patches + p, HALF:, :] = result[f][1]
        return carry

    lax.fori_loop(0, patches, one_patch, 0)


def middle_kernel(scale, frames, patches, *refs):
    start = refs[:frames]
    pixels = refs[frames : 2 * frames]
    (
        pupil_ref,
        focal_ref,
        transfer_ref,
        z_ref,
        mask_ref,
        ta_ref,
        tb_ref,
        tc1_ref,
        tc2_ref,
        tf1_ref,
        tf2_ref,
        tg1_ref,
        tg2_ref,
        window_ref,
        weight_ref,
        freq_ref,
    ) = refs[2 * frames : 2 * frames + 16]
    (
        pupil_out,
        focal_out,
        grads_out,
        current_out,
        energy_out,
        estimate_out,
        data_ref,
        cols_ref,
        back_ref,
        ramp_ref,
    ) = refs[2 * frames + 16 :]
    items = frames * patches
    lane = lax.broadcasted_iota(jnp.int32, (items, LANES), 1)
    for f in range(frames):
        s = start[f][pl.ds(0, 1), :]
        angle = freq_ref[0] * s[:, MPAD : MPAD + 1] + freq_ref[1] * s[:, MPAD + 1 : MPAD + 2]
        zero = jnp.zeros(angle.shape, jnp.int32)
        ramp_ref[f, 0] = quadrant_cos(angle, zero)
        ramp_ref[f, 1] = quadrant_cos(angle, zero + 1)

    def one_patch(p, carry):
        weight = weight_ref[...]
        planes = [unpack_pixels(pixels[f][p]) * window_ref[...] for f in range(frames)]
        spectra = half_spectrum(planes, tc1_ref, tc2_ref)
        data = []
        total = None
        for f in range(frames):
            real, imag = spectra[f]
            cr, ci = ramp_ref[f, 0], ramp_ref[f, 1]
            dr, di = real * cr - imag * ci, real * ci + imag * cr
            data.append((dr, di))
            data_ref[f * patches + p, :HALF, :] = dr
            data_ref[f * patches + p, HALF:, :] = di
            part = weight * (dr * dr + di * di)
            total = part if total is None else total + part
        energy = jnp.sum(jnp.sum(total, axis=0, keepdims=True), axis=1, keepdims=True)
        for f in range(frames):
            energy_out[pl.ds(f * patches + p, 1), :] = jnp.broadcast_to(energy, (1, LANES))
        transfer = [
            (transfer_ref[f * patches + p, :HALF, :], transfer_ref[f * patches + p, HALF:, :])
            for f in range(frames)
        ]
        est = estimate_of(data, transfer)
        grads = gradient_of(data, transfer, est, weight)
        back_to_pupil(
            scale, frames, patches, p, grads, tf1_ref, tf2_ref, tg1_ref, tg2_ref, focal_ref, back_ref
        )
        return carry

    lax.fori_loop(0, patches, one_patch, 0)
    current = jnp.concatenate([s[...] for s in start], axis=0)
    current = jnp.where(lane < MPAD, current, 0.0)
    grad = coefficient_gradient(items, z_ref, pupil_ref, back_ref)
    current = current - step_size * frames * grad / energy_out[...]
    current_out[...] = current
    pupil_and_columns(current, z_ref, mask_ref, ta_ref, pupil_out, cols_ref)

    def next_patch(p, carry):
        weight = weight_ref[...]
        transfer = transfers(
            scale, frames, patches, p, tb_ref, tc1_ref, tc2_ref, cols_ref, focal_out
        )
        data = [
            (data_ref[f * patches + p, :HALF, :], data_ref[f * patches + p, HALF:, :])
            for f in range(frames)
        ]
        est = estimate_of(data, transfer)
        estimate_out[p, 0] = est[0] * (1.0 / PATCH)
        estimate_out[p, 1] = est[1] * (1.0 / PATCH)
        grads = gradient_of(data, transfer, est, weight)
        for f in range(frames):
            grads_out[f * patches + p, :HALF, :] = grads[f][0]
            grads_out[f * patches + p, HALF:, :] = grads[f][1]
        return carry

    lax.fori_loop(0, patches, next_patch, 0)


def last_kernel(scale, frames, patches, *refs):
    (
        pupil_ref,
        focal_ref,
        grads_ref,
        current_ref,
        energy_ref,
        z_ref,
        tf1_ref,
        tf2_ref,
        tg1_ref,
        tg2_ref,
    ) = refs[:10]
    outs = refs[10 : 10 + frames]
    (back_ref,) = refs[10 + frames :]
    items = frames * patches

    def one_patch(p, carry):
        grads = [
            (grads_ref[f * patches + p, :HALF, :], grads_ref[f * patches + p, HALF:, :])
            for f in range(frames)
        ]
        back_to_pupil(
            scale, frames, patches, p, grads, tf1_ref, tf2_ref, tg1_ref, tg2_ref, focal_ref, back_ref
        )
        return carry

    lax.fori_loop(0, patches, one_patch, 0)
    grad = coefficient_gradient(items, z_ref, pupil_ref, back_ref)
    current = current_ref[...] - step_size * frames * grad / energy_ref[...]
    for f in range(frames):
        outs[f][...] = current[f * patches : (f + 1) * patches]


def slot_fields(axes, count):
    frames, strips = axes
    per = count // strips
    splits = frames // per
    return per, splits, strips // splits


def slot_of(axes, count, me, group, rank):
    frames = axes[0]
    per, splits, block = slot_fields(axes, count)
    owner = rank * splits + lax.div(group, block)
    relative = lax.rem(owner - me + frames, frames)
    return relative * block + lax.rem(group, block)


def fill_slots(axes, count, assign_ref, counts_ref, visit):
    me = lax.axis_index("frm")
    for g in range(axes[1]):
        counts_ref[g] = 0

    def one(p, carry):
        group = assign_ref[p]
        rank = counts_ref[group]
        counts_ref[group] = rank + 1
        visit(p, slot_of(axes, count, me, group, rank))
        return carry

    lax.fori_loop(0, count, one, 0)


def prepare_kernel(axes, count, assign_ref, shifts_ref, coefs_ref, *refs):
    frames = axes[0]
    outs, (sorted_ref, counts_ref) = refs[:frames], refs[frames:]
    modes = coefs_ref.shape[-1]
    patches = count // frames
    sorted_ref[...] = jnp.zeros(sorted_ref.shape, f32)

    def visit(p, slot):
        sorted_ref[pl.ds(slot, 1), :modes] = coefs_ref[pl.ds(p, 1), :]

    fill_slots(axes, count, assign_ref, counts_ref, visit)
    lane = lax.broadcasted_iota(jnp.int32, (patches, LANES), 1)
    for f in range(frames):
        rows = sorted_ref[f * patches : (f + 1) * patches, :]
        rows = jnp.where(lane == MPAD, shifts_ref[0, 0], rows)
        outs[f][...] = jnp.where(lane == MPAD + 1, shifts_ref[0, 1], rows)


def cut_kernel(axes, count, assign_ref, anchors_ref, strip_ref, below_ref, *refs):
    frames = axes[0]
    outs, (tall_ref, counts_ref, order_ref) = refs[:frames], refs[frames:]
    patches = count // frames
    height, width = strip_ref.shape
    tall_ref[:height, :width] = strip_ref[...]
    tall_ref[height : height + PATCH, :width] = below_ref[...]
    first = lax.axis_index("pat") * height

    def visit(p, slot):
        order_ref[slot] = p

    fill_slots(axes, count, assign_ref, counts_ref, visit)
    lane = lax.broadcasted_iota(jnp.int32, (24, LANES), 1)
    for f in range(frames):

        def one(j, carry):
            p = order_ref[f * patches + j]
            row = anchors_ref[p, 0] - first
            col = anchors_ref[p, 1]
            tile = lax.div(col, LANES)
            base = pl.multiple_of(tile * LANES, LANES)
            above = pl.multiple_of(lax.div(row, 8) * 8, 8)
            block = tall_ref[pl.ds(above, FULL), pl.ds(base, 2 * LANES)]
            back = lax.rem(2 * LANES - (col - base), 2 * LANES)
            block = pltpu.roll(block, back, 1)[:, :LANES]
            block = pltpu.roll(block, lax.rem(FULL - (row - above), FULL), 0)[:PATCH]
            rest = block[PACK:]
            outs[f][j, 0:24, :] = jnp.where(lane < 88, block[0:24], pltpu.roll(rest, 88, 1))
            outs[f][j, 24:48, :] = jnp.where(lane < 88, block[24:48], pltpu.roll(rest, 48, 1))
            third = jnp.where(
                lane[:8] < 96,
                pltpu.roll(rest[:8], 8, 1),
                jnp.where(
                    lane[:8] < 104, pltpu.roll(rest[8:16], 16, 1), pltpu.roll(rest[16:24], 24, 1)
                ),
            )
            outs[f][j, 48:56, :] = jnp.where(lane[:8] < 88, block[48:56], third)
            outs[f][j, 56:64, :] = block[56:64]
            return carry

        lax.fori_loop(0, patches, one, 0, unroll=2)


def restore_kernel(axes, count, assign_ref, *refs):
    frames = axes[0]
    parts, (out_ref, all_ref, counts_ref) = refs[:frames], refs[frames:]
    patches = count // frames
    modes = out_ref.shape[-1]
    for f in range(frames):
        all_ref[f * patches : (f + 1) * patches, :] = parts[f][...]

    def visit(p, slot):
        out_ref[pl.ds(p, 1), :] = all_ref[pl.ds(slot, 1), :modes]

    fill_slots(axes, count, assign_ref, counts_ref, visit)


def call(body, outs, scratch, operands, smem=0, name=None):
    vmem = pl.BlockSpec(memory_space=pltpu.VMEM)
    scalar = pl.BlockSpec(memory_space=pltpu.SMEM)
    return pl.pallas_call(
        body,
        out_shape=[jax.ShapeDtypeStruct(s, f32) for s in outs],
        in_specs=[scalar] * smem + [vmem] * (len(operands) - smem),
        out_specs=[vmem] * len(outs),
        scratch_shapes=scratch,
        name=name,
    )(*operands)


def around(value, axis, steps):
    count = lax.axis_size(axis)
    return lax.ppermute(value, axis, [(s, (s + steps) % count) for s in range(count)])


def shards(frames, shifts, coefficients, anchors, assign):
    t = tables()
    scale = t["scale"]
    c = {k: jnp.asarray(v) for k, v in t.items() if k != "scale"}
    height = frames.shape[1]
    width = frames.shape[2]
    count = assign.shape[0]
    n_frm = lax.axis_size("frm")
    n_pat = lax.axis_size("pat")
    axes = (n_frm, n_pat)
    patches = count // n_frm
    items = n_frm * patches
    per, splits, block = slot_fields(axes, count)

    below = lax.ppermute(
        frames[0, :PATCH, :], "pat", [(s, s - 1) for s in range(1, n_pat)]
    )
    ready = call(
        functools.partial(prepare_kernel, axes, count),
        [(patches, LANES)] * n_frm,
        [pltpu.VMEM((count, LANES), f32), pltpu.SMEM((n_pat,), jnp.int32)],
        [assign, shifts, coefficients[0]],
        smem=2,
        name="prepare",
    )
    start = [ready[0]] + [around(ready[r], "frm", r) for r in range(1, n_frm)]

    pupil, focal, transfer = call(
        functools.partial(first_kernel, scale, n_frm, patches),
        [(BOX * items, LANES), (items, PATCH, 2 * LANES), (items, 2 * HALF, LANES)],
        [pltpu.VMEM((2, BOX * items, LANES), f32)],
        start + [c["z"], c["mask"], c["ta"], c["tb"], c["tc1"], c["tc2"]],
        name="first",
    )
    cuts = call(
        functools.partial(cut_kernel, axes, count),
        [(patches, PACK, LANES)] * n_frm,
        [
            pltpu.VMEM((height + PATCH, width + LANES), f32),
            pltpu.SMEM((n_pat,), jnp.int32),
            pltpu.SMEM((count,), jnp.int32),
        ],
        [assign, anchors, frames[0], below],
        smem=2,
        name="cut",
    )
    pixels = [cuts[0]] + [around(cuts[r], "frm", r) for r in range(1, n_frm)]

    pupil, focal, grads, current, energy, estimate = call(
        functools.partial(middle_kernel, scale, n_frm, patches),
        [
            (BOX * items, LANES),
            (items, PATCH, 2 * LANES),
            (items, 2 * HALF, LANES),
            (items, LANES),
            (items, LANES),
            (patches, 2, HALF, LANES),
        ],
        [
            pltpu.VMEM((items, 2 * HALF, LANES), f32),
            pltpu.VMEM((2, BOX * items, LANES), f32),
            pltpu.VMEM((BOX * items, LANES), f32),
            pltpu.VMEM((n_frm, 2, HALF, LANES), f32),
        ],
        start
        + pixels
        + [pupil, focal, transfer]
        + [
            c[k]
            for k in (
                "z", "mask", "ta", "tb", "tc1", "tc2", "tf1", "tf2", "tg1", "tg2",
                "window", "weight", "freq",
            )
        ],
        name="middle",
    )

    me = lax.axis_index("frm")
    if splits > 1:
        slots = jnp.zeros((n_pat,) + estimate.shape[1:], f32)
        slots = lax.dynamic_update_slice(slots, estimate, (lax.rem(me, splits) * block, 0, 0, 0))
    else:
        slots = estimate
    slots = lax.all_to_all(slots, "pat", split_axis=0, concat_axis=0, tiled=True)
    slots = lax.all_to_all(slots, "frm", split_axis=0, concat_axis=0, tiled=True)
    strips = n_pat // n_frm
    slots = slots.reshape((per, splits, strips) + estimate.shape[1:])
    if splits > 1:
        slots = lax.dynamic_index_in_dim(
            slots, lax.div(lax.axis_index("pat"), block), 1, keepdims=False
        )
    else:
        slots = slots[:, 0]
    half = jnp.swapaxes(slots, 0, 1).reshape((strips * per,) + estimate.shape[1:])

    finals = call(
        functools.partial(last_kernel, scale, n_frm, patches),
        [(patches, LANES)] * n_frm,
        [pltpu.VMEM((BOX * items, LANES), f32)],
        [pupil, focal, grads, current, energy]
        + [c[k] for k in ("z", "tf1", "tf2", "tg1", "tg2")],
        name="last",
    )
    parts = [finals[0]] + [around(finals[r], "frm", -r) for r in range(1, n_frm)]
    (restored,) = call(
        functools.partial(restore_kernel, axes, count),
        [(count, MODES)],
        [pltpu.VMEM((count, LANES), f32), pltpu.SMEM((n_pat,), jnp.int32)],
        [assign] + parts,
        smem=1,
        name="restore",
    )
    new_coefficients = restored[None]

    mid = PATCH // 2
    top = half[:, :, : mid + 1, :PATCH]
    nyquist = half[:, :, 1:mid, PATCH : PATCH + 1]
    low = jnp.flip(half[:, :, 1:mid, :PATCH], axis=2)
    low_nyquist = jnp.flip(nyquist, axis=2)
    low = jnp.concatenate(
        [low[..., :1], jnp.flip(low[..., mid + 1 :], axis=3), low_nyquist, jnp.flip(low[..., 1:mid], axis=3)],
        axis=3,
    )
    low = low * jnp.array([1.0, -1.0], f32)[None, :, None, None]
    spectra = jnp.concatenate([top, low], axis=2)
    object_spectra = spectra.reshape(spectra.shape[0], 2, PATCH * PATCH)
    return (new_coefficients, object_spectra)


def solution(mesh):
    in_specs = (
        P("frm", "pat", None),
        P("frm", None),
        P("frm", "pat", None),
        P("pat", None),
        P("pat"),
    )
    out_specs = (P("frm", "pat", None), P(("pat", "frm"), None, None))
    return jax.shard_map(shards, mesh=mesh, in_specs=in_specs, out_specs=out_specs, check_vma=False)
```

```python
import functools
import math

import jax
import jax.numpy as jnp
import ml_dtypes
import numpy as np
from jax import lax
from jax.experimental import pallas as pl
from jax.experimental.pallas import tpu as pltpu
from jax.sharding import PartitionSpec as P

PATCH = 88
MODES = 40
ITERS = 2

BOX = 48
HALF = 48
MPAD = 48
LANES = 128
PACK = 64
FULL = 96

damping = 0.05
step_size = 64.0
f32 = jnp.float32
bf16 = jnp.bfloat16


def noll_index(j):
    n = 0
    remaining = j - 1
    while remaining > n:
        n += 1
        remaining -= n
    m = (-1) ** j * (n % 2 + 2 * ((remaining + (n + 1) % 2) // 2))
    return (n, m)


def zernike_table(length, number):
    centre = length / 2.0
    coords = (np.arange(length) - centre) / (length / 4.0)
    rows, cols = np.meshgrid(coords, coords, indexing="ij")
    radius = np.sqrt(rows * rows + cols * cols)
    angle = np.arctan2(rows, cols)
    inside = (radius <= 1.0).astype(np.float64)
    surfaces = []
    for j in range(2, number + 2):
        n, m = noll_index(j)
        order = abs(m)
        radial = np.zeros((length, length))
        for k in range((n - order) // 2 + 1):
            factor = (
                (-1) ** k
                * math.factorial(n - k)
                / (
                    math.factorial(k)
                    * math.factorial((n + order) // 2 - k)
                    * math.factorial((n - order) // 2 - k)
                )
            )
            radial = radial + factor * radius ** (n - 2 * k)
        if m == 0:
            surface = math.sqrt(n + 1) * radial
        elif m > 0:
            surface = math.sqrt(2 * (n + 1)) * radial * np.cos(order * angle)
        else:
            surface = math.sqrt(2 * (n + 1)) * radial * np.sin(order * angle)
        surfaces.append(surface * inside)
    return (np.stack(surfaces), inside)


def split_table(table):
    table = np.asarray(table, np.float32)
    high = table.astype(ml_dtypes.bfloat16)
    low = (table - high.astype(np.float32)).astype(ml_dtypes.bfloat16)
    return np.stack([high, low])


def left_table(table):
    high, low = split_table(table)
    return np.concatenate([high, low, high], axis=1)


@functools.lru_cache(None)
def tables():
    n = PATCH
    start = n // 2 - n // 4
    grid = np.arange(n)
    full = np.zeros(LANES, np.int64)
    full[:n] = grid
    full[n] = n // 2
    full_ok = np.zeros(LANES)
    full_ok[: n + 1] = 1.0
    box = start + np.arange(BOX)
    half = np.arange(HALF)
    half_ok = (half <= n // 2).astype(np.float64)
    ang = lambda a, b: 2.0 * np.pi * (np.multiply.outer(a, b) % n) / n
    t = ang(box, grid)
    ta = np.zeros((LANES, 2 * LANES))
    ta[:BOX, :n] = np.cos(t)
    ta[64 : 64 + BOX, :n] = np.sin(t)
    ta[:BOX, LANES : LANES + n] = -np.sin(t)
    ta[64 : 64 + BOX, LANES : LANES + n] = np.cos(t)
    t = ang(grid, box)
    tb = np.block([[np.cos(t), np.sin(t)], [-np.sin(t), np.cos(t)]])
    t = ang(half, grid)
    tc1 = np.zeros((2 * HALF, FULL))
    tc1[:HALF, :n] = np.cos(t) * half_ok[:, None]
    tc1[HALF:, :n] = -np.sin(t) * half_ok[:, None]
    t = ang(grid, full)
    tc2 = np.zeros((2 * LANES, 2 * LANES))
    tc2[:n, :LANES] = np.cos(t) * full_ok
    tc2[:n, LANES:] = -np.sin(t) * full_ok
    tc2[LANES : LANES + n, :LANES] = np.sin(t) * full_ok
    tc2[LANES : LANES + n, LANES:] = np.cos(t) * full_ok
    tf1 = tc2.T
    t = ang(grid, half)
    tf2 = np.concatenate([np.cos(t) * half_ok, -np.sin(t) * half_ok], axis=1)
    t = ang(box, grid)
    tg1 = np.block([[np.cos(t), -np.sin(t)], [np.sin(t), np.cos(t)]])
    t = ang(grid, box)
    tg2 = np.zeros((2 * LANES, LANES))
    tg2[:n, :BOX] = np.sin(t)
    tg2[LANES : LANES + n, :BOX] = np.cos(t)
    tg2[:n, 64 : 64 + BOX] = -np.cos(t)
    tg2[LANES : LANES + n, 64 : 64 + BOX] = np.sin(t)
    modes, inside = zernike_table(n, MODES)
    z = np.zeros((BOX, MPAD, LANES))
    mask = np.zeros((BOX, LANES))
    width = min(BOX, n - start)
    cut = slice(start, start + width)
    for off in (0, 64):
        z[:width, :MODES, off : off + width] = np.transpose(modes[:, cut, cut], (1, 0, 2))
        mask[:width, off : off + width] = inside[cut, cut]
    zs = split_table(z)
    ztab = np.concatenate([zs[0], zs[1]], axis=1)
    ztab = np.concatenate([ztab[0::2], ztab[1::2]], axis=2)
    scale = 1.0 / (n * n * inside.sum())
    profile = 0.5 - 0.5 * np.cos(2.0 * np.pi * (grid + 0.5) / n)
    window = np.zeros((n, LANES), np.float32)
    window[:, :n] = profile[:, None] * profile[None, :]
    weight = np.zeros((HALF, LANES), np.float32)
    weight[0, :n] = 1.0
    weight[n // 2, :n] = 1.0
    weight[1 : n // 2, : n + 1] = 2.0
    weight[1 : n // 2, n // 2] = 1.0
    weight[1 : n // 2, n] = 1.0
    fu = np.where(half < n // 2, half, -half) * half_ok
    fv = np.where(full < n // 2, full, full - n) * full_ok
    fv[n] = n // 2
    freq = np.zeros((2, HALF, LANES), np.float32)
    freq[0] = fu[:, None] * (-2.0 * np.pi / n)
    freq[1] = fv[None, :] * (-2.0 * np.pi / n)
    return dict(
        ta=split_table(ta),
        tb=left_table(tb),
        tc1=left_table(tc1),
        tc2=split_table(tc2),
        tf1=split_table(tf1),
        tf2=left_table(tf2),
        tg1=left_table(tg1),
        tg2=np.concatenate(list(split_table(tg2)), axis=1),
        z=ztab,
        mask=mask.astype(np.float32),
        window=window,
        weight=weight,
        freq=freq,
        scale=float(scale),
    )


def split(x):
    high = x.astype(bf16)
    low = (x - high.astype(f32)).astype(bf16)
    return high, low


def mm(a, b):
    return jnp.dot(a, b, preferred_element_type=f32)


def left(table_ref, x):
    high, low = split(x)
    return mm(table_ref[...], jnp.concatenate([high, high, low], axis=0))


def right(x, table_ref):
    high, low = split(x)
    table = jnp.concatenate([table_ref[0], table_ref[0], table_ref[1]], axis=0)
    return mm(jnp.concatenate([high, low, high], axis=1), table)


def quadrant_cos(x, offset):
    turns = jnp.floor(x * (2.0 / math.pi) + 0.5)
    r = x - turns * 1.5703125
    r = r - turns * 4.837512969970703125e-4
    r = r - turns * 7.54978995489188216e-8
    r2 = r * r
    s = r + r * r2 * (-1.6666654611e-1 + r2 * (8.3321608736e-3 + r2 * -1.9515295891e-4))
    c = (
        1.0
        - 0.5 * r2
        + r2 * r2 * (4.166664568298827e-2 + r2 * (-1.388731625493765e-3 + r2 * 2.443315711809948e-5))
    )
    k = turns.astype(jnp.int32) - offset
    value = jnp.where((k & 1) == 0, c, s)
    return jnp.where(((k + 1) & 2) == 0, value, -value)


def lane_offset(shape):
    return (lax.broadcasted_iota(jnp.int32, shape, len(shape) - 1) >= 64).astype(jnp.int32)


def pupil_and_columns(current, z_ref, mask_ref, ta_ref, pupil_ref, cols_ref):
    items = current.shape[0]
    doubled = current + pltpu.roll(current, MPAD, 1)
    high, low = split(doubled[:, : 2 * MPAD])
    stacked = jnp.concatenate([high, low], axis=0)
    offset = lane_offset((items, LANES))

    def two_rows(i, carry):
        both = mm(stacked, z_ref[i])
        phase = both[:items] + both[items:]
        for k in range(2):
            row = 2 * i + k
            pupil = quadrant_cos(phase[:, k * LANES : (k + 1) * LANES], offset)
            pupil = pupil * mask_ref[pl.ds(row, 1), :]
            pupil_ref[pl.ds(pl.multiple_of(row * items, 8), items), :] = pupil
        return carry

    lax.fori_loop(0, BOX // 2, two_rows, 0, unroll=4)
    steps = 4
    chunk = BOX * items // steps

    def one_chunk(i, carry):
        rows = pl.ds(pl.multiple_of(i * chunk, 8), chunk)
        wide = right(pupil_ref[rows, :], ta_ref)
        cols_ref[0, rows, :] = wide[:, :LANES]
        cols_ref[1, rows, :] = wide[:, LANES:]
        return carry

    lax.fori_loop(0, steps, one_chunk, 0)


def half_spectrum(pairs, frames, tc1_ref, tc2_ref):
    rows = []
    pad = jnp.zeros((FULL - PATCH, 2 * LANES), f32)
    for pair in pairs:
        both = left(tc1_ref, jnp.concatenate([pair, pad], axis=0))
        for k in range(2):
            lanes = slice(k * LANES, (k + 1) * LANES)
            rows.append(jnp.concatenate([both[:HALF, lanes], both[HALF:, lanes]], axis=1))
    spectra = right(jnp.concatenate(rows[:frames], axis=0), tc2_ref)
    return [spectra[HALF * f : HALF * (f + 1)] for f in range(frames)]


def pair_up(values):
    if len(values) % 2:
        values = values + values[-1:]
    return [jnp.concatenate(values[i : i + 2], axis=1) for i in range(0, len(values), 2)]


def transfers(scale, frames, patches, p, tb_ref, tc1_ref, tc2_ref, cols_ref, focal_ref):
    items = frames * patches
    cols = []
    for f in range(frames):
        rows = pl.ds(f * patches + p, BOX, stride=items)
        cols.append(jnp.concatenate([cols_ref[0, rows, :], cols_ref[1, rows, :]], axis=0))
    pairs = []
    for i, pair in enumerate(pair_up(cols)):
        focal = left(tb_ref, pair)
        for f in range(2 * i, min(2 * i + 2, frames)):
            k = f - 2 * i
            focal_ref[f * patches + p] = focal[:, k * LANES : (k + 1) * LANES]
        real, imag = focal[:PATCH], focal[PATCH:]
        pairs.append(scale * (real * real + imag * imag))
    return half_spectrum(pairs, frames, tc1_ref, tc2_ref)


def estimate_of(data, transfer):
    pairs = [(d[:, :LANES], d[:, LANES:], t[:, :LANES], t[:, LANES:]) for d, t in zip(data, transfer)]
    cross_real = sum(dr * tr + di * ti for dr, di, tr, ti in pairs)
    cross_imag = sum(di * tr - dr * ti for dr, di, tr, ti in pairs)
    power = sum(tr * tr + ti * ti for dr, di, tr, ti in pairs) + damping
    return cross_real / power, cross_imag / power


def gradient_of(data, transfer, est, weight):
    er, ei = est
    double = -2.0 * weight
    grads = []
    for d, t in zip(data, transfer):
        tr, ti = t[:, :LANES], t[:, LANES:]
        mr = d[:, :LANES] - (er * tr - ei * ti)
        mi = d[:, LANES:] - (er * ti + ei * tr)
        grads.append(
            jnp.concatenate([double * (er * mr + ei * mi), double * (er * mi - ei * mr)], axis=1)
        )
    return grads


def back_to_pupil(scale, frames, patches, p, grads, tf1_ref, tf2_ref, tg1_ref, tg2_ref, focal_ref, back_ref):
    items = frames * patches
    wide = right(jnp.concatenate(grads, axis=0), tf1_ref)
    columns = []
    for f in range(frames):
        rows = wide[HALF * f : HALF * (f + 1)]
        columns.append(jnp.concatenate([rows[:, :LANES], rows[:, LANES:]], axis=0))
    halves = []
    for i, pair in enumerate(pair_up(columns)):
        spread = left(tf2_ref, pair) * (2.0 * scale)
        fields = []
        for f in range(2 * i, min(2 * i + 2, frames)):
            k = f - 2 * i
            one = spread[:, k * LANES : (k + 1) * LANES]
            fields.append(focal_ref[f * patches + p] * jnp.concatenate([one, one], axis=0))
        pupil = left(tg1_ref, pair_up(fields)[0])
        for k in range(len(fields)):
            lanes = slice(k * LANES, (k + 1) * LANES)
            halves.append(jnp.concatenate([pupil[:BOX, lanes], pupil[BOX:, lanes]], axis=1))
    high, low = split(jnp.concatenate(halves, axis=0))
    first = mm(high, tg2_ref[...])
    back = first[:, :LANES] + first[:, LANES:] + mm(low, tg2_ref[:, :LANES])
    for f in range(frames):
        item = f * patches + p
        back_ref[pl.ds(item, BOX, stride=items), :] = back[f * BOX : (f + 1) * BOX]


def coefficient_gradient(items, z_ref, pupil_ref, back_ref):
    def two_rows(i, total):
        sides = []
        for k in range(2):
            rows = pl.ds(pl.multiple_of((2 * i + k) * items, 8), items)
            sides.append(pupil_ref[rows, :] * back_ref[rows, :])
        high, low = split(jnp.concatenate(sides, axis=1))
        return total + lax.dot_general(
            jnp.concatenate([high, low], axis=0),
            z_ref[i],
            (((1,), (1,)), ((), ())),
            preferred_element_type=f32,
        )

    total = lax.fori_loop(
        0, BOX // 2, two_rows, jnp.zeros((2 * items, 2 * MPAD), f32), unroll=4
    )
    total = total[:items] + total[items:]
    total = jnp.concatenate([total, jnp.zeros((items, LANES - 2 * MPAD), f32)], axis=1)
    total = total + pltpu.roll(total, LANES - MPAD, 1)
    lane = lax.broadcasted_iota(jnp.int32, total.shape, 1)
    return jnp.where(lane < MPAD, total, 0.0)


def unpack_pixels(packed):
    lane = lax.broadcasted_iota(jnp.int32, (PACK - 40, LANES), 1)
    third = jnp.concatenate(
        [pltpu.roll(packed[48:56], LANES - 8 - 8 * t, 1) for t in range(3)], axis=0
    )
    rest = jnp.where(
        lane < 40,
        pltpu.roll(packed[:24], 40, 1),
        jnp.where(lane < 80, pltpu.roll(packed[24:48], 80, 1), third),
    )
    return jnp.concatenate([packed, rest], axis=0)


def starting_values(start, chunk, patches):
    rows = slice(chunk * patches, (chunk + 1) * patches)
    current = jnp.concatenate([s[rows, :] for s in start], axis=0)
    lane = lax.broadcasted_iota(jnp.int32, current.shape, 1)
    return jnp.where(lane < MPAD, current, 0.0)


def first_kernel(scale, frames, patches, chunks, *refs):
    start = refs[:frames]
    z_ref, mask_ref, ta_ref, tb_ref, tc1_ref, tc2_ref = refs[frames : frames + 6]
    outs = refs[frames + 6 : frames + 6 + 3 * chunks]
    (cols_ref,) = refs[frames + 6 + 3 * chunks :]
    for c in range(chunks):
        pupil_ref, focal_ref, transfer_ref = outs[3 * c : 3 * c + 3]
        current = starting_values(start, c, patches)
        pupil_and_columns(current, z_ref, mask_ref, ta_ref, pupil_ref, cols_ref)

        def one_patch(p, carry):
            result = transfers(
                scale, frames, patches, p, tb_ref, tc1_ref, tc2_ref, cols_ref, focal_ref
            )
            for f in range(frames):
                transfer_ref[f * patches + p] = result[f]
            return carry

        lax.fori_loop(0, patches, one_patch, 0)


def middle_kernel(scale, frames, patches, chunk, finish, *refs):
    start = refs[:frames]
    pixels = refs[frames : 2 * frames]
    pupil_ref, focal_ref, transfer_ref = refs[2 * frames : 2 * frames + 3]
    (
        z_ref,
        mask_ref,
        ta_ref,
        tb_ref,
        tc1_ref,
        tc2_ref,
        tf1_ref,
        tf2_ref,
        tg1_ref,
        tg2_ref,
        window_ref,
        weight_ref,
        freq_ref,
    ) = refs[2 * frames + 3 : 2 * frames + 16]
    (
        estimate_out,
        current_out,
        energy_out,
        pupil_out,
        focal_out,
        grads_out,
        data_ref,
        cols_ref,
        back_ref,
        ramp_ref,
    ) = refs[2 * frames + 16 :]
    items = frames * patches
    for f in range(frames):
        s = start[f][pl.ds(0, 1), :]
        angle = freq_ref[0] * s[:, MPAD : MPAD + 1] + freq_ref[1] * s[:, MPAD + 1 : MPAD + 2]
        zero = jnp.zeros(angle.shape, jnp.int32)
        ramp_ref[f, :, :LANES] = quadrant_cos(angle, zero)
        ramp_ref[f, :, LANES:] = quadrant_cos(angle, zero + 1)
    back_args = (tf1_ref, tf2_ref, tg1_ref, tg2_ref)

    def one_patch(p, carry):
        weight = weight_ref[...]
        window = window_ref[...]
        planes = [unpack_pixels(pixels[f][p]) * window for f in range(frames)]
        spectra = half_spectrum(pair_up(planes), frames, tc1_ref, tc2_ref)
        data = []
        total = None
        for f in range(frames):
            real, imag = spectra[f][:, :LANES], spectra[f][:, LANES:]
            cr, ci = ramp_ref[f, :, :LANES], ramp_ref[f, :, LANES:]
            dr, di = real * cr - imag * ci, real * ci + imag * cr
            both = jnp.concatenate([dr, di], axis=1)
            data.append(both)
            data_ref[f * patches + p] = both
            part = weight * (dr * dr + di * di)
            total = part if total is None else total + part
        energy = jnp.sum(jnp.sum(total, axis=0, keepdims=True), axis=1, keepdims=True)
        for f in range(frames):
            energy_out[pl.ds(f * patches + p, 1), :] = jnp.broadcast_to(energy, (1, LANES))
        transfer = [transfer_ref[f * patches + p] for f in range(frames)]
        est = estimate_of(data, transfer)
        grads = gradient_of(data, transfer, est, weight)
        back_to_pupil(scale, frames, patches, p, grads, *back_args, focal_ref, back_ref)
        return carry

    lax.fori_loop(0, patches, one_patch, 0)
    grad = coefficient_gradient(items, z_ref, pupil_ref, back_ref)
    current = starting_values(start, chunk, patches)
    current = current - step_size * frames * grad / energy_out[...]
    current_out[...] = current
    pupil_and_columns(current, z_ref, mask_ref, ta_ref, pupil_out, cols_ref)

    def next_patch(p, carry):
        transfer = transfers(
            scale, frames, patches, p, tb_ref, tc1_ref, tc2_ref, cols_ref, focal_out
        )
        data = [data_ref[f * patches + p] for f in range(frames)]
        est = estimate_of(data, transfer)
        estimate_out[p, 0] = est[0] * (1.0 / PATCH)
        estimate_out[p, 1] = est[1] * (1.0 / PATCH)
        grads = gradient_of(data, transfer, est, weight_ref[...])
        if finish:
            back_to_pupil(scale, frames, patches, p, grads, *back_args, focal_out, back_ref)
        else:
            for f in range(frames):
                grads_out[f * patches + p] = grads[f]
        return carry

    lax.fori_loop(0, patches, next_patch, 0)
    if finish:
        grad = coefficient_gradient(items, z_ref, pupil_out, back_ref)
        current_out[...] = current_out[...] - step_size * frames * grad / energy_out[...]


def last_kernel(scale, frames, patches, earlier, *refs):
    (
        current_ref,
        energy_ref,
        pupil_ref,
        focal_ref,
        grads_ref,
        z_ref,
        tf1_ref,
        tf2_ref,
        tg1_ref,
        tg2_ref,
    ) = refs[:10]
    before = refs[10 : 10 + earlier]
    outs = refs[10 + earlier : 10 + earlier + frames]
    (back_ref,) = refs[10 + earlier + frames :]
    items = frames * patches

    def one_patch(p, carry):
        grads = [grads_ref[f * patches + p] for f in range(frames)]
        back_to_pupil(
            scale, frames, patches, p, grads, tf1_ref, tf2_ref, tg1_ref, tg2_ref, focal_ref, back_ref
        )
        return carry

    lax.fori_loop(0, patches, one_patch, 0)
    grad = coefficient_gradient(items, z_ref, pupil_ref, back_ref)
    current = current_ref[...] - step_size * frames * grad / energy_ref[...]
    for f in range(frames):
        rows = slice(f * patches, (f + 1) * patches)
        for c in range(earlier):
            outs[f][c * patches : (c + 1) * patches, :] = before[c][rows, :]
        outs[f][earlier * patches : (earlier + 1) * patches, :] = current[rows]


def slot_of(axes, count, me, strip, group, rank):
    frames, strips = axes
    chunks = strips // frames
    per = count // strips
    relative = lax.rem(lax.div(group, chunks) - me + frames, frames)
    chunk = lax.rem(group + strip, chunks)
    return (relative * chunks + chunk) * per + rank


def fill_slots(axes, count, assign_ref, counts_ref, visit):
    me = lax.axis_index("frm")
    strip = lax.axis_index("pat")
    for g in range(axes[1]):
        counts_ref[g] = 0

    def one(p, carry):
        group = assign_ref[p]
        rank = counts_ref[group]
        counts_ref[group] = rank + 1
        visit(p, slot_of(axes, count, me, strip, group, rank))
        return carry

    lax.fori_loop(0, count, one, 0)


def prepare_kernel(axes, count, assign_ref, shifts_ref, coefs_ref, *refs):
    frames = axes[0]
    outs, (sorted_ref, counts_ref) = refs[:frames], refs[frames:]
    modes = coefs_ref.shape[-1]
    patches = count // frames
    sorted_ref[...] = jnp.zeros(sorted_ref.shape, f32)

    def visit(p, slot):
        sorted_ref[pl.ds(slot, 1), :modes] = coefs_ref[pl.ds(p, 1), :]

    fill_slots(axes, count, assign_ref, counts_ref, visit)
    lane = lax.broadcasted_iota(jnp.int32, (patches, LANES), 1)
    for f in range(frames):
        rows = sorted_ref[f * patches : (f + 1) * patches, :]
        rows = jnp.where(lane == MPAD, shifts_ref[0, 0], rows)
        outs[f][...] = jnp.where(lane == MPAD + 1, shifts_ref[0, 1], rows)


def cut_kernel(axes, count, assign_ref, anchors_ref, strip_ref, below_ref, *refs):
    pieces = axes[1]
    outs, (tall_ref, counts_ref, order_ref) = refs[:pieces], refs[pieces:]
    patches = count // pieces
    height, width = strip_ref.shape
    tall_ref[:height, :width] = strip_ref[...]
    tall_ref[height : height + PATCH, :width] = below_ref[...]
    first = lax.axis_index("pat") * height

    def visit(p, slot):
        order_ref[slot] = p

    fill_slots(axes, count, assign_ref, counts_ref, visit)
    lane = lax.broadcasted_iota(jnp.int32, (24, LANES), 1)
    for f in range(pieces):

        def one(j, carry):
            p = order_ref[f * patches + j]
            row = anchors_ref[p, 0] - first
            col = anchors_ref[p, 1]
            tile = lax.div(col, LANES)
            base = pl.multiple_of(tile * LANES, LANES)
            above = pl.multiple_of(lax.div(row, 8) * 8, 8)
            block = tall_ref[pl.ds(above, FULL), pl.ds(base, 2 * LANES)]
            back = lax.rem(2 * LANES - (col - base), 2 * LANES)
            block = pltpu.roll(block, back, 1)[:, :LANES]
            block = pltpu.roll(block, lax.rem(FULL - (row - above), FULL), 0)[:PATCH]
            rest = block[PACK:]
            outs[f][j, 0:24, :] = jnp.where(lane < 88, block[0:24], pltpu.roll(rest, 88, 1))
            outs[f][j, 24:48, :] = jnp.where(lane < 88, block[24:48], pltpu.roll(rest, 48, 1))
            third = jnp.where(
                lane[:8] < 96,
                pltpu.roll(rest[:8], 8, 1),
                jnp.where(
                    lane[:8] < 104, pltpu.roll(rest[8:16], 16, 1), pltpu.roll(rest[16:24], 24, 1)
                ),
            )
            outs[f][j, 48:56, :] = jnp.where(lane[:8] < 88, block[48:56], third)
            outs[f][j, 56:64, :] = block[56:64]
            return carry

        lax.fori_loop(0, patches, one, 0, unroll=2)


def restore_kernel(axes, count, assign_ref, *refs):
    frames = axes[0]
    parts, (out_ref, all_ref, counts_ref) = refs[:frames], refs[frames:]
    patches = count // frames
    modes = out_ref.shape[-1]
    for f in range(frames):
        all_ref[f * patches : (f + 1) * patches, :] = parts[f][...]

    def visit(p, slot):
        out_ref[pl.ds(p, 1), :] = all_ref[pl.ds(slot, 1), :modes]

    fill_slots(axes, count, assign_ref, counts_ref, visit)


def call(body, outs, scratch, operands, smem=0, name=None):
    vmem = pl.BlockSpec(memory_space=pltpu.VMEM)
    scalar = pl.BlockSpec(memory_space=pltpu.SMEM)
    return pl.pallas_call(
        body,
        out_shape=[jax.ShapeDtypeStruct(s, f32) for s in outs],
        in_specs=[scalar] * smem + [vmem] * (len(operands) - smem),
        out_specs=[vmem] * len(outs),
        scratch_shapes=scratch,
        name=name,
    )(*operands)


def around(value, axis, steps):
    count = lax.axis_size(axis)
    return lax.ppermute(value, axis, [(s, (s + steps) % count) for s in range(count)])


def assemble(half):
    mid = PATCH // 2
    top = half[:, :, : mid + 1, :PATCH]
    nyquist = half[:, :, 1:mid, PATCH : PATCH + 1]
    low = jnp.flip(half[:, :, 1:mid, :PATCH], axis=2)
    low_nyquist = jnp.flip(nyquist, axis=2)
    low = jnp.concatenate(
        [low[..., :1], jnp.flip(low[..., mid + 1 :], axis=3), low_nyquist, jnp.flip(low[..., 1:mid], axis=3)],
        axis=3,
    )
    low = low * jnp.array([1.0, -1.0], f32)[None, :, None, None]
    spectra = jnp.concatenate([top, low], axis=2)
    return spectra.reshape(spectra.shape[0], 2, PATCH * PATCH)


def shards(frames, shifts, coefficients, anchors, assign):
    t = tables()
    scale = t["scale"]
    c = {k: jnp.asarray(v) for k, v in t.items() if k != "scale"}
    height = frames.shape[1]
    width = frames.shape[2]
    count = assign.shape[0]
    n_frm = lax.axis_size("frm")
    n_pat = lax.axis_size("pat")
    axes = (n_frm, n_pat)
    chunks = n_pat // n_frm
    per = count // n_pat
    items = n_frm * per

    below = lax.ppermute(
        frames[0, :PATCH, :], "pat", [(s, s - 1) for s in range(1, n_pat)]
    )
    ready = call(
        functools.partial(prepare_kernel, axes, count),
        [(chunks * per, LANES)] * n_frm,
        [pltpu.VMEM((count, LANES), f32), pltpu.SMEM((n_pat,), jnp.int32)],
        [assign, shifts, coefficients[0]],
        smem=2,
        name="prepare",
    )
    start = [ready[0]] + [around(ready[r], "frm", r) for r in range(1, n_frm)]

    state = [(BOX * items, LANES), (items, 2 * PATCH, LANES), (items, HALF, 2 * LANES)]
    first = call(
        functools.partial(first_kernel, scale, n_frm, per, chunks),
        state * chunks,
        [pltpu.VMEM((2, BOX * items, LANES), f32)],
        start + [c[k] for k in ("z", "mask", "ta", "tb", "tc1", "tc2")],
        name="first",
    )
    cuts = call(
        functools.partial(cut_kernel, axes, count),
        [(per, PACK, LANES)] * n_pat,
        [
            pltpu.VMEM((height + PATCH, width + LANES), f32),
            pltpu.SMEM((n_pat,), jnp.int32),
            pltpu.SMEM((count,), jnp.int32),
        ],
        [assign, anchors, frames[0], below],
        smem=2,
        name="cut",
    )
    pixels = []
    for k in range(chunks):
        mine = [cuts[r * chunks + k] for r in range(n_frm)]
        pixels.append([mine[0]] + [around(mine[r], "frm", r) for r in range(1, n_frm)])

    both = ("frm", "pat")
    halves = []
    before = []
    for k in range(chunks):
        final = k == chunks - 1
        outs = [(per, 2, HALF, LANES), (items, LANES), (items, LANES)]
        scratch = [
            pltpu.VMEM((items, HALF, 2 * LANES), f32),
            pltpu.VMEM((2, BOX * items, LANES), f32),
            pltpu.VMEM((BOX * items, LANES), f32),
            pltpu.VMEM((n_frm, HALF, 2 * LANES), f32),
        ]
        if final:
            outs = outs + state
        else:
            scratch = [pltpu.VMEM(shape, f32) for shape in state] + scratch
        result = call(
            functools.partial(middle_kernel, scale, n_frm, per, k, not final),
            outs,
            scratch,
            start
            + pixels[k]
            + list(first[3 * k : 3 * k + 3])
            + [
                c[name]
                for name in (
                    "z", "mask", "ta", "tb", "tc1", "tc2", "tf1", "tf2", "tg1", "tg2",
                    "window", "weight", "freq",
                )
            ],
            name="middle" if final else "midfull",
        )
        pairs = []
        for f in range(n_frm):
            for s in range(n_pat):
                group = chunks * f + (s + k) % chunks
                pairs.append((f * n_pat + s, (s // chunks) * n_pat + group))
        halves.append(lax.ppermute(result[0], both, pairs))
        if not final:
            before.append(result[1])
    finals = call(
        functools.partial(last_kernel, scale, n_frm, per, chunks - 1),
        [(chunks * per, LANES)] * n_frm,
        [pltpu.VMEM((BOX * items, LANES), f32)],
        list(result[1:]) + [c[k] for k in ("z", "tf1", "tf2", "tg1", "tg2")] + before,
        name="last",
    )
    parts = [finals[0]] + [around(finals[r], "frm", -r) for r in range(1, n_frm)]
    (restored,) = call(
        functools.partial(restore_kernel, axes, count),
        [(count, coefficients.shape[2])],
        [pltpu.VMEM((count, LANES), f32), pltpu.SMEM((n_pat,), jnp.int32)],
        [assign] + parts,
        smem=1,
        name="restore",
    )
    new_coefficients = restored[None]

    group = lax.axis_index("pat")
    stacked = jnp.stack(halves[::-1] * 2)
    begin = lax.rem(chunks - 1 + chunks - lax.rem(group, chunks), chunks)
    ordered = lax.dynamic_slice_in_dim(stacked, begin, chunks, 0)
    return (new_coefficients, assemble(ordered.reshape((chunks * per,) + halves[0].shape[1:])))


def solution(mesh):
    in_specs = (
        P("frm", "pat", None),
        P("frm", None),
        P("frm", "pat", None),
        P("pat", None),
        P("pat"),
    )
    out_specs = (P("frm", "pat", None), P(("pat", "frm"), None, None))
    return jax.shard_map(shards, mesh=mesh, in_specs=in_specs, out_specs=out_specs, check_vma=False)
```

```python
import functools
import math

import jax
import jax.numpy as jnp
import ml_dtypes
import numpy as np
from jax import lax
from jax.experimental import pallas as pl
from jax.experimental.pallas import tpu as pltpu
from jax.sharding import PartitionSpec as P

PATCH = 88
MODES = 40
ITERS = 2

BOX = 48
HALF = 48
MPAD = 48
LANES = 128
PACK = 64
FULL = 96

damping = 0.05
step_size = 64.0
f32 = jnp.float32
bf16 = jnp.bfloat16


def noll_index(j):
    n = 0
    remaining = j - 1
    while remaining > n:
        n += 1
        remaining -= n
    m = (-1) ** j * (n % 2 + 2 * ((remaining + (n + 1) % 2) // 2))
    return (n, m)


def zernike_table(length, number):
    centre = length / 2.0
    coords = (np.arange(length) - centre) / (length / 4.0)
    rows, cols = np.meshgrid(coords, coords, indexing="ij")
    radius = np.sqrt(rows * rows + cols * cols)
    angle = np.arctan2(rows, cols)
    inside = (radius <= 1.0).astype(np.float64)
    surfaces = []
    for j in range(2, number + 2):
        n, m = noll_index(j)
        order = abs(m)
        radial = np.zeros((length, length))
        for k in range((n - order) // 2 + 1):
            factor = (
                (-1) ** k
                * math.factorial(n - k)
                / (
                    math.factorial(k)
                    * math.factorial((n + order) // 2 - k)
                    * math.factorial((n - order) // 2 - k)
                )
            )
            radial = radial + factor * radius ** (n - 2 * k)
        if m == 0:
            surface = math.sqrt(n + 1) * radial
        elif m > 0:
            surface = math.sqrt(2 * (n + 1)) * radial * np.cos(order * angle)
        else:
            surface = math.sqrt(2 * (n + 1)) * radial * np.sin(order * angle)
        surfaces.append(surface * inside)
    return (np.stack(surfaces), inside)


def split_table(table):
    table = np.asarray(table, np.float32)
    high = table.astype(ml_dtypes.bfloat16)
    low = (table - high.astype(np.float32)).astype(ml_dtypes.bfloat16)
    return np.stack([high, low])


def left_table(table):
    high, low = split_table(table)
    return np.concatenate([high, low, high], axis=1)


@functools.lru_cache(None)
def tables():
    n = PATCH
    start = n // 2 - n // 4
    grid = np.arange(n)
    full = np.zeros(LANES, np.int64)
    full[:n] = grid
    full[n] = n // 2
    full_ok = np.zeros(LANES)
    full_ok[: n + 1] = 1.0
    box = start + np.arange(BOX)
    half = np.arange(HALF)
    half_ok = (half <= n // 2).astype(np.float64)
    ang = lambda a, b: 2.0 * np.pi * (np.multiply.outer(a, b) % n) / n
    t = ang(box, grid)
    ta = np.zeros((LANES, 2 * LANES))
    ta[:BOX, :n] = np.cos(t)
    ta[64 : 64 + BOX, :n] = np.sin(t)
    ta[:BOX, LANES : LANES + n] = -np.sin(t)
    ta[64 : 64 + BOX, LANES : LANES + n] = np.cos(t)
    t = ang(grid, box)
    tb = np.block([[np.cos(t), np.sin(t)], [-np.sin(t), np.cos(t)]])
    t = ang(half, grid)
    tc1 = np.zeros((2 * HALF, FULL))
    tc1[:HALF, :n] = np.cos(t) * half_ok[:, None]
    tc1[HALF:, :n] = -np.sin(t) * half_ok[:, None]
    t = ang(grid, full)
    tc2 = np.zeros((2 * LANES, 2 * LANES))
    tc2[:n, :LANES] = np.cos(t) * full_ok
    tc2[:n, LANES:] = -np.sin(t) * full_ok
    tc2[LANES : LANES + n, :LANES] = np.sin(t) * full_ok
    tc2[LANES : LANES + n, LANES:] = np.cos(t) * full_ok
    t = ang(grid, half)
    tf2 = np.concatenate([np.cos(t) * half_ok, -np.sin(t) * half_ok], axis=1)
    t = ang(box, grid)
    tg1 = np.block([[np.cos(t), -np.sin(t)], [np.sin(t), np.cos(t)]])
    t = ang(grid, box)
    tg2 = np.zeros((2 * LANES, LANES))
    tg2[:n, :BOX] = np.sin(t)
    tg2[LANES : LANES + n, :BOX] = np.cos(t)
    tg2[:n, 64 : 64 + BOX] = -np.cos(t)
    tg2[LANES : LANES + n, 64 : 64 + BOX] = np.sin(t)
    modes, inside = zernike_table(n, MODES)
    z = np.zeros((BOX, MPAD, 64))
    mask = np.zeros((BOX, LANES))
    width = min(BOX, n - start)
    cut = slice(start, start + width)
    z[:width, :MODES, :width] = np.transpose(modes[:, cut, cut], (1, 0, 2))
    for off in (0, 64):
        mask[:width, off : off + width] = inside[cut, cut]
    zs = split_table(z)
    ztab = np.concatenate([zs[0], zs[1]], axis=1)
    ztab = np.concatenate([ztab[0::2], ztab[1::2]], axis=2)
    scale = 1.0 / (n * n * inside.sum())
    profile = 0.5 - 0.5 * np.cos(2.0 * np.pi * (grid + 0.5) / n)
    window = np.zeros((n, LANES), np.float32)
    window[:, :n] = profile[:, None] * profile[None, :]
    weight = np.zeros((HALF, LANES), np.float32)
    weight[0, :n] = 1.0
    weight[n // 2, :n] = 1.0
    weight[1 : n // 2, : n + 1] = 2.0
    weight[1 : n // 2, n // 2] = 1.0
    weight[1 : n // 2, n] = 1.0
    fu = np.where(half < n // 2, half, -half) * half_ok
    fv = np.where(full < n // 2, full, full - n) * full_ok
    fv[n] = n // 2
    freq = np.zeros((2, HALF, LANES), np.float32)
    freq[0] = fu[:, None] * (-2.0 * np.pi / n)
    freq[1] = fv[None, :] * (-2.0 * np.pi / n)
    return dict(
        ta=split_table(ta),
        tb=left_table(tb),
        tc1=left_table(tc1),
        tc2=split_table(tc2),
        tf2=np.concatenate(list(split_table(tf2)), axis=0),
        tg1=np.concatenate(list(split_table(tg1)), axis=0),
        tg2=np.concatenate(list(split_table(tg2)), axis=1),
        z=ztab,
        mask=mask.astype(np.float32),
        window=window,
        weight=weight,
        freq=freq,
        scale=float(scale),
    )


def split(x):
    high = x.astype(bf16)
    low = (x - high.astype(f32)).astype(bf16)
    return high, low


def mm_t(a, b):
    return lax.dot_general(a, b, (((1,), (1,)), ((), ())), preferred_element_type=f32)


def mm(a, b):
    return jnp.dot(a, b, preferred_element_type=f32)


def left(table_ref, x):
    high, low = split(x)
    return mm(table_ref[...], jnp.concatenate([high, high, low], axis=0))


def left_rows(table_ref, x):
    high, low = split(x)
    rows = table_ref.shape[0] // 2
    both = mm(table_ref[...], high)
    return both[:rows] + both[rows:] + mm(table_ref[:rows, :], low)


def right(x, table_ref):
    high, low = split(x)
    table = jnp.concatenate([table_ref[0], table_ref[0], table_ref[1]], axis=0)
    return mm(jnp.concatenate([high, low, high], axis=1), table)


def right_t(x, table_ref):
    high, low = split(x)
    table = jnp.concatenate([table_ref[0], table_ref[0], table_ref[1]], axis=1)
    return mm_t(jnp.concatenate([high, low, high], axis=1), table)


def sine(x, quarter):
    turns = jnp.floor(x * (1.0 / math.pi) + (quarter + 0.5))
    part = turns - quarter
    r = x - part * 3.140625
    r = r - part * 9.67502593994140625e-4
    r = r - part * 1.509957990978376432e-7
    r2 = r * r
    poly = 0.008333016341242573 + r2 * (-0.00019806546261204837 + r2 * 2.599901665630011e-06)
    value = r + (r * r2) * (-0.16666657057852008 + r2 * poly)
    pair = turns * 0.5
    return value * (1.0 - 4.0 * (pair - jnp.floor(pair)))


def lane_quarter(shape):
    lane = lax.broadcasted_iota(jnp.int32, shape, len(shape) - 1)
    return jnp.where(lane < 64, 0.5, 0.0).astype(f32)


def pupils(currents, z_ref, mask_ref, pupil_refs):
    items = currents[0].shape[0]
    total = items * len(currents)
    current = jnp.concatenate(currents, axis=0)
    doubled = current + pltpu.roll(current, MPAD, 1)
    high, low = split(doubled[:, : 2 * MPAD])
    stacked = jnp.concatenate([high, low], axis=0)
    quarter = lane_quarter((total, LANES))

    lower = lax.broadcasted_iota(jnp.int32, (total, LANES), 1) < 64

    def two_rows(i, carry):
        both = mm(stacked, z_ref[i])
        phase = both[:total] + both[total:]
        turned = pltpu.roll(phase, 64, 1)
        for k in range(2):
            row = 2 * i + k
            doubled = jnp.where(lower, turned, phase) if k else jnp.where(lower, phase, turned)
            pupil = sine(doubled, quarter) * mask_ref[pl.ds(row, 1), :]
            for c, pupil_ref in enumerate(pupil_refs):
                pupil_ref[pl.ds(pl.multiple_of(row * items, 8), items), :] = pupil[
                    c * items : (c + 1) * items
                ]
        return carry

    lax.fori_loop(0, BOX // 2, two_rows, 0, unroll=4)


def columns(pupil_ref, ta_ref, cols_ref):
    steps = 2
    chunk = pupil_ref.shape[0] // steps
    for i in range(steps):
        rows = slice(i * chunk, (i + 1) * chunk)
        wide = right(pupil_ref[rows, :], ta_ref)
        cols_ref[0, rows, :] = wide[:, :LANES]
        cols_ref[1, rows, :] = wide[:, LANES:]


def item_rows(item):
    if isinstance(item, int):
        return slice(item * HALF, (item + 1) * HALF)
    return pl.ds(pl.multiple_of(item * HALF, 8), HALF)


def half_rows(pair, inside, patches, p, tc1_ref, rows_ref):
    pad = jnp.zeros((FULL - PATCH, 2 * LANES), f32)
    both = left(tc1_ref, jnp.concatenate([pair, pad], axis=0))
    for k, f in enumerate(inside):
        lanes = slice(k * LANES, (k + 1) * LANES)
        rows = item_rows(f * patches + p)
        rows_ref[rows, :LANES] = both[:HALF, lanes]
        rows_ref[rows, LANES:] = both[HALF:, lanes]


def frame_pairs(frames):
    return [range(f, min(f + 2, frames)) for f in range(0, frames, 2)]


def staggered(frames, patches, early, late):
    waiting = None
    for p in range(patches):
        for inside in frame_pairs(frames):
            result = early(p, inside)
            if waiting is not None:
                late(*waiting)
            waiting = (p, inside, result)
    late(*waiting)


def pair_up(values):
    if len(values) % 2:
        values = values + values[-1:]
    return [jnp.concatenate(values[i : i + 2], axis=1) for i in range(0, len(values), 2)]


def transfers(scale, frames, patches, tb_ref, tc1_ref, tc2_ref, cols_ref, focal_ref, rows_ref, transfer_ref):
    items = frames * patches

    def focal_stage(p, inside):
        cols = []
        for f in inside:
            rows = pl.ds(f * patches + p, BOX, stride=items)
            cols.append(jnp.concatenate([cols_ref[0, rows, :], cols_ref[1, rows, :]], axis=0))
        focal = left(tb_ref, pair_up(cols)[0])
        for k, f in enumerate(inside):
            focal_ref[f * patches + p] = focal[:, k * LANES : (k + 1) * LANES]
        real, imag = focal[:PATCH], focal[PATCH:]
        return scale * (real * real + imag * imag)

    def half_stage(p, inside, pair):
        half_rows(pair, inside, patches, p, tc1_ref, rows_ref)

    staggered(frames, patches, focal_stage, half_stage)
    transfer_ref[...] = right(rows_ref[...], tc2_ref)


def estimate_of(data, transfer):
    pairs = [(d[:, :LANES], d[:, LANES:], t[:, :LANES], t[:, LANES:]) for d, t in zip(data, transfer)]
    cross_real = sum(dr * tr + di * ti for dr, di, tr, ti in pairs)
    cross_imag = sum(di * tr - dr * ti for dr, di, tr, ti in pairs)
    power = sum(tr * tr + ti * ti for dr, di, tr, ti in pairs) + damping
    return cross_real / power, cross_imag / power


def gradient_of(data, transfer, est, weight):
    er, ei = est
    double = -2.0 * weight
    grads = []
    for d, t in zip(data, transfer):
        tr, ti = t[:, :LANES], t[:, LANES:]
        mr = d[:, :LANES] - (er * tr - ei * ti)
        mi = d[:, LANES:] - (er * ti + ei * tr)
        grads.append(
            jnp.concatenate([double * (er * mr + ei * mi), double * (er * mi - ei * mr)], axis=1)
        )
    return grads


def back_to_pupil(scale, frames, patches, tc2_ref, tf2_ref, tg1_ref, tg2_ref, grads_ref, focal_ref, rows_ref, back_ref):
    items = frames * patches
    rows_ref[...] = right_t(grads_ref[...], tc2_ref)

    def spread_stage(p, inside):
        cols = []
        for f in inside:
            rows = item_rows(f * patches + p)
            cols.append(jnp.concatenate([rows_ref[rows, :LANES], rows_ref[rows, LANES:]], axis=0))
        spread = left_rows(tf2_ref, pair_up(cols)[0]) * (2.0 * scale)
        fields = []
        for k, f in enumerate(inside):
            one = spread[:, k * LANES : (k + 1) * LANES]
            fields.append(focal_ref[f * patches + p] * jnp.concatenate([one, one], axis=0))
        return pair_up(fields)[0]

    def pupil_stage(p, inside, field):
        pupil = left_rows(tg1_ref, field)
        for k, f in enumerate(inside):
            lanes = slice(k * LANES, (k + 1) * LANES)
            rows = item_rows(f * patches + p)
            grads_ref[rows, :LANES] = pupil[:BOX, lanes]
            grads_ref[rows, LANES:] = pupil[BOX:, lanes]

    staggered(frames, patches, spread_stage, pupil_stage)
    high, low = split(grads_ref[...])
    first = mm(high, tg2_ref[...])
    back = first[:, :LANES] + first[:, LANES:] + mm(low, tg2_ref[:, :LANES])
    for item in range(items):
        back_ref[pl.ds(item, BOX, stride=items), :] = back[item * BOX : (item + 1) * BOX]


def coefficient_gradient(items, z_ref, pupil_ref, back_ref):
    lower = lax.broadcasted_iota(jnp.int32, (items, LANES), 1) < 64

    def two_rows(i, total):
        sides = []
        for k in range(2):
            rows = pl.ds(pl.multiple_of((2 * i + k) * items, 8), items)
            product = pupil_ref[rows, :] * back_ref[rows, :]
            sides.append(product + pltpu.roll(product, 64, 1))
        high, low = split(jnp.where(lower, sides[0], sides[1]))
        return total + mm_t(jnp.concatenate([high, low], axis=0), z_ref[i])

    total = lax.fori_loop(
        0, BOX // 2, two_rows, jnp.zeros((2 * items, 2 * MPAD), f32), unroll=4
    )
    total = total[:items] + total[items:]
    total = jnp.concatenate([total, jnp.zeros((items, LANES - 2 * MPAD), f32)], axis=1)
    total = total + pltpu.roll(total, LANES - MPAD, 1)
    lane = lax.broadcasted_iota(jnp.int32, total.shape, 1)
    return jnp.where(lane < MPAD, total, 0.0)


def unpack_pixels(packed):
    lane = lax.broadcasted_iota(jnp.int32, (PACK - 40, LANES), 1)
    third = jnp.concatenate(
        [pltpu.roll(packed[48:56], LANES - 8 - 8 * t, 1) for t in range(3)], axis=0
    )
    rest = jnp.where(
        lane < 40,
        pltpu.roll(packed[:24], 40, 1),
        jnp.where(lane < 80, pltpu.roll(packed[24:48], 80, 1), third),
    )
    return jnp.concatenate([packed, rest], axis=0)


def padded(patches):
    return -(-patches // 8) * 8


def starting_values(start, chunk, patches):
    rows = pl.ds(pl.multiple_of(chunk * padded(patches), 8), padded(patches))
    current = jnp.concatenate([s[rows, :][:patches] for s in start], axis=0)
    lane = lax.broadcasted_iota(jnp.int32, current.shape, 1)
    return jnp.where(lane < MPAD, current, 0.0)


def first_kernel(scale, frames, patches, chunks, *refs):
    start = refs[:frames]
    z_ref, mask_ref, ta_ref, tb_ref, tc1_ref, tc2_ref = refs[frames : frames + 6]
    outs = refs[frames + 6 : frames + 6 + 3 * chunks]
    cols_ref, rows_ref = refs[frames + 6 + 3 * chunks :]
    currents = [starting_values(start, c, patches) for c in range(chunks)]
    pupils(currents, z_ref, mask_ref, [outs[3 * c] for c in range(chunks)])
    for c in range(chunks):
        pupil_ref, focal_ref, transfer_ref = outs[3 * c : 3 * c + 3]
        columns(pupil_ref, ta_ref, cols_ref)
        transfers(
            scale, frames, patches, tb_ref, tc1_ref, tc2_ref, cols_ref, focal_ref, rows_ref, transfer_ref
        )


def middle_kernel(scale, frames, patches, chunk_ref, order_ref, *refs):
    chunk = chunk_ref[0]
    start = refs[:frames]
    pixels = refs[frames : 2 * frames]
    pupil_ref, focal_ref, transfer_ref = refs[2 * frames : 2 * frames + 3]
    (
        z_ref,
        mask_ref,
        ta_ref,
        tb_ref,
        tc1_ref,
        tc2_ref,
        tf2_ref,
        tg1_ref,
        tg2_ref,
        window_ref,
        weight_ref,
        freq_ref,
    ) = refs[2 * frames + 3 : 2 * frames + 15]
    before = refs[2 * frames + 15 : 3 * frames + 15]
    estimate_out = refs[3 * frames + 15]
    outs = refs[3 * frames + 16 : 4 * frames + 16]
    (
        current_out,
        energy_out,
        pupil_out,
        focal_out,
        grads_out,
        data_ref,
        cols_ref,
        back_ref,
        ramp_ref,
        rows_ref,
    ) = refs[4 * frames + 16 :]
    items = frames * patches
    for f in range(frames):
        s = start[f][pl.ds(0, 1), :]
        angle = freq_ref[0] * s[:, MPAD : MPAD + 1] + freq_ref[1] * s[:, MPAD + 1 : MPAD + 2]
        ramp_ref[f, :, :LANES] = sine(angle, 0.5)
        ramp_ref[f, :, LANES:] = sine(angle, 0.0)
    back_args = (tc2_ref, tf2_ref, tg1_ref, tg2_ref)

    def pixel_rows(p, carry):
        window = window_ref[...]
        for inside in frame_pairs(frames):
            planes = [unpack_pixels(pixels[f][p]) * window for f in inside]
            half_rows(pair_up(planes)[0], inside, patches, p, tc1_ref, rows_ref)
        return carry

    lax.fori_loop(0, patches, pixel_rows, 0)
    data_ref[...] = right(rows_ref[...], tc2_ref)

    def first_gradient(p, carry):
        weight = weight_ref[...]
        data = []
        total = None
        for f in range(frames):
            rows = item_rows(f * patches + p)
            real, imag = data_ref[rows, :LANES], data_ref[rows, LANES:]
            cr, ci = ramp_ref[f, :, :LANES], ramp_ref[f, :, LANES:]
            dr, di = real * cr - imag * ci, real * ci + imag * cr
            both = jnp.concatenate([dr, di], axis=1)
            data.append(both)
            data_ref[rows, :] = both
            part = weight * (dr * dr + di * di)
            total = part if total is None else total + part
        energy = jnp.sum(jnp.sum(total, axis=0, keepdims=True), axis=1, keepdims=True)
        for f in range(frames):
            energy_out[pl.ds(f * patches + p, 1), :] = jnp.broadcast_to(energy, (1, LANES))
        transfer = [transfer_ref[item_rows(f * patches + p), :] for f in range(frames)]
        grads = gradient_of(data, transfer, estimate_of(data, transfer), weight)
        for f in range(frames):
            grads_out[item_rows(f * patches + p), :] = grads[f]
        return carry

    lax.fori_loop(0, patches, first_gradient, 0)
    back_to_pupil(scale, frames, patches, *back_args, grads_out, focal_ref, rows_ref, back_ref)
    grad = coefficient_gradient(items, z_ref, pupil_ref, back_ref)
    current = starting_values(start, chunk, patches)
    current = current - step_size * frames * grad / energy_out[...]
    current_out[...] = current
    pupils([current], z_ref, mask_ref, [pupil_out])
    columns(pupil_out, ta_ref, cols_ref)
    transfers(
        scale, frames, patches, tb_ref, tc1_ref, tc2_ref, cols_ref, focal_out, rows_ref, grads_out
    )

    def next_gradient(p, carry):
        rows = [item_rows(f * patches + p) for f in range(frames)]
        transfer = [grads_out[r, :] for r in rows]
        data = [data_ref[r, :] for r in rows]
        est = estimate_of(data, transfer)
        estimate_out[p, 0] = est[0] * (1.0 / PATCH)
        estimate_out[p, 1] = est[1] * (1.0 / PATCH)
        grads = gradient_of(data, transfer, est, weight_ref[...])
        for f in range(frames):
            grads_out[rows[f], :] = grads[f]
        return carry

    lax.fori_loop(0, patches, next_gradient, 0)
    back_to_pupil(scale, frames, patches, *back_args, grads_out, focal_out, rows_ref, back_ref)
    grad = coefficient_gradient(items, z_ref, pupil_out, back_ref)
    current_out[...] = current_out[...] - step_size * frames * grad / energy_out[...]
    for f in range(frames):
        outs[f][...] = before[f][...]
    for j in range(patches):
        p = order_ref[chunk * patches + j]
        for f in range(frames):
            row = f * patches + j
            outs[f][pl.ds(p, 1), :] = current_out[row : row + 1, :]


def piece_of(axes, me, strip, group):
    frames, strips = axes
    chunks = strips // frames
    relative = lax.rem(lax.div(group, chunks) - me + frames, frames)
    return relative * chunks + lax.rem(group + strip, chunks)


def prepare_kernel(axes, count, assign_ref, shifts_ref, coefs_ref, *refs):
    frames = axes[0]
    outs = refs[:frames]
    order_ref, sorted_ref, counts_ref = refs[frames:]
    modes = coefs_ref.shape[-1]
    per = count // axes[1]
    room = padded(per)
    me = lax.axis_index("frm")
    strip = lax.axis_index("pat")
    for g in range(axes[1]):
        counts_ref[g] = 0

    def one(p, carry):
        group = assign_ref[p]
        rank = counts_ref[group]
        counts_ref[group] = rank + 1
        piece = piece_of(axes, me, strip, group)
        order_ref[piece * per + rank] = p
        sorted_ref[pl.ds(piece * room + rank, 1), :modes] = coefs_ref[pl.ds(p, 1), :]
        return carry

    sorted_ref[...] = jnp.zeros(sorted_ref.shape, f32)
    lax.fori_loop(0, count, one, 0)
    rows_each = sorted_ref.shape[0] // frames
    lane = lax.broadcasted_iota(jnp.int32, (rows_each, LANES), 1)
    for f in range(frames):
        rows = sorted_ref[f * rows_each : (f + 1) * rows_each, :]
        rows = jnp.where(lane == MPAD, shifts_ref[0, 0], rows)
        outs[f][...] = jnp.where(lane == MPAD + 1, shifts_ref[0, 1], rows)


def cut_kernel(axes, count, order_ref, anchors_ref, strip_ref, below_ref, *refs):
    pieces = axes[1]
    outs, (tall_ref,) = refs[:pieces], refs[pieces:]
    patches = count // pieces
    height, width = strip_ref.shape
    tall_ref[:height, :width] = strip_ref[...]
    tall_ref[height : height + PATCH, :width] = below_ref[...]
    first = lax.axis_index("pat") * height

    lane = lax.broadcasted_iota(jnp.int32, (24, LANES), 1)
    for f in range(pieces):

        def one(j, carry):
            p = order_ref[f * patches + j]
            row = anchors_ref[p, 0] - first
            col = anchors_ref[p, 1]
            tile = lax.div(col, LANES)
            base = pl.multiple_of(tile * LANES, LANES)
            above = pl.multiple_of(lax.div(row, 8) * 8, 8)
            block = tall_ref[pl.ds(above, FULL), pl.ds(base, 2 * LANES)]
            back = lax.rem(2 * LANES - (col - base), 2 * LANES)
            block = pltpu.roll(block, back, 1)[:, :LANES]
            block = pltpu.roll(block, lax.rem(FULL - (row - above), FULL), 0)[:PATCH]
            rest = block[PACK:]
            outs[f][j, 0:24, :] = jnp.where(lane < 88, block[0:24], pltpu.roll(rest, 88, 1))
            outs[f][j, 24:48, :] = jnp.where(lane < 88, block[24:48], pltpu.roll(rest, 48, 1))
            third = jnp.where(
                lane[:8] < 96,
                pltpu.roll(rest[:8], 8, 1),
                jnp.where(
                    lane[:8] < 104, pltpu.roll(rest[8:16], 16, 1), pltpu.roll(rest[16:24], 24, 1)
                ),
            )
            outs[f][j, 48:56, :] = jnp.where(lane[:8] < 88, block[48:56], third)
            outs[f][j, 56:64, :] = block[56:64]
            return carry

        lax.fori_loop(0, patches, one, 0, unroll=2)


def call(body, outs, scratch, operands, smem=0, name=None, micros=1, after=(), order=0):
    vmem = pl.BlockSpec(memory_space=pltpu.VMEM)
    scalar = pl.BlockSpec(memory_space=pltpu.SMEM)
    whole = pl.BlockSpec(memory_space=pl.ANY)

    def ordered(*refs):
        body(*refs[: len(operands)], *refs[len(operands) + len(after) :])

    return pl.pallas_call(
        ordered,
        out_shape=[jax.ShapeDtypeStruct(s, f32) for s in outs]
        + [jax.ShapeDtypeStruct((order,), jnp.int32)] * bool(order),
        in_specs=[scalar] * smem + [vmem] * (len(operands) - smem) + [whole] * len(after),
        out_specs=[vmem] * len(outs) + [scalar] * bool(order),
        scratch_shapes=scratch,
        cost_estimate=pl.CostEstimate(
            flops=int(micros * 1e9), bytes_accessed=1 << 20, transcendentals=0
        ),
        name=name,
    )(*operands, *after)


def around(value, axis, steps):
    count = lax.axis_size(axis)
    return lax.ppermute(value, axis, [(s, (s + steps) % count) for s in range(count)])


def assemble(half):
    mid = PATCH // 2
    top = half[:, :, : mid + 1, :PATCH]
    nyquist = half[:, :, 1:mid, PATCH : PATCH + 1]
    low = jnp.flip(half[:, :, 1:mid, :PATCH], axis=2)
    low_nyquist = jnp.flip(nyquist, axis=2)
    low = jnp.concatenate(
        [low[..., :1], jnp.flip(low[..., mid + 1 :], axis=3), low_nyquist, jnp.flip(low[..., 1:mid], axis=3)],
        axis=3,
    )
    low = low * jnp.array([1.0, -1.0], f32)[None, :, None, None]
    spectra = jnp.concatenate([top, low], axis=2)
    return spectra.reshape(spectra.shape[0], 2, PATCH * PATCH)


def shards(frames, shifts, coefficients, anchors, assign):
    t = tables()
    scale = t["scale"]
    c = {k: jnp.asarray(v) for k, v in t.items() if k != "scale"}
    height = frames.shape[1]
    width = frames.shape[2]
    count = assign.shape[0]
    n_frm = lax.axis_size("frm")
    n_pat = lax.axis_size("pat")
    axes = (n_frm, n_pat)
    chunks = n_pat // n_frm
    per = count // n_pat
    items = n_frm * per

    below = lax.ppermute(
        frames[0, :PATCH, :], "pat", [(s, s - 1) for s in range(1, n_pat)]
    )
    ready = call(
        functools.partial(prepare_kernel, axes, count),
        [(chunks * padded(per), LANES)] * n_frm,
        [pltpu.VMEM((n_pat * padded(per), LANES), f32), pltpu.SMEM((n_pat,), jnp.int32)],
        [assign, shifts, coefficients[0]],
        smem=2,
        name="prepare",
        order=count,
    )
    order = ready[n_frm]
    start = [ready[0]] + [around(ready[r], "frm", r) for r in range(1, n_frm)]

    state = [(BOX * items, LANES), (items, 2 * PATCH, LANES), (items * HALF, 2 * LANES)]
    wide = pltpu.VMEM((items * HALF, 2 * LANES), f32)
    first = call(
        functools.partial(first_kernel, scale, n_frm, per, chunks),
        state * chunks,
        [pltpu.VMEM((2, BOX * items, LANES), f32), wide],
        start + [c[k] for k in ("z", "mask", "ta", "tb", "tc1", "tc2")],
        name="first",
        micros=10,
    )
    cuts = call(
        functools.partial(cut_kernel, axes, count),
        [(per, PACK, LANES)] * n_pat,
        [pltpu.VMEM((height + PATCH, width + LANES), f32)],
        [order, anchors, frames[0], below],
        smem=2,
        name="cut",
        micros=5,
        after=[first[2]],
    )
    pixels = []
    for k in range(chunks):
        mine = [cuts[r * chunks + k] for r in range(n_frm)]
        pixels.append([mine[0]] + [around(mine[r], "frm", r) for r in range(1, n_frm)])

    both = ("frm", "pat")
    halves = []
    finals = [jnp.zeros((count, LANES), f32)] * n_frm
    after = []
    for k in range(chunks):
        result = call(
            functools.partial(middle_kernel, scale, n_frm, per),
            [(per, 2, HALF, LANES)] + [(count, LANES)] * n_frm,
            [pltpu.VMEM((items, LANES), f32)] * 2
            + [pltpu.VMEM(shape, f32) for shape in state]
            + [
                wide,
                pltpu.VMEM((2, BOX * items, LANES), f32),
                pltpu.VMEM((BOX * items, LANES), f32),
                pltpu.VMEM((n_frm, HALF, 2 * LANES), f32),
                wide,
            ],
            [jnp.full((1,), k, jnp.int32), order]
            + start
            + pixels[k]
            + list(first[3 * k : 3 * k + 3])
            + [
                c[name]
                for name in (
                    "z", "mask", "ta", "tb", "tc1", "tc2", "tf2", "tg1", "tg2",
                    "window", "weight", "freq",
                )
            ]
            + finals,
            smem=2,
            name="middle",
            micros=15,
        )
        pairs = []
        for f in range(n_frm):
            for s in range(n_pat):
                group = chunks * f + (s + k) % chunks
                pairs.append((f * n_pat + s, (s // chunks) * n_pat + group))
        halves.append(lax.ppermute(result[0], both, pairs))
        finals = list(result[1:])
    parts = [finals[0]] + [around(finals[r], "frm", -r) for r in range(1, n_frm)]
    new_coefficients = sum(parts)[None, :, : coefficients.shape[2]]

    group = lax.axis_index("pat")
    stacked = jnp.stack(halves[::-1] * 2)
    begin = lax.rem(chunks - 1 + chunks - lax.rem(group, chunks), chunks)
    ordered = lax.dynamic_slice_in_dim(stacked, begin, chunks, 0)
    return (new_coefficients, assemble(ordered.reshape((chunks * per,) + halves[0].shape[1:])))


def solution(mesh):
    in_specs = (
        P("frm", "pat", None),
        P("frm", None),
        P("frm", "pat", None),
        P("pat", None),
        P("pat"),
    )
    out_specs = (P("frm", "pat", None), P(("pat", "frm"), None, None))
    return jax.shard_map(shards, mesh=mesh, in_specs=in_specs, out_specs=out_specs, check_vma=False)
```

```python
import functools
import math

import jax
import jax.numpy as jnp
import ml_dtypes
import numpy as np
from jax import lax
from jax.experimental import pallas as pl
from jax.experimental.pallas import tpu as pltpu
from jax.sharding import PartitionSpec as P

PATCH = 88
MODES = 40

BOX = 48
HALF = 48
MPAD = 48
LANES = 128
PACK = 64
FULL = 96

VMEM_LIMIT = 30 << 20

damping = 0.05
step_size = 64.0
f32 = jnp.float32
bf16 = jnp.bfloat16


def noll_index(j):
    n = 0
    remaining = j - 1
    while remaining > n:
        n += 1
        remaining -= n
    m = (-1) ** j * (n % 2 + 2 * ((remaining + (n + 1) % 2) // 2))
    return (n, m)


def zernike_table(length, number):
    centre = length / 2.0
    coords = (np.arange(length) - centre) / (length / 4.0)
    rows, cols = np.meshgrid(coords, coords, indexing="ij")
    radius = np.sqrt(rows * rows + cols * cols)
    angle = np.arctan2(rows, cols)
    inside = (radius <= 1.0).astype(np.float64)
    surfaces = []
    for j in range(2, number + 2):
        n, m = noll_index(j)
        order = abs(m)
        radial = np.zeros((length, length))
        for k in range((n - order) // 2 + 1):
            factor = (
                (-1) ** k
                * math.factorial(n - k)
                / (
                    math.factorial(k)
                    * math.factorial((n + order) // 2 - k)
                    * math.factorial((n - order) // 2 - k)
                )
            )
            radial = radial + factor * radius ** (n - 2 * k)
        if m == 0:
            surface = math.sqrt(n + 1) * radial
        elif m > 0:
            surface = math.sqrt(2 * (n + 1)) * radial * np.cos(order * angle)
        else:
            surface = math.sqrt(2 * (n + 1)) * radial * np.sin(order * angle)
        surfaces.append(surface * inside)
    return (np.stack(surfaces), inside)


def split_table(table):
    table = np.asarray(table, np.float32)
    high = table.astype(ml_dtypes.bfloat16)
    low = (table - high.astype(np.float32)).astype(ml_dtypes.bfloat16)
    return np.stack([high, low])


def left_table(table):
    high, low = split_table(table)
    return np.concatenate([high, low, high], axis=1)


@functools.lru_cache(None)
def tables():
    n = PATCH
    start = n // 2 - n // 4
    grid = np.arange(n)
    full = np.zeros(LANES, np.int64)
    full[:n] = grid
    full[n] = n // 2
    full_ok = np.zeros(LANES)
    full_ok[: n + 1] = 1.0
    box = start + np.arange(BOX)
    half = np.arange(HALF)
    half_ok = (half <= n // 2).astype(np.float64)
    ang = lambda a, b: 2.0 * np.pi * (np.multiply.outer(a, b) % n) / n
    t = ang(box, grid)
    ta = np.zeros((LANES, 2 * LANES))
    ta[:BOX, :n] = np.cos(t)
    ta[64 : 64 + BOX, :n] = np.sin(t)
    ta[:BOX, LANES : LANES + n] = -np.sin(t)
    ta[64 : 64 + BOX, LANES : LANES + n] = np.cos(t)
    t = ang(grid, box)
    tb = np.block([[np.cos(t), np.sin(t)], [-np.sin(t), np.cos(t)]])
    t = ang(half, grid)
    tc1 = np.zeros((2 * HALF, FULL))
    tc1[:HALF, :n] = np.cos(t) * half_ok[:, None]
    tc1[HALF:, :n] = -np.sin(t) * half_ok[:, None]
    t = ang(grid, full)
    tc2 = np.zeros((2 * LANES, 2 * LANES))
    tc2[:n, :LANES] = np.cos(t) * full_ok
    tc2[:n, LANES:] = -np.sin(t) * full_ok
    tc2[LANES : LANES + n, :LANES] = np.sin(t) * full_ok
    tc2[LANES : LANES + n, LANES:] = np.cos(t) * full_ok
    t = ang(grid, half)
    tf2 = np.concatenate([np.cos(t) * half_ok, -np.sin(t) * half_ok], axis=1)
    t = ang(box, grid)
    tg1 = np.block([[np.cos(t), -np.sin(t)], [np.sin(t), np.cos(t)]])
    t = ang(grid, box)
    tg2 = np.zeros((2 * LANES, LANES))
    tg2[:n, :BOX] = np.sin(t)
    tg2[LANES : LANES + n, :BOX] = np.cos(t)
    tg2[:n, 64 : 64 + BOX] = -np.cos(t)
    tg2[LANES : LANES + n, 64 : 64 + BOX] = np.sin(t)
    modes, inside = zernike_table(n, MODES)
    z = np.zeros((BOX, MPAD, 64))
    mask = np.zeros((BOX, LANES))
    width = min(BOX, n - start)
    cut = slice(start, start + width)
    z[:width, :MODES, :width] = np.transpose(modes[:, cut, cut], (1, 0, 2))
    for off in (0, 64):
        mask[:width, off : off + width] = inside[cut, cut]
    zs = split_table(z)
    ztab = np.concatenate([zs[0], zs[1]], axis=1)
    ztab = np.concatenate([ztab[0::2], ztab[1::2]], axis=2)
    scale = 1.0 / (n * n * inside.sum())
    profile = 0.5 - 0.5 * np.cos(2.0 * np.pi * (grid + 0.5) / n)
    window = np.zeros((n, LANES), np.float32)
    window[:, :n] = profile[:, None] * profile[None, :]
    weight = np.zeros((HALF, LANES), np.float32)
    weight[0, :n] = 1.0
    weight[n // 2, :n] = 1.0
    weight[1 : n // 2, : n + 1] = 2.0
    weight[1 : n // 2, n // 2] = 1.0
    weight[1 : n // 2, n] = 1.0
    fu = np.where(half < n // 2, half, -half) * half_ok
    fv = np.where(full < n // 2, full, full - n) * full_ok
    fv[n] = n // 2
    freq = np.zeros((2, HALF, LANES), np.float32)
    freq[0] = fu[:, None] * (-2.0 * np.pi / n)
    freq[1] = fv[None, :] * (-2.0 * np.pi / n)
    return dict(
        ta=split_table(ta),
        tb=left_table(tb),
        tc1=left_table(tc1),
        tc2=split_table(tc2),
        tf2=np.concatenate(list(split_table(tf2)), axis=0),
        tg1=np.concatenate(list(split_table(tg1)), axis=0),
        tg2=np.concatenate(list(split_table(tg2)), axis=1),
        z=ztab,
        mask=mask.astype(np.float32),
        window=window,
        weight=weight,
        freq=freq,
        scale=float(scale),
    )


def split(x):
    high = x.astype(bf16)
    low = (x - high.astype(f32)).astype(bf16)
    return high, low


def mm_t(a, b):
    return lax.dot_general(a, b, (((1,), (1,)), ((), ())), preferred_element_type=f32)


def mm(a, b):
    return jnp.dot(a, b, preferred_element_type=f32)


def left(table_ref, x):
    high, low = split(x)
    return mm(table_ref[...], jnp.concatenate([high, high, low], axis=0))


def left_rows(table_ref, x):
    high, low = split(x)
    rows = table_ref.shape[0] // 2
    both = mm(table_ref[...], high)
    return both[:rows] + both[rows:] + mm(table_ref[:rows, :], low)


def right(x, table_ref):
    high, low = split(x)
    table = jnp.concatenate([table_ref[0], table_ref[0], table_ref[1]], axis=0)
    return mm(jnp.concatenate([high, low, high], axis=1), table)


def right_t(x, table_ref):
    high, low = split(x)
    table = jnp.concatenate([table_ref[0], table_ref[0], table_ref[1]], axis=1)
    return mm_t(jnp.concatenate([high, low, high], axis=1), table)


def sine(x, quarter):
    turns = jnp.floor(x * (1.0 / math.pi) + (quarter + 0.5))
    part = turns - quarter
    r = x - part * 3.140625
    r = r - part * 9.67502593994140625e-4
    r = r - part * 1.509957990978376432e-7
    r2 = r * r
    poly = 0.008333016341242573 + r2 * (-0.00019806546261204837 + r2 * 2.599901665630011e-06)
    value = r + (r * r2) * (-0.16666657057852008 + r2 * poly)
    pair = turns * 0.5
    return value * (1.0 - 4.0 * (pair - jnp.floor(pair)))


def lane_quarter(shape):
    lane = lax.broadcasted_iota(jnp.int32, shape, len(shape) - 1)
    return jnp.where(lane < 64, 0.5, 0.0).astype(f32)


def pupils(currents, z_ref, mask_ref, pupil_refs):
    items = currents[0].shape[0]
    total = items * len(currents)
    current = jnp.concatenate(currents, axis=0)
    doubled = current + pltpu.roll(current, MPAD, 1)
    high, low = split(doubled[:, : 2 * MPAD])
    stacked = jnp.concatenate([high, low], axis=0)
    quarter = lane_quarter((total, LANES))

    lower = lax.broadcasted_iota(jnp.int32, (total, LANES), 1) < 64

    def two_rows(i, carry):
        both = mm(stacked, z_ref[i])
        phase = both[:total] + both[total:]
        turned = pltpu.roll(phase, 64, 1)
        for k in range(2):
            row = 2 * i + k
            doubled = jnp.where(lower, turned, phase) if k else jnp.where(lower, phase, turned)
            pupil = sine(doubled, quarter) * mask_ref[pl.ds(row, 1), :]
            for c, pupil_ref in enumerate(pupil_refs):
                pupil_ref[pl.ds(pl.multiple_of(row * items, 8), items), :] = pupil[
                    c * items : (c + 1) * items
                ]
        return carry

    lax.fori_loop(0, BOX // 2, two_rows, 0, unroll=4)


def columns(pupil_ref, ta_ref, cols_ref):
    steps = 2
    chunk = pupil_ref.shape[0] // steps
    for i in range(steps):
        rows = slice(i * chunk, (i + 1) * chunk)
        wide = right(pupil_ref[rows, :], ta_ref)
        cols_ref[0, rows, :] = wide[:, :LANES]
        cols_ref[1, rows, :] = wide[:, LANES:]


def item_rows(item):
    if isinstance(item, int):
        return slice(item * HALF, (item + 1) * HALF)
    return pl.ds(pl.multiple_of(item * HALF, 8), HALF)


def half_rows(pair, inside, patches, p, tc1_ref, rows_ref):
    pad = jnp.zeros((FULL - PATCH, 2 * LANES), f32)
    both = left(tc1_ref, jnp.concatenate([pair, pad], axis=0))
    for k, f in enumerate(inside):
        lanes = slice(k * LANES, (k + 1) * LANES)
        rows = item_rows(f * patches + p)
        rows_ref[rows, :LANES] = both[:HALF, lanes]
        rows_ref[rows, LANES:] = both[HALF:, lanes]


def frame_pairs(frames):
    return [range(f, min(f + 2, frames)) for f in range(0, frames, 2)]


def staggered(frames, patches, early, late):
    waiting = None
    for p in range(patches):
        for inside in frame_pairs(frames):
            result = early(p, inside)
            if waiting is not None:
                late(*waiting)
            waiting = (p, inside, result)
    late(*waiting)


def pair_up(values):
    if len(values) % 2:
        values = values + values[-1:]
    return [jnp.concatenate(values[i : i + 2], axis=1) for i in range(0, len(values), 2)]


def transfers(scale, frames, patches, tb_ref, tc1_ref, tc2_ref, cols_ref, focal_ref, rows_ref, transfer_ref):
    items = frames * patches

    def focal_stage(p, inside):
        cols = []
        for f in inside:
            rows = pl.ds(f * patches + p, BOX, stride=items)
            cols.append(jnp.concatenate([cols_ref[0, rows, :], cols_ref[1, rows, :]], axis=0))
        focal = left(tb_ref, pair_up(cols)[0])
        for k, f in enumerate(inside):
            focal_ref[f * patches + p] = focal[:, k * LANES : (k + 1) * LANES]
        real, imag = focal[:PATCH], focal[PATCH:]
        return scale * (real * real + imag * imag)

    def half_stage(p, inside, pair):
        half_rows(pair, inside, patches, p, tc1_ref, rows_ref)

    staggered(frames, patches, focal_stage, half_stage)
    transfer_ref[...] = right(rows_ref[...], tc2_ref)


def estimate_of(data, transfer):
    pairs = [(d[:, :LANES], d[:, LANES:], t[:, :LANES], t[:, LANES:]) for d, t in zip(data, transfer)]
    cross_real = sum(dr * tr + di * ti for dr, di, tr, ti in pairs)
    cross_imag = sum(di * tr - dr * ti for dr, di, tr, ti in pairs)
    power = sum(tr * tr + ti * ti for dr, di, tr, ti in pairs) + damping
    return cross_real / power, cross_imag / power


def gradient_of(data, transfer, est, weight):
    er, ei = est
    double = -2.0 * weight
    grads = []
    for d, t in zip(data, transfer):
        tr, ti = t[:, :LANES], t[:, LANES:]
        mr = d[:, :LANES] - (er * tr - ei * ti)
        mi = d[:, LANES:] - (er * ti + ei * tr)
        grads.append(
            jnp.concatenate([double * (er * mr + ei * mi), double * (er * mi - ei * mr)], axis=1)
        )
    return grads


def back_to_pupil(scale, frames, patches, tc2_ref, tf2_ref, tg1_ref, tg2_ref, grads_ref, focal_ref, rows_ref, back_ref, work_ref):
    items = frames * patches
    rows_ref[...] = right_t(grads_ref[...], tc2_ref)

    def spread_stage(p, inside):
        cols = []
        for f in inside:
            rows = item_rows(f * patches + p)
            cols.append(jnp.concatenate([rows_ref[rows, :LANES], rows_ref[rows, LANES:]], axis=0))
        spread = left_rows(tf2_ref, pair_up(cols)[0]) * (2.0 * scale)
        fields = []
        for k, f in enumerate(inside):
            one = spread[:, k * LANES : (k + 1) * LANES]
            fields.append(focal_ref[f * patches + p] * jnp.concatenate([one, one], axis=0))
        return pair_up(fields)[0]

    def pupil_stage(p, inside, field):
        pupil = left_rows(tg1_ref, field)
        for k, f in enumerate(inside):
            lanes = slice(k * LANES, (k + 1) * LANES)
            rows = item_rows(f * patches + p)
            work_ref[rows, :LANES] = pupil[:BOX, lanes]
            work_ref[rows, LANES:] = pupil[BOX:, lanes]

    staggered(frames, patches, spread_stage, pupil_stage)
    high, low = split(work_ref[...])
    first = mm(high, tg2_ref[...])
    back = first[:, :LANES] + first[:, LANES:] + mm(low, tg2_ref[:, :LANES])
    for item in range(items):
        back_ref[pl.ds(item, BOX, stride=items), :] = back[item * BOX : (item + 1) * BOX]


def coefficient_gradient(items, z_ref, pupil_ref, back_ref):
    lower = lax.broadcasted_iota(jnp.int32, (items, LANES), 1) < 64

    def two_rows(i, total):
        sides = []
        for k in range(2):
            rows = pl.ds(pl.multiple_of((2 * i + k) * items, 8), items)
            product = pupil_ref[rows, :] * back_ref[rows, :]
            sides.append(product + pltpu.roll(product, 64, 1))
        high, low = split(jnp.where(lower, sides[0], sides[1]))
        return total + mm_t(jnp.concatenate([high, low], axis=0), z_ref[i])

    total = lax.fori_loop(
        0, BOX // 2, two_rows, jnp.zeros((2 * items, 2 * MPAD), f32), unroll=4
    )
    total = total[:items] + total[items:]
    total = jnp.concatenate([total, jnp.zeros((items, LANES - 2 * MPAD), f32)], axis=1)
    total = total + pltpu.roll(total, LANES - MPAD, 1)
    lane = lax.broadcasted_iota(jnp.int32, total.shape, 1)
    return jnp.where(lane < MPAD, total, 0.0)


def unpack_pixels(packed):
    lane = lax.broadcasted_iota(jnp.int32, (PACK - 40, LANES), 1)
    third = jnp.concatenate(
        [pltpu.roll(packed[48:56], LANES - 8 - 8 * t, 1) for t in range(3)], axis=0
    )
    rest = jnp.where(
        lane < 40,
        pltpu.roll(packed[:24], 40, 1),
        jnp.where(lane < 80, pltpu.roll(packed[24:48], 80, 1), third),
    )
    return jnp.concatenate([packed, rest], axis=0)


def padded(patches):
    return -(-patches // 8) * 8


def starting_values(start, chunk, patches):
    rows = pl.ds(pl.multiple_of(chunk * padded(patches), 8), padded(patches))
    current = jnp.concatenate([s[rows, :][:patches] for s in start], axis=0)
    lane = lax.broadcasted_iota(jnp.int32, current.shape, 1)
    return jnp.where(lane < MPAD, current, 0.0)


def first_kernel(scale, frames, patches, chunks, *refs):
    start = refs[:frames]
    z_ref, mask_ref, ta_ref, tb_ref, tc1_ref, tc2_ref = refs[frames : frames + 6]
    outs = refs[frames + 6 : frames + 6 + 3 * chunks]
    cols_ref, rows_ref = refs[frames + 6 + 3 * chunks :]
    currents = [starting_values(start, c, patches) for c in range(chunks)]
    pupils(currents, z_ref, mask_ref, [outs[3 * c] for c in range(chunks)])
    for c in range(chunks):
        pupil_ref, focal_ref, transfer_ref = outs[3 * c : 3 * c + 3]
        columns(pupil_ref, ta_ref, cols_ref)
        transfers(
            scale, frames, patches, tb_ref, tc1_ref, tc2_ref, cols_ref, focal_ref, rows_ref, transfer_ref
        )


def middle_kernel(scale, frames, patches, chunk_ref, *refs):
    chunk = chunk_ref[0]
    start = refs[:frames]
    pixels = refs[frames : 2 * frames]
    pupil_ref, focal_ref, transfer_ref = refs[2 * frames : 2 * frames + 3]
    (
        z_ref,
        mask_ref,
        ta_ref,
        tb_ref,
        tc1_ref,
        tc2_ref,
        tf2_ref,
        tg1_ref,
        tg2_ref,
        window_ref,
        weight_ref,
        freq_ref,
    ) = refs[2 * frames + 3 : 2 * frames + 15]
    (
        estimate_out,
        current_out,
        energy_out,
        pupil_out,
        focal_out,
        grads_out,
        data_ref,
        cols_ref,
        back_ref,
        ramp_ref,
        rows_ref,
    ) = refs[2 * frames + 15 :]
    items = frames * patches
    for f in range(frames):
        s = start[f][pl.ds(0, 1), :]
        angle = freq_ref[0] * s[:, MPAD : MPAD + 1] + freq_ref[1] * s[:, MPAD + 1 : MPAD + 2]
        ramp_ref[f, :, :LANES] = sine(angle, 0.5)
        ramp_ref[f, :, LANES:] = sine(angle, 0.0)
    back_args = (tc2_ref, tf2_ref, tg1_ref, tg2_ref)

    def pixel_rows(p, carry):
        window = window_ref[...]
        for inside in frame_pairs(frames):
            planes = [unpack_pixels(pixels[f][p]) * window for f in inside]
            half_rows(pair_up(planes)[0], inside, patches, p, tc1_ref, rows_ref)
        return carry

    lax.fori_loop(0, patches, pixel_rows, 0)
    data_ref[...] = right(rows_ref[...], tc2_ref)

    def first_gradient(p, carry):
        weight = weight_ref[...]
        data = []
        total = None
        for f in range(frames):
            rows = item_rows(f * patches + p)
            real, imag = data_ref[rows, :LANES], data_ref[rows, LANES:]
            cr, ci = ramp_ref[f, :, :LANES], ramp_ref[f, :, LANES:]
            dr, di = real * cr - imag * ci, real * ci + imag * cr
            both = jnp.concatenate([dr, di], axis=1)
            data.append(both)
            data_ref[rows, :] = both
            part = weight * (dr * dr + di * di)
            total = part if total is None else total + part
        energy = jnp.sum(jnp.sum(total, axis=0, keepdims=True), axis=1, keepdims=True)
        for f in range(frames):
            energy_out[pl.ds(f * patches + p, 1), :] = jnp.broadcast_to(energy, (1, LANES))
        transfer = [transfer_ref[item_rows(f * patches + p), :] for f in range(frames)]
        grads = gradient_of(data, transfer, estimate_of(data, transfer), weight)
        for f in range(frames):
            grads_out[item_rows(f * patches + p), :] = grads[f]
        return carry

    lax.fori_loop(0, patches, first_gradient, 0)
    back_to_pupil(scale, frames, patches, *back_args, grads_out, focal_ref, rows_ref, back_ref, grads_out)
    grad = coefficient_gradient(items, z_ref, pupil_ref, back_ref)
    current = starting_values(start, chunk, patches)
    current = current - step_size * frames * grad / energy_out[...]
    current_out[...] = current
    pupils([current], z_ref, mask_ref, [pupil_out])
    columns(pupil_out, ta_ref, cols_ref)
    transfers(
        scale, frames, patches, tb_ref, tc1_ref, tc2_ref, cols_ref, focal_out, rows_ref, grads_out
    )

    def next_gradient(p, carry):
        rows = [item_rows(f * patches + p) for f in range(frames)]
        transfer = [grads_out[r, :] for r in rows]
        data = [data_ref[r, :] for r in rows]
        est = estimate_of(data, transfer)
        estimate_out[p, 0] = est[0] * (1.0 / PATCH)
        estimate_out[p, 1] = est[1] * (1.0 / PATCH)
        grads = gradient_of(data, transfer, est, weight_ref[...])
        for f in range(frames):
            grads_out[rows[f], :] = grads[f]
        return carry

    lax.fori_loop(0, patches, next_gradient, 0)


def last_kernel(scale, frames, patches, chunks, order_ref, *refs):
    states = [refs[5 * c : 5 * c + 5] for c in range(chunks)]
    z_ref, tc2_ref, tf2_ref, tg1_ref, tg2_ref = refs[5 * chunks : 5 * chunks + 5]
    outs = refs[5 * chunks + 5 : 5 * chunks + 5 + frames]
    back_ref, rows_ref, work_ref, final_ref = refs[5 * chunks + 5 + frames :]
    items = frames * patches

    for f in range(frames):
        outs[f][...] = jnp.zeros(outs[f].shape, f32)
    for c in range(chunks):
        current_ref, energy_ref, pupil_ref, focal_ref, grads_ref = states[c]
        back_to_pupil(
            scale, frames, patches, tc2_ref, tf2_ref, tg1_ref, tg2_ref, grads_ref, focal_ref, rows_ref, back_ref, work_ref
        )
        grad = coefficient_gradient(items, z_ref, pupil_ref, back_ref)
        final_ref[...] = current_ref[...] - step_size * frames * grad / energy_ref[...]
        for j in range(patches):
            p = order_ref[c * patches + j]
            for f in range(frames):
                row = f * patches + j
                outs[f][pl.ds(p, 1), :] = final_ref[row : row + 1, :]


def slot_of(axes, me, strip, group, rank):
    frames, strips = axes
    chunks = strips // frames
    owner = lax.div(group, chunks)
    chunk = lax.rem(group + strip, chunks)
    relative = lax.rem(owner - me + frames, frames)
    return relative * chunks + chunk, rank


def prepare_kernel(axes, count, assign_ref, shifts_ref, coefs_ref, *refs):
    frames = axes[0]
    outs = refs[:frames]
    order_ref, sorted_ref, counts_ref = refs[frames:]
    modes = coefs_ref.shape[-1]
    per = count // axes[1]
    room = padded(per)
    me = lax.axis_index("frm")
    strip = lax.axis_index("pat")
    for g in range(axes[1]):
        counts_ref[g] = 0

    def one(p, carry):
        group = assign_ref[p]
        rank = counts_ref[group]
        counts_ref[group] = rank + 1
        piece, place = slot_of(axes, me, strip, group, rank)
        order_ref[piece * per + place] = p
        sorted_ref[pl.ds(piece * room + place, 1), :modes] = coefs_ref[pl.ds(p, 1), :]
        return carry

    sorted_ref[...] = jnp.zeros(sorted_ref.shape, f32)
    lax.fori_loop(0, count, one, 0)
    rows_each = sorted_ref.shape[0] // frames
    lane = lax.broadcasted_iota(jnp.int32, (rows_each, LANES), 1)
    for f in range(frames):
        rows = sorted_ref[f * rows_each : (f + 1) * rows_each, :]
        rows = jnp.where(lane == MPAD, shifts_ref[0, 0], rows)
        outs[f][...] = jnp.where(lane == MPAD + 1, shifts_ref[0, 1], rows)


def cut_kernel(axes, count, chunk, order_ref, anchors_ref, strip_ref, below_ref, *refs):
    frames, strips = axes
    outs, (tall_ref,) = refs[:frames], refs[frames:]
    patches = count // strips
    chunks = strips // frames
    height, width = strip_ref.shape
    tall_ref[:height, :width] = strip_ref[...]
    tall_ref[height : height + PATCH, :width] = below_ref[...]
    first = lax.axis_index("pat") * height

    lane = lax.broadcasted_iota(jnp.int32, (24, LANES), 1)
    for f in range(frames):

        def one(j, carry):
            p = order_ref[(f * chunks + chunk) * patches + j]
            row = anchors_ref[p, 0] - first
            col = anchors_ref[p, 1]
            tile = lax.div(col, LANES)
            base = pl.multiple_of(tile * LANES, LANES)
            above = pl.multiple_of(lax.div(row, 8) * 8, 8)
            block = tall_ref[pl.ds(above, FULL), pl.ds(base, 2 * LANES)]
            back = lax.rem(2 * LANES - (col - base), 2 * LANES)
            block = pltpu.roll(block, back, 1)[:, :LANES]
            block = pltpu.roll(block, lax.rem(FULL - (row - above), FULL), 0)[:PATCH]
            rest = block[PACK:]
            outs[f][j, 0:24, :] = jnp.where(lane < 88, block[0:24], pltpu.roll(rest, 88, 1))
            outs[f][j, 24:48, :] = jnp.where(lane < 88, block[24:48], pltpu.roll(rest, 48, 1))
            third = jnp.where(
                lane[:8] < 96,
                pltpu.roll(rest[:8], 8, 1),
                jnp.where(
                    lane[:8] < 104, pltpu.roll(rest[8:16], 16, 1), pltpu.roll(rest[16:24], 24, 1)
                ),
            )
            outs[f][j, 48:56, :] = jnp.where(lane[:8] < 88, block[48:56], third)
            outs[f][j, 56:64, :] = block[56:64]
            return carry

        lax.fori_loop(0, patches, one, 0, unroll=2)


def call(body, outs, scratch, operands, smem=0, micros=1, after=(), order=0):
    vmem = pl.BlockSpec(memory_space=pltpu.VMEM)
    scalar = pl.BlockSpec(memory_space=pltpu.SMEM)
    whole = pl.BlockSpec(memory_space=pl.ANY)

    def ordered(*refs):
        body(*refs[: len(operands)], *refs[len(operands) + len(after) :])

    return pl.pallas_call(
        ordered,
        out_shape=[jax.ShapeDtypeStruct(s, f32) for s in outs]
        + [jax.ShapeDtypeStruct((order,), jnp.int32)] * bool(order),
        in_specs=[scalar] * smem + [vmem] * (len(operands) - smem) + [whole] * len(after),
        out_specs=[vmem] * len(outs) + [scalar] * bool(order),
        scratch_shapes=scratch,
        cost_estimate=pl.CostEstimate(
            flops=int(micros * 1e9), bytes_accessed=1 << 20, transcendentals=0
        ),
        compiler_params=pltpu.CompilerParams(vmem_limit_bytes=VMEM_LIMIT),
    )(*operands, *after)


def around(value, axis, steps):
    count = lax.axis_size(axis)
    return lax.ppermute(value, axis, [(s, (s + steps) % count) for s in range(count)])


def assemble(half):
    mid = PATCH // 2
    top = half[:, :, : mid + 1, :PATCH]
    nyquist = half[:, :, 1:mid, PATCH : PATCH + 1]
    low = jnp.flip(half[:, :, 1:mid, :PATCH], axis=2)
    low_nyquist = jnp.flip(nyquist, axis=2)
    low = jnp.concatenate(
        [low[..., :1], jnp.flip(low[..., mid + 1 :], axis=3), low_nyquist, jnp.flip(low[..., 1:mid], axis=3)],
        axis=3,
    )
    low = low * jnp.array([1.0, -1.0], f32)[None, :, None, None]
    spectra = jnp.concatenate([top, low], axis=2)
    return spectra.reshape(spectra.shape[0], 2, PATCH * PATCH)


def shards(frames, shifts, coefficients, anchors, assign):
    t = tables()
    scale = t["scale"]
    c = {k: jnp.asarray(v) for k, v in t.items() if k != "scale"}
    height = frames.shape[1]
    width = frames.shape[2]
    count = assign.shape[0]
    n_frm = lax.axis_size("frm")
    n_pat = lax.axis_size("pat")
    axes = (n_frm, n_pat)
    chunks = n_pat // n_frm
    per = count // n_pat
    items = n_frm * per

    upper = frames[0, :PATCH, :]
    below = lax.ppermute(upper, "pat", [(s, s - 1) for s in range(1, n_pat)])
    ready = call(
        functools.partial(prepare_kernel, axes, count),
        [(chunks * padded(per), LANES)] * n_frm,
        [pltpu.VMEM((n_pat * padded(per), LANES), f32), pltpu.SMEM((n_pat,), jnp.int32)],
        [assign, shifts, coefficients[0]],
        smem=2,
        order=count,
        after=[upper],
    )
    order = ready[n_frm]
    start = [ready[0]] + [around(ready[r], "frm", r) for r in range(1, n_frm)]

    state = [(BOX * items, LANES), (items, 2 * PATCH, LANES), (items * HALF, 2 * LANES)]
    wide = pltpu.VMEM((items * HALF, 2 * LANES), f32)

    def cut(k, after):
        pieces = call(
            functools.partial(cut_kernel, axes, count, k),
            [(per, PACK, LANES)] * n_frm,
            [pltpu.VMEM((height + PATCH, width + LANES), f32)],
            [order, anchors, frames[0], below],
            smem=2,
            micros=3,
            after=after,
        )
        return pieces, [pieces[0]] + [around(pieces[r], "frm", r) for r in range(1, n_frm)]

    pieces, sent = cut(0, [])
    pixels = [sent]
    first = call(
        functools.partial(first_kernel, scale, n_frm, per, chunks),
        state * chunks,
        [pltpu.VMEM((2, BOX * items, LANES), f32), wide],
        start + [c[k] for k in ("z", "mask", "ta", "tb", "tc1", "tc2")],
        micros=9,
        after=[pieces[0]],
    )
    for k in range(1, chunks):
        pixels.append(cut(k, [first[2]])[1])

    halves = []
    states = []
    after = []
    for k in range(chunks):
        result = call(
            functools.partial(middle_kernel, scale, n_frm, per),
            [(per, 2, HALF, LANES), (items, LANES), (items, LANES)] + state,
            [
                wide,
                pltpu.VMEM((2, BOX * items, LANES), f32),
                pltpu.VMEM((BOX * items, LANES), f32),
                pltpu.VMEM((n_frm, HALF, 2 * LANES), f32),
                wide,
            ],
            [jnp.full((1,), k, jnp.int32)]
            + start
            + pixels[k]
            + list(first[3 * k : 3 * k + 3])
            + [
                c[name]
                for name in (
                    "z", "mask", "ta", "tb", "tc1", "tc2", "tf2", "tg1", "tg2",
                    "window", "weight", "freq",
                )
            ],
            smem=1,
            micros=12,
            after=after,
        )
        after = [result[2]]
        states += list(result[1:])
        halves.append(send_estimates(axes, k, result[0]))
    finals = call(
        functools.partial(last_kernel, scale, n_frm, per, chunks),
        [(count, LANES)] * n_frm,
        [pltpu.VMEM((BOX * items, LANES), f32), wide, wide, pltpu.VMEM((items, LANES), f32)],
        [order] + states + [c[k] for k in ("z", "tc2", "tf2", "tg1", "tg2")],
        smem=1,
        micros=9,
    )
    parts = [finals[0]] + [around(finals[r], "frm", -r) for r in range(1, n_frm)]
    new_coefficients = sum(parts)[None, :, : coefficients.shape[2]]
    return (new_coefficients, assemble(in_order(axes, halves)))


def send_estimates(axes, k, estimate):
    n_frm, n_pat = axes
    chunks = n_pat // n_frm
    pairs = []
    for f in range(n_frm):
        for s in range(n_pat):
            group = chunks * f + (s + k) % chunks
            pairs.append((f * n_pat + s, (s // chunks) * n_pat + group))
    return lax.ppermute(estimate, ("frm", "pat"), pairs)


def in_order(axes, halves):
    n_frm, n_pat = axes
    chunks = n_pat // n_frm
    side = lax.rem(lax.axis_index("pat"), chunks)
    begin = lax.rem(2 * chunks - 1 - side, chunks)
    stacked = jnp.stack(halves[::-1] * 2)
    ordered = lax.dynamic_slice_in_dim(stacked, begin, chunks, 0)
    return ordered.reshape((-1,) + halves[0].shape[1:])


def solution(mesh):
    in_specs = (
        P("frm", "pat", None),
        P("frm", None),
        P("frm", "pat", None),
        P("pat", None),
        P("pat"),
    )
    out_specs = (P("frm", "pat", None), P(("pat", "frm"), None, None))

    return jax.shard_map(shards, mesh=mesh, in_specs=in_specs, out_specs=out_specs, check_vma=False)
```

```python
import functools
import math

import jax
import jax.numpy as jnp
import ml_dtypes
import numpy as np
from jax import lax
from jax.experimental import pallas as pl
from jax.experimental.pallas import tpu as pltpu
from jax.sharding import PartitionSpec as P

PATCH = 88
MODES = 40

BOX = 48
HALF = 48
MPAD = 48
LANES = 128
PACK = 64
FULL = 96

VMEM_LIMIT = 30 << 20

damping = 0.05
step_size = 64.0
f32 = jnp.float32
bf16 = jnp.bfloat16


def noll_index(j):
    n = 0
    remaining = j - 1
    while remaining > n:
        n += 1
        remaining -= n
    m = (-1) ** j * (n % 2 + 2 * ((remaining + (n + 1) % 2) // 2))
    return (n, m)


def zernike_table(length, number):
    centre = length / 2.0
    coords = (np.arange(length) - centre) / (length / 4.0)
    rows, cols = np.meshgrid(coords, coords, indexing="ij")
    radius = np.sqrt(rows * rows + cols * cols)
    angle = np.arctan2(rows, cols)
    inside = (radius <= 1.0).astype(np.float64)
    surfaces = []
    for j in range(2, number + 2):
        n, m = noll_index(j)
        order = abs(m)
        radial = np.zeros((length, length))
        for k in range((n - order) // 2 + 1):
            factor = (
                (-1) ** k
                * math.factorial(n - k)
                / (
                    math.factorial(k)
                    * math.factorial((n + order) // 2 - k)
                    * math.factorial((n - order) // 2 - k)
                )
            )
            radial = radial + factor * radius ** (n - 2 * k)
        if m == 0:
            surface = math.sqrt(n + 1) * radial
        elif m > 0:
            surface = math.sqrt(2 * (n + 1)) * radial * np.cos(order * angle)
        else:
            surface = math.sqrt(2 * (n + 1)) * radial * np.sin(order * angle)
        surfaces.append(surface * inside)
    return (np.stack(surfaces), inside)


def split_table(table):
    table = np.asarray(table, np.float32)
    high = table.astype(ml_dtypes.bfloat16)
    low = (table - high.astype(np.float32)).astype(ml_dtypes.bfloat16)
    return np.stack([high, low])


def left_table(table):
    high, low = split_table(table)
    return np.concatenate([high, low, high], axis=1)


@functools.lru_cache(None)
def tables():
    n = PATCH
    start = n // 2 - n // 4
    grid = np.arange(n)
    full = np.zeros(LANES, np.int64)
    full[:n] = grid
    full[n] = n // 2
    full_ok = np.zeros(LANES)
    full_ok[: n + 1] = 1.0
    box = start + np.arange(BOX)
    half = np.arange(HALF)
    half_ok = (half <= n // 2).astype(np.float64)
    ang = lambda a, b: 2.0 * np.pi * (np.multiply.outer(a, b) % n) / n
    t = ang(box, grid)
    ta = np.zeros((LANES, 2 * LANES))
    ta[:BOX, :n] = np.cos(t)
    ta[64 : 64 + BOX, :n] = np.sin(t)
    ta[:BOX, LANES : LANES + n] = -np.sin(t)
    ta[64 : 64 + BOX, LANES : LANES + n] = np.cos(t)
    t = ang(grid, box)
    tb = np.block([[np.cos(t), np.sin(t)], [-np.sin(t), np.cos(t)]])
    t = ang(half, grid)
    tc1 = np.zeros((2 * HALF, FULL))
    tc1[:HALF, :n] = np.cos(t) * half_ok[:, None]
    tc1[HALF:, :n] = -np.sin(t) * half_ok[:, None]
    t = ang(grid, full)
    tc2 = np.zeros((2 * LANES, 2 * LANES))
    tc2[:n, :LANES] = np.cos(t) * full_ok
    tc2[:n, LANES:] = -np.sin(t) * full_ok
    tc2[LANES : LANES + n, :LANES] = np.sin(t) * full_ok
    tc2[LANES : LANES + n, LANES:] = np.cos(t) * full_ok
    t = ang(grid, half)
    tf2 = np.concatenate([np.cos(t) * half_ok, -np.sin(t) * half_ok], axis=1)
    t = ang(box, grid)
    tg1 = np.block([[np.cos(t), -np.sin(t)], [np.sin(t), np.cos(t)]])
    t = ang(grid, box)
    tg2 = np.zeros((2 * LANES, LANES))
    tg2[:n, :BOX] = np.sin(t)
    tg2[LANES : LANES + n, :BOX] = np.cos(t)
    tg2[:n, 64 : 64 + BOX] = -np.cos(t)
    tg2[LANES : LANES + n, 64 : 64 + BOX] = np.sin(t)
    modes, inside = zernike_table(n, MODES)
    z = np.zeros((BOX, MPAD, 64))
    mask = np.zeros((BOX, LANES))
    width = min(BOX, n - start)
    cut = slice(start, start + width)
    z[:width, :MODES, :width] = np.transpose(modes[:, cut, cut], (1, 0, 2))
    for off in (0, 64):
        mask[:width, off : off + width] = inside[cut, cut]
    zs = split_table(z)
    ztab = np.concatenate([zs[0], zs[1]], axis=1)
    ztab = np.concatenate([ztab[0::2], ztab[1::2]], axis=2)
    scale = 1.0 / (n * n * inside.sum())
    profile = 0.5 - 0.5 * np.cos(2.0 * np.pi * (grid + 0.5) / n)
    window = np.zeros((n, LANES), np.float32)
    window[:, :n] = profile[:, None] * profile[None, :]
    weight = np.zeros((HALF, LANES), np.float32)
    weight[0, :n] = 1.0
    weight[n // 2, :n] = 1.0
    weight[1 : n // 2, : n + 1] = 2.0
    weight[1 : n // 2, n // 2] = 1.0
    weight[1 : n // 2, n] = 1.0
    fu = np.where(half < n // 2, half, -half) * half_ok
    fv = np.where(full < n // 2, full, full - n) * full_ok
    fv[n] = n // 2
    freq = np.zeros((2, HALF, LANES), np.float32)
    freq[0] = fu[:, None] * (-2.0 * np.pi / n)
    freq[1] = fv[None, :] * (-2.0 * np.pi / n)
    return dict(
        ta=split_table(ta),
        tb=left_table(tb),
        tc1=left_table(tc1),
        tc2=split_table(tc2),
        tf2=np.concatenate(list(split_table(tf2)), axis=0),
        tg1=np.concatenate(list(split_table(tg1)), axis=0),
        tg2=np.concatenate(list(split_table(tg2)), axis=1),
        z=ztab,
        mask=mask.astype(np.float32),
        window=window,
        weight=weight,
        freq=freq,
        scale=float(scale),
    )


def split(x):
    high = x.astype(bf16)
    low = (x - high.astype(f32)).astype(bf16)
    return high, low


def mm_t(a, b):
    return lax.dot_general(a, b, (((1,), (1,)), ((), ())), preferred_element_type=f32)


def mm(a, b):
    return jnp.dot(a, b, preferred_element_type=f32)


def left(table_ref, x):
    high, low = split(x)
    return mm(table_ref[...], jnp.concatenate([high, high, low], axis=0))


def left_rows(table_ref, x):
    high, low = split(x)
    rows = table_ref.shape[0] // 2
    both = mm(table_ref[...], high)
    return both[:rows] + both[rows:] + mm(table_ref[:rows, :], low)


def right(x, table_ref):
    high, low = split(x)
    table = jnp.concatenate([table_ref[0], table_ref[0], table_ref[1]], axis=0)
    return mm(jnp.concatenate([high, low, high], axis=1), table)


def right_t(x, table_ref):
    high, low = split(x)
    table = jnp.concatenate([table_ref[0], table_ref[0], table_ref[1]], axis=1)
    return mm_t(jnp.concatenate([high, low, high], axis=1), table)


def sine(x, quarter):
    turns = jnp.floor(x * (1.0 / math.pi) + (quarter + 0.5))
    part = turns - quarter
    r = x - part * 3.140625
    r = r - part * 9.67502593994140625e-4
    r = r - part * 1.509957990978376432e-7
    r2 = r * r
    poly = 0.008333016341242573 + r2 * (-0.00019806546261204837 + r2 * 2.599901665630011e-06)
    value = r + (r * r2) * (-0.16666657057852008 + r2 * poly)
    pair = turns * 0.5
    return value * (1.0 - 4.0 * (pair - jnp.floor(pair)))


def lane_quarter(shape):
    lane = lax.broadcasted_iota(jnp.int32, shape, len(shape) - 1)
    return jnp.where(lane < 64, 0.5, 0.0).astype(f32)


def pupils(currents, z_ref, mask_ref, pupil_refs):
    items = currents[0].shape[0]
    total = items * len(currents)
    current = jnp.concatenate(currents, axis=0)
    doubled = current + pltpu.roll(current, MPAD, 1)
    high, low = split(doubled[:, : 2 * MPAD])
    stacked = jnp.concatenate([high, low], axis=0)
    quarter = lane_quarter((total, LANES))

    lower = lax.broadcasted_iota(jnp.int32, (total, LANES), 1) < 64

    def two_rows(i, carry):
        both = mm(stacked, z_ref[i])
        phase = both[:total] + both[total:]
        turned = pltpu.roll(phase, 64, 1)
        for k in range(2):
            row = 2 * i + k
            doubled = jnp.where(lower, turned, phase) if k else jnp.where(lower, phase, turned)
            pupil = sine(doubled, quarter) * mask_ref[pl.ds(row, 1), :]
            for c, pupil_ref in enumerate(pupil_refs):
                pupil_ref[pl.ds(pl.multiple_of(row * items, 8), items), :] = pupil[
                    c * items : (c + 1) * items
                ]
        return carry

    lax.fori_loop(0, BOX // 2, two_rows, 0, unroll=4)


def columns(pupil_ref, ta_ref, cols_ref):
    steps = 2
    chunk = pupil_ref.shape[0] // steps
    for i in range(steps):
        rows = slice(i * chunk, (i + 1) * chunk)
        wide = right(pupil_ref[rows, :], ta_ref)
        cols_ref[0, rows, :] = wide[:, :LANES]
        cols_ref[1, rows, :] = wide[:, LANES:]


def item_rows(item):
    if isinstance(item, int):
        return slice(item * HALF, (item + 1) * HALF)
    return pl.ds(pl.multiple_of(item * HALF, 8), HALF)


def half_rows(pair, inside, patches, p, tc1_ref, rows_ref):
    pad = jnp.zeros((FULL - PATCH, 2 * LANES), f32)
    both = left(tc1_ref, jnp.concatenate([pair, pad], axis=0))
    for k, f in enumerate(inside):
        lanes = slice(k * LANES, (k + 1) * LANES)
        rows = item_rows(f * patches + p)
        rows_ref[rows, :LANES] = both[:HALF, lanes]
        rows_ref[rows, LANES:] = both[HALF:, lanes]


def frame_pairs(frames):
    return [range(f, min(f + 2, frames)) for f in range(0, frames, 2)]


def staggered(frames, patches, early, late):
    waiting = None
    for p in range(patches):
        for inside in frame_pairs(frames):
            result = early(p, inside)
            if waiting is not None:
                late(*waiting)
            waiting = (p, inside, result)
    late(*waiting)


def pair_up(values):
    if len(values) % 2:
        values = values + values[-1:]
    return [jnp.concatenate(values[i : i + 2], axis=1) for i in range(0, len(values), 2)]


def transfers(scale, frames, patches, tb_ref, tc1_ref, tc2_ref, cols_ref, focal_ref, rows_ref, transfer_ref):
    items = frames * patches

    def focal_stage(p, inside):
        cols = []
        for f in inside:
            rows = pl.ds(f * patches + p, BOX, stride=items)
            cols.append(jnp.concatenate([cols_ref[0, rows, :], cols_ref[1, rows, :]], axis=0))
        focal = left(tb_ref, pair_up(cols)[0])
        for k, f in enumerate(inside):
            focal_ref[f * patches + p] = focal[:, k * LANES : (k + 1) * LANES]
        real, imag = focal[:PATCH], focal[PATCH:]
        return scale * (real * real + imag * imag)

    def half_stage(p, inside, pair):
        half_rows(pair, inside, patches, p, tc1_ref, rows_ref)

    staggered(frames, patches, focal_stage, half_stage)
    transfer_ref[...] = right(rows_ref[...], tc2_ref)


def estimate_of(data, transfer):
    pairs = [(d[:, :LANES], d[:, LANES:], t[:, :LANES], t[:, LANES:]) for d, t in zip(data, transfer)]
    cross_real = sum(dr * tr + di * ti for dr, di, tr, ti in pairs)
    cross_imag = sum(di * tr - dr * ti for dr, di, tr, ti in pairs)
    power = sum(tr * tr + ti * ti for dr, di, tr, ti in pairs) + damping
    return cross_real / power, cross_imag / power


def gradient_of(data, transfer, est, weight):
    er, ei = est
    double = -2.0 * weight
    grads = []
    for d, t in zip(data, transfer):
        tr, ti = t[:, :LANES], t[:, LANES:]
        mr = d[:, :LANES] - (er * tr - ei * ti)
        mi = d[:, LANES:] - (er * ti + ei * tr)
        grads.append(
            jnp.concatenate([double * (er * mr + ei * mi), double * (er * mi - ei * mr)], axis=1)
        )
    return grads


def back_to_pupil(scale, frames, patches, tc2_ref, tf2_ref, tg1_ref, tg2_ref, grads_ref, focal_ref, rows_ref, back_ref, work_ref):
    items = frames * patches
    rows_ref[...] = right_t(grads_ref[...], tc2_ref)

    def spread_stage(p, inside):
        cols = []
        for f in inside:
            rows = item_rows(f * patches + p)
            cols.append(jnp.concatenate([rows_ref[rows, :LANES], rows_ref[rows, LANES:]], axis=0))
        spread = left_rows(tf2_ref, pair_up(cols)[0]) * (2.0 * scale)
        fields = []
        for k, f in enumerate(inside):
            one = spread[:, k * LANES : (k + 1) * LANES]
            fields.append(focal_ref[f * patches + p] * jnp.concatenate([one, one], axis=0))
        return pair_up(fields)[0]

    def pupil_stage(p, inside, field):
        pupil = left_rows(tg1_ref, field)
        for k, f in enumerate(inside):
            lanes = slice(k * LANES, (k + 1) * LANES)
            rows = item_rows(f * patches + p)
            work_ref[rows, :LANES] = pupil[:BOX, lanes]
            work_ref[rows, LANES:] = pupil[BOX:, lanes]

    staggered(frames, patches, spread_stage, pupil_stage)
    high, low = split(work_ref[...])
    first = mm(high, tg2_ref[...])
    back = first[:, :LANES] + first[:, LANES:] + mm(low, tg2_ref[:, :LANES])
    for item in range(items):
        back_ref[pl.ds(item, BOX, stride=items), :] = back[item * BOX : (item + 1) * BOX]


def coefficient_gradient(items, z_ref, pupil_ref, back_ref):
    lower = lax.broadcasted_iota(jnp.int32, (items, LANES), 1) < 64

    def two_rows(i, total):
        sides = []
        for k in range(2):
            rows = pl.ds(pl.multiple_of((2 * i + k) * items, 8), items)
            product = pupil_ref[rows, :] * back_ref[rows, :]
            sides.append(product + pltpu.roll(product, 64, 1))
        high, low = split(jnp.where(lower, sides[0], sides[1]))
        return total + mm_t(jnp.concatenate([high, low], axis=0), z_ref[i])

    total = lax.fori_loop(
        0, BOX // 2, two_rows, jnp.zeros((2 * items, 2 * MPAD), f32), unroll=4
    )
    total = total[:items] + total[items:]
    total = jnp.concatenate([total, jnp.zeros((items, LANES - 2 * MPAD), f32)], axis=1)
    total = total + pltpu.roll(total, LANES - MPAD, 1)
    lane = lax.broadcasted_iota(jnp.int32, total.shape, 1)
    return jnp.where(lane < MPAD, total, 0.0)


def unpack_pixels(packed):
    lane = lax.broadcasted_iota(jnp.int32, (PACK - 40, LANES), 1)
    third = jnp.concatenate(
        [pltpu.roll(packed[48:56], LANES - 8 - 8 * t, 1) for t in range(3)], axis=0
    )
    rest = jnp.where(
        lane < 40,
        pltpu.roll(packed[:24], 40, 1),
        jnp.where(lane < 80, pltpu.roll(packed[24:48], 80, 1), third),
    )
    return jnp.concatenate([packed, rest], axis=0)


def padded(patches):
    return -(-patches // 8) * 8


def starting_values(start, chunk, patches):
    rows = pl.ds(pl.multiple_of(chunk * padded(patches), 8), padded(patches))
    current = jnp.concatenate([s[rows, :][:patches] for s in start], axis=0)
    lane = lax.broadcasted_iota(jnp.int32, current.shape, 1)
    return jnp.where(lane < MPAD, current, 0.0)


def first_kernel(scale, frames, patches, chunk, *refs):
    start = refs[:frames]
    z_ref, mask_ref, ta_ref, tb_ref, tc1_ref, tc2_ref = refs[frames : frames + 6]
    pupil_ref, focal_ref, transfer_ref, cols_ref, rows_ref = refs[frames + 6 :]
    pupils([starting_values(start, chunk, patches)], z_ref, mask_ref, [pupil_ref])
    columns(pupil_ref, ta_ref, cols_ref)
    transfers(
        scale, frames, patches, tb_ref, tc1_ref, tc2_ref, cols_ref, focal_ref, rows_ref, transfer_ref
    )


def middle_kernel(scale, frames, patches, chunk_ref, *refs):
    chunk = chunk_ref[0]
    start = refs[:frames]
    pixels = refs[frames : 2 * frames]
    pupil_ref, focal_ref, transfer_ref = refs[2 * frames : 2 * frames + 3]
    (
        z_ref,
        mask_ref,
        ta_ref,
        tb_ref,
        tc1_ref,
        tc2_ref,
        tf2_ref,
        tg1_ref,
        tg2_ref,
        window_ref,
        weight_ref,
        freq_ref,
    ) = refs[2 * frames + 3 : 2 * frames + 15]
    (
        estimate_out,
        current_out,
        energy_out,
        pupil_out,
        focal_out,
        grads_out,
        data_ref,
        cols_ref,
        back_ref,
        ramp_ref,
        rows_ref,
    ) = refs[2 * frames + 15 :]
    items = frames * patches
    for f in range(frames):
        s = start[f][pl.ds(0, 1), :]
        angle = freq_ref[0] * s[:, MPAD : MPAD + 1] + freq_ref[1] * s[:, MPAD + 1 : MPAD + 2]
        ramp_ref[f, :, :LANES] = sine(angle, 0.5)
        ramp_ref[f, :, LANES:] = sine(angle, 0.0)
    back_args = (tc2_ref, tf2_ref, tg1_ref, tg2_ref)

    def pixel_rows(p, carry):
        window = window_ref[...]
        for inside in frame_pairs(frames):
            planes = [unpack_pixels(pixels[f][p]) * window for f in inside]
            half_rows(pair_up(planes)[0], inside, patches, p, tc1_ref, rows_ref)
        return carry

    lax.fori_loop(0, patches, pixel_rows, 0)
    data_ref[...] = right(rows_ref[...], tc2_ref)

    def first_gradient(p, carry):
        weight = weight_ref[...]
        data = []
        total = None
        for f in range(frames):
            rows = item_rows(f * patches + p)
            real, imag = data_ref[rows, :LANES], data_ref[rows, LANES:]
            cr, ci = ramp_ref[f, :, :LANES], ramp_ref[f, :, LANES:]
            dr, di = real * cr - imag * ci, real * ci + imag * cr
            both = jnp.concatenate([dr, di], axis=1)
            data.append(both)
            data_ref[rows, :] = both
            part = weight * (dr * dr + di * di)
            total = part if total is None else total + part
        energy = jnp.sum(jnp.sum(total, axis=0, keepdims=True), axis=1, keepdims=True)
        for f in range(frames):
            energy_out[pl.ds(f * patches + p, 1), :] = jnp.broadcast_to(energy, (1, LANES))
        transfer = [transfer_ref[item_rows(f * patches + p), :] for f in range(frames)]
        grads = gradient_of(data, transfer, estimate_of(data, transfer), weight)
        for f in range(frames):
            grads_out[item_rows(f * patches + p), :] = grads[f]
        return carry

    lax.fori_loop(0, patches, first_gradient, 0)
    back_to_pupil(scale, frames, patches, *back_args, grads_out, focal_ref, rows_ref, back_ref, grads_out)
    grad = coefficient_gradient(items, z_ref, pupil_ref, back_ref)
    current = starting_values(start, chunk, patches)
    current = current - step_size * frames * grad / energy_out[...]
    current_out[...] = current
    pupils([current], z_ref, mask_ref, [pupil_out])
    columns(pupil_out, ta_ref, cols_ref)
    transfers(
        scale, frames, patches, tb_ref, tc1_ref, tc2_ref, cols_ref, focal_out, rows_ref, grads_out
    )

    def next_gradient(p, carry):
        rows = [item_rows(f * patches + p) for f in range(frames)]
        transfer = [grads_out[r, :] for r in rows]
        data = [data_ref[r, :] for r in rows]
        est = estimate_of(data, transfer)
        estimate_out[p, 0] = est[0] * (1.0 / PATCH)
        estimate_out[p, 1] = est[1] * (1.0 / PATCH)
        grads = gradient_of(data, transfer, est, weight_ref[...])
        for f in range(frames):
            grads_out[rows[f], :] = grads[f]
        return carry

    lax.fori_loop(0, patches, next_gradient, 0)


def last_kernel(scale, frames, patches, chunks, order_ref, *refs):
    states = [refs[5 * c : 5 * c + 5] for c in range(chunks)]
    z_ref, tc2_ref, tf2_ref, tg1_ref, tg2_ref = refs[5 * chunks : 5 * chunks + 5]
    outs = refs[5 * chunks + 5 : 5 * chunks + 5 + frames]
    back_ref, rows_ref, work_ref, final_ref = refs[5 * chunks + 5 + frames :]
    items = frames * patches

    for f in range(frames):
        outs[f][...] = jnp.zeros(outs[f].shape, f32)
    for c in range(chunks):
        current_ref, energy_ref, pupil_ref, focal_ref, grads_ref = states[c]
        back_to_pupil(
            scale, frames, patches, tc2_ref, tf2_ref, tg1_ref, tg2_ref, grads_ref, focal_ref, rows_ref, back_ref, work_ref
        )
        grad = coefficient_gradient(items, z_ref, pupil_ref, back_ref)
        final_ref[...] = current_ref[...] - step_size * frames * grad / energy_ref[...]
        for j in range(patches):
            p = order_ref[c * patches + j]
            for f in range(frames):
                row = f * patches + j
                outs[f][pl.ds(p, 1), :] = final_ref[row : row + 1, :]


def slot_of(axes, me, strip, group, rank):
    frames, strips = axes
    chunks = strips // frames
    owner = lax.div(group, chunks)
    chunk = lax.rem(group + strip, chunks)
    relative = lax.rem(owner - me + frames, frames)
    return relative * chunks + chunk, rank


def prepare_kernel(axes, count, assign_ref, shifts_ref, coefs_ref, *refs):
    frames = axes[0]
    outs = refs[:frames]
    order_ref, sorted_ref, counts_ref = refs[frames:]
    modes = coefs_ref.shape[-1]
    per = count // axes[1]
    room = padded(per)
    me = lax.axis_index("frm")
    strip = lax.axis_index("pat")
    for g in range(axes[1]):
        counts_ref[g] = 0

    def one(p, carry):
        group = assign_ref[p]
        rank = counts_ref[group]
        counts_ref[group] = rank + 1
        piece, place = slot_of(axes, me, strip, group, rank)
        order_ref[piece * per + place] = p
        sorted_ref[pl.ds(piece * room + place, 1), :modes] = coefs_ref[pl.ds(p, 1), :]
        return carry

    sorted_ref[...] = jnp.zeros(sorted_ref.shape, f32)
    lax.fori_loop(0, count, one, 0)
    rows_each = sorted_ref.shape[0] // frames
    lane = lax.broadcasted_iota(jnp.int32, (rows_each, LANES), 1)
    for f in range(frames):
        rows = sorted_ref[f * rows_each : (f + 1) * rows_each, :]
        rows = jnp.where(lane == MPAD, shifts_ref[0, 0], rows)
        outs[f][...] = jnp.where(lane == MPAD + 1, shifts_ref[0, 1], rows)


def cut_kernel(axes, count, chunk, order_ref, anchors_ref, strip_ref, below_ref, *refs):
    frames, strips = axes
    outs, (tall_ref,) = refs[:frames], refs[frames:]
    patches = count // strips
    chunks = strips // frames
    height, width = strip_ref.shape
    tall_ref[:height, :width] = strip_ref[...]
    tall_ref[height : height + PATCH, :width] = below_ref[...]
    first = lax.axis_index("pat") * height

    lane = lax.broadcasted_iota(jnp.int32, (24, LANES), 1)
    for f in range(frames):

        def one(j, carry):
            p = order_ref[(f * chunks + chunk) * patches + j]
            row = anchors_ref[p, 0] - first
            col = anchors_ref[p, 1]
            tile = lax.div(col, LANES)
            base = pl.multiple_of(tile * LANES, LANES)
            above = pl.multiple_of(lax.div(row, 8) * 8, 8)
            block = tall_ref[pl.ds(above, FULL), pl.ds(base, 2 * LANES)]
            back = lax.rem(2 * LANES - (col - base), 2 * LANES)
            block = pltpu.roll(block, back, 1)[:, :LANES]
            block = pltpu.roll(block, lax.rem(FULL - (row - above), FULL), 0)[:PATCH]
            rest = block[PACK:]
            outs[f][j, 0:24, :] = jnp.where(lane < 88, block[0:24], pltpu.roll(rest, 88, 1))
            outs[f][j, 24:48, :] = jnp.where(lane < 88, block[24:48], pltpu.roll(rest, 48, 1))
            third = jnp.where(
                lane[:8] < 96,
                pltpu.roll(rest[:8], 8, 1),
                jnp.where(
                    lane[:8] < 104, pltpu.roll(rest[8:16], 16, 1), pltpu.roll(rest[16:24], 24, 1)
                ),
            )
            outs[f][j, 48:56, :] = jnp.where(lane[:8] < 88, block[48:56], third)
            outs[f][j, 56:64, :] = block[56:64]
            return carry

        lax.fori_loop(0, patches, one, 0, unroll=2)


def call(body, outs, scratch, operands, smem=0, micros=1, after=(), order=0):
    vmem = pl.BlockSpec(memory_space=pltpu.VMEM)
    scalar = pl.BlockSpec(memory_space=pltpu.SMEM)
    whole = pl.BlockSpec(memory_space=pl.ANY)

    def ordered(*refs):
        body(*refs[: len(operands)], *refs[len(operands) + len(after) :])

    return pl.pallas_call(
        ordered,
        out_shape=[jax.ShapeDtypeStruct(s, f32) for s in outs]
        + [jax.ShapeDtypeStruct((order,), jnp.int32)] * bool(order),
        in_specs=[scalar] * smem + [vmem] * (len(operands) - smem) + [whole] * len(after),
        out_specs=[vmem] * len(outs) + [scalar] * bool(order),
        scratch_shapes=scratch,
        cost_estimate=pl.CostEstimate(
            flops=int(micros * 1e9), bytes_accessed=1 << 20, transcendentals=0
        ),
        compiler_params=pltpu.CompilerParams(vmem_limit_bytes=VMEM_LIMIT),
    )(*operands, *after)


def around(value, axis, steps):
    count = lax.axis_size(axis)
    return lax.ppermute(value, axis, [(s, (s + steps) % count) for s in range(count)])


def assemble(half):
    mid = PATCH // 2
    top = half[:, :, : mid + 1, :PATCH]
    nyquist = half[:, :, 1:mid, PATCH : PATCH + 1]
    low = jnp.flip(half[:, :, 1:mid, :PATCH], axis=2)
    low_nyquist = jnp.flip(nyquist, axis=2)
    low = jnp.concatenate(
        [low[..., :1], jnp.flip(low[..., mid + 1 :], axis=3), low_nyquist, jnp.flip(low[..., 1:mid], axis=3)],
        axis=3,
    )
    low = low * jnp.array([1.0, -1.0], f32)[None, :, None, None]
    spectra = jnp.concatenate([top, low], axis=2)
    return spectra.reshape(spectra.shape[0], 2, PATCH * PATCH)


def shards(frames, shifts, coefficients, anchors, assign):
    t = tables()
    scale = t["scale"]
    c = {k: jnp.asarray(v) for k, v in t.items() if k != "scale"}
    height = frames.shape[1]
    width = frames.shape[2]
    count = assign.shape[0]
    n_frm = lax.axis_size("frm")
    n_pat = lax.axis_size("pat")
    axes = (n_frm, n_pat)
    chunks = n_pat // n_frm
    per = count // n_pat
    items = n_frm * per

    upper = frames[0, :PATCH, :]
    below = lax.ppermute(upper, "pat", [(s, s - 1) for s in range(1, n_pat)])
    ready = call(
        functools.partial(prepare_kernel, axes, count),
        [(chunks * padded(per), LANES)] * n_frm,
        [pltpu.VMEM((n_pat * padded(per), LANES), f32), pltpu.SMEM((n_pat,), jnp.int32)],
        [assign, shifts, coefficients[0]],
        smem=2,
        order=count,
        after=[upper],
    )
    order = ready[n_frm]
    start = [ready[0]] + [around(ready[r], "frm", r) for r in range(1, n_frm)]

    state = [(BOX * items, LANES), (items, 2 * PATCH, LANES), (items * HALF, 2 * LANES)]
    wide = pltpu.VMEM((items * HALF, 2 * LANES), f32)

    def cut(k, after):
        pieces = call(
            functools.partial(cut_kernel, axes, count, k),
            [(per, PACK, LANES)] * n_frm,
            [pltpu.VMEM((height + PATCH, width + LANES), f32)],
            [order, anchors, frames[0], below],
            smem=2,
            micros=3,
            after=after,
        )
        return pieces, [pieces[0]] + [around(pieces[r], "frm", r) for r in range(1, n_frm)]

    def first_pass(k, after):
        return call(
            functools.partial(first_kernel, scale, n_frm, per, k),
            state,
            [pltpu.VMEM((2, BOX * items, LANES), f32), wide],
            start + [c[name] for name in ("z", "mask", "ta", "tb", "tc1", "tc2")],
            micros=4,
            after=after,
        )

    first = first_pass(0, [])
    pixels = []
    for k in range(chunks):
        pieces, sent = cut(k, [first[3 * k + 2]])
        pixels.append(sent)
        if k + 1 < chunks:
            first += first_pass(k + 1, [pieces[0]])

    halves = []
    states = []
    after = []
    for k in range(chunks):
        result = call(
            functools.partial(middle_kernel, scale, n_frm, per),
            [(per, 2, HALF, LANES), (items, LANES), (items, LANES)] + state,
            [
                wide,
                pltpu.VMEM((2, BOX * items, LANES), f32),
                pltpu.VMEM((BOX * items, LANES), f32),
                pltpu.VMEM((n_frm, HALF, 2 * LANES), f32),
                wide,
            ],
            [jnp.full((1,), k, jnp.int32)]
            + start
            + pixels[k]
            + list(first[3 * k : 3 * k + 3])
            + [
                c[name]
                for name in (
                    "z", "mask", "ta", "tb", "tc1", "tc2", "tf2", "tg1", "tg2",
                    "window", "weight", "freq",
                )
            ],
            smem=1,
            micros=12,
            after=after,
        )
        after = [result[2]]
        states += list(result[1:])
        halves.append(send_estimates(axes, k, result[0]))
    finals = call(
        functools.partial(last_kernel, scale, n_frm, per, chunks),
        [(count, LANES)] * n_frm,
        [pltpu.VMEM((BOX * items, LANES), f32), wide, wide, pltpu.VMEM((items, LANES), f32)],
        [order] + states + [c[k] for k in ("z", "tc2", "tf2", "tg1", "tg2")],
        smem=1,
        micros=9,
    )
    parts = [finals[0]]
    for r in range(1, n_frm):
        parts.append(around(finals[r], "frm", -r))
    new_coefficients = sum(parts)[None, :, : coefficients.shape[2]]
    object_spectra = assemble(in_order(axes, halves))
    return (new_coefficients, object_spectra)


def send_estimates(axes, k, estimate):
    n_frm, n_pat = axes
    chunks = n_pat // n_frm
    pairs = []
    for f in range(n_frm):
        for s in range(n_pat):
            group = chunks * f + (s + k) % chunks
            pairs.append((f * n_pat + s, (s // chunks) * n_pat + group))
    return lax.ppermute(estimate, ("frm", "pat"), pairs)


def in_order(axes, halves):
    n_frm, n_pat = axes
    chunks = n_pat // n_frm
    side = lax.rem(lax.axis_index("pat"), chunks)
    begin = lax.rem(2 * chunks - 1 - side, chunks)
    stacked = jnp.stack(halves[::-1] * 2)
    ordered = lax.dynamic_slice_in_dim(stacked, begin, chunks, 0)
    return ordered.reshape((-1,) + halves[0].shape[1:])


def solution(mesh):
    in_specs = (
        P("frm", "pat", None),
        P("frm", None),
        P("frm", "pat", None),
        P("pat", None),
        P("pat"),
    )
    out_specs = (P("frm", "pat", None), P(("pat", "frm"), None, None))

    return jax.shard_map(shards, mesh=mesh, in_specs=in_specs, out_specs=out_specs, check_vma=False)
```

```python
import functools
import math

import jax
import jax.numpy as jnp
import ml_dtypes
import numpy as np
from jax import lax
from jax.experimental import pallas as pl
from jax.experimental.pallas import tpu as pltpu
from jax.sharding import PartitionSpec as P

PATCH = 88
MODES = 40

BOX = 48
HALF = 48
MPAD = 48
LANES = 128
PACK = 64
FULL = 96

VMEM_LIMIT = 30 << 20

damping = 0.05
step_size = 64.0
f32 = jnp.float32
bf16 = jnp.bfloat16


def noll_index(j):
    n = 0
    remaining = j - 1
    while remaining > n:
        n += 1
        remaining -= n
    m = (-1) ** j * (n % 2 + 2 * ((remaining + (n + 1) % 2) // 2))
    return (n, m)


def zernike_table(length, number):
    centre = length / 2.0
    coords = (np.arange(length) - centre) / (length / 4.0)
    rows, cols = np.meshgrid(coords, coords, indexing="ij")
    radius = np.sqrt(rows * rows + cols * cols)
    angle = np.arctan2(rows, cols)
    inside = (radius <= 1.0).astype(np.float64)
    surfaces = []
    for j in range(2, number + 2):
        n, m = noll_index(j)
        order = abs(m)
        radial = np.zeros((length, length))
        for k in range((n - order) // 2 + 1):
            factor = (
                (-1) ** k
                * math.factorial(n - k)
                / (
                    math.factorial(k)
                    * math.factorial((n + order) // 2 - k)
                    * math.factorial((n - order) // 2 - k)
                )
            )
            radial = radial + factor * radius ** (n - 2 * k)
        if m == 0:
            surface = math.sqrt(n + 1) * radial
        elif m > 0:
            surface = math.sqrt(2 * (n + 1)) * radial * np.cos(order * angle)
        else:
            surface = math.sqrt(2 * (n + 1)) * radial * np.sin(order * angle)
        surfaces.append(surface * inside)
    return (np.stack(surfaces), inside)


def split_table(table):
    table = np.asarray(table, np.float32)
    high = table.astype(ml_dtypes.bfloat16)
    low = (table - high.astype(np.float32)).astype(ml_dtypes.bfloat16)
    return np.stack([high, low])


def left_table(table):
    high, low = split_table(table)
    return np.concatenate([high, low, high], axis=1)


@functools.lru_cache(None)
def tables():
    n = PATCH
    start = n // 2 - n // 4
    grid = np.arange(n)
    full = np.zeros(LANES, np.int64)
    full[:n] = grid
    full[n] = n // 2
    full_ok = np.zeros(LANES)
    full_ok[: n + 1] = 1.0
    box = start + np.arange(BOX)
    half = np.arange(HALF)
    half_ok = (half <= n // 2).astype(np.float64)
    ang = lambda a, b: 2.0 * np.pi * (np.multiply.outer(a, b) % n) / n
    t = ang(box, grid)
    ta = np.zeros((LANES, 2 * LANES))
    ta[:BOX, :n] = np.cos(t)
    ta[64 : 64 + BOX, :n] = np.sin(t)
    ta[:BOX, LANES : LANES + n] = -np.sin(t)
    ta[64 : 64 + BOX, LANES : LANES + n] = np.cos(t)
    t = ang(grid, box)
    tb = np.block([[np.cos(t), np.sin(t)], [-np.sin(t), np.cos(t)]])
    t = ang(half, grid)
    tc1 = np.zeros((2 * HALF, FULL))
    tc1[:HALF, :n] = np.cos(t) * half_ok[:, None]
    tc1[HALF:, :n] = -np.sin(t) * half_ok[:, None]
    t = ang(grid, full)
    tc2 = np.zeros((2 * LANES, 2 * LANES))
    tc2[:n, :LANES] = np.cos(t) * full_ok
    tc2[:n, LANES:] = -np.sin(t) * full_ok
    tc2[LANES : LANES + n, :LANES] = np.sin(t) * full_ok
    tc2[LANES : LANES + n, LANES:] = np.cos(t) * full_ok
    t = ang(grid, half)
    tf2 = np.concatenate([np.cos(t) * half_ok, -np.sin(t) * half_ok], axis=1)
    t = ang(box, grid)
    tg1 = np.block([[np.cos(t), -np.sin(t)], [np.sin(t), np.cos(t)]])
    t = ang(grid, box)
    tg2 = np.zeros((2 * LANES, LANES))
    tg2[:n, :BOX] = np.sin(t)
    tg2[LANES : LANES + n, :BOX] = np.cos(t)
    tg2[:n, 64 : 64 + BOX] = -np.cos(t)
    tg2[LANES : LANES + n, 64 : 64 + BOX] = np.sin(t)
    modes, inside = zernike_table(n, MODES)
    z = np.zeros((BOX, MPAD, 64))
    mask = np.zeros((BOX, LANES))
    width = min(BOX, n - start)
    cut = slice(start, start + width)
    z[:width, :MODES, :width] = np.transpose(modes[:, cut, cut], (1, 0, 2))
    for off in (0, 64):
        mask[:width, off : off + width] = inside[cut, cut]
    zs = split_table(z)
    ztab = np.concatenate([zs[0], zs[1]], axis=1)
    ztab = np.concatenate([ztab[0::2], ztab[1::2]], axis=2)
    scale = 1.0 / (n * n * inside.sum())
    profile = 0.5 - 0.5 * np.cos(2.0 * np.pi * (grid + 0.5) / n)
    window = np.zeros((n, LANES), np.float32)
    window[:, :n] = profile[:, None] * profile[None, :]
    weight = np.zeros((HALF, LANES), np.float32)
    weight[0, :n] = 1.0
    weight[n // 2, :n] = 1.0
    weight[1 : n // 2, : n + 1] = 2.0
    weight[1 : n // 2, n // 2] = 1.0
    weight[1 : n // 2, n] = 1.0
    fu = np.where(half < n // 2, half, -half) * half_ok
    fv = np.where(full < n // 2, full, full - n) * full_ok
    fv[n] = n // 2
    freq = np.zeros((2, HALF, LANES), np.float32)
    freq[0] = fu[:, None] * (-2.0 * np.pi / n)
    freq[1] = fv[None, :] * (-2.0 * np.pi / n)
    return dict(
        ta=split_table(ta),
        tb=left_table(tb),
        tc1=left_table(tc1),
        tc2=split_table(tc2),
        tf2=np.concatenate(list(split_table(tf2)), axis=0),
        tg1=np.concatenate(list(split_table(tg1)), axis=0),
        tg2=np.concatenate(list(split_table(tg2)), axis=1),
        z=ztab,
        mask=mask.astype(np.float32),
        window=window,
        weight=weight,
        freq=freq,
        scale=float(scale),
    )


def split(x):
    high = x.astype(bf16)
    low = (x - high.astype(f32)).astype(bf16)
    return high, low


def mm_t(a, b):
    return lax.dot_general(a, b, (((1,), (1,)), ((), ())), preferred_element_type=f32)


def mm(a, b):
    return jnp.dot(a, b, preferred_element_type=f32)


def left(table_ref, x):
    high, low = split(x)
    return mm(table_ref[...], jnp.concatenate([high, high, low], axis=0))


def left_rows(table_ref, x):
    high, low = split(x)
    rows = table_ref.shape[0] // 2
    both = mm(table_ref[...], high)
    return both[:rows] + both[rows:] + mm(table_ref[:rows, :], low)


def right(x, table_ref):
    high, low = split(x)
    table = jnp.concatenate([table_ref[0], table_ref[0], table_ref[1]], axis=0)
    return mm(jnp.concatenate([high, low, high], axis=1), table)


def right_t(x, table_ref):
    high, low = split(x)
    table = jnp.concatenate([table_ref[0], table_ref[0], table_ref[1]], axis=1)
    return mm_t(jnp.concatenate([high, low, high], axis=1), table)


def sine(x, quarter):
    turns = jnp.floor(x * (1.0 / math.pi) + (quarter + 0.5))
    part = turns - quarter
    r = x - part * 3.140625
    r = r - part * 9.67502593994140625e-4
    r = r - part * 1.509957990978376432e-7
    r2 = r * r
    poly = 0.008333016341242573 + r2 * (-0.00019806546261204837 + r2 * 2.599901665630011e-06)
    value = r + (r * r2) * (-0.16666657057852008 + r2 * poly)
    pair = turns * 0.5
    return value * (1.0 - 4.0 * (pair - jnp.floor(pair)))


def lane_quarter(shape):
    lane = lax.broadcasted_iota(jnp.int32, shape, len(shape) - 1)
    return jnp.where(lane < 64, 0.5, 0.0).astype(f32)


def pupils(currents, z_ref, mask_ref, pupil_refs):
    items = currents[0].shape[0]
    total = items * len(currents)
    current = jnp.concatenate(currents, axis=0)
    doubled = current + pltpu.roll(current, MPAD, 1)
    high, low = split(doubled[:, : 2 * MPAD])
    stacked = jnp.concatenate([high, low], axis=0)
    quarter = lane_quarter((total, LANES))

    lower = lax.broadcasted_iota(jnp.int32, (total, LANES), 1) < 64

    def two_rows(i, carry):
        both = mm(stacked, z_ref[i])
        phase = both[:total] + both[total:]
        turned = pltpu.roll(phase, 64, 1)
        for k in range(2):
            row = 2 * i + k
            doubled = jnp.where(lower, turned, phase) if k else jnp.where(lower, phase, turned)
            pupil = sine(doubled, quarter) * mask_ref[pl.ds(row, 1), :]
            for c, pupil_ref in enumerate(pupil_refs):
                pupil_ref[pl.ds(pl.multiple_of(row * items, 8), items), :] = pupil[
                    c * items : (c + 1) * items
                ]
        return carry

    lax.fori_loop(0, BOX // 2, two_rows, 0, unroll=4)


def columns(pupil_ref, ta_ref, cols_ref):
    steps = 2
    chunk = pupil_ref.shape[0] // steps
    for i in range(steps):
        rows = slice(i * chunk, (i + 1) * chunk)
        wide = right(pupil_ref[rows, :], ta_ref)
        cols_ref[0, rows, :] = wide[:, :LANES]
        cols_ref[1, rows, :] = wide[:, LANES:]


def item_rows(item):
    if isinstance(item, int):
        return slice(item * HALF, (item + 1) * HALF)
    return pl.ds(pl.multiple_of(item * HALF, 8), HALF)


def half_rows(pair, inside, patches, p, tc1_ref, rows_ref):
    pad = jnp.zeros((FULL - PATCH, 2 * LANES), f32)
    both = left(tc1_ref, jnp.concatenate([pair, pad], axis=0))
    for k, f in enumerate(inside):
        lanes = slice(k * LANES, (k + 1) * LANES)
        rows = item_rows(f * patches + p)
        rows_ref[rows, :LANES] = both[:HALF, lanes]
        rows_ref[rows, LANES:] = both[HALF:, lanes]


def frame_pairs(frames):
    return [range(f, min(f + 2, frames)) for f in range(0, frames, 2)]


def staggered(frames, patches, early, late):
    waiting = None
    for p in range(patches):
        for inside in frame_pairs(frames):
            result = early(p, inside)
            if waiting is not None:
                late(*waiting)
            waiting = (p, inside, result)
    late(*waiting)


def pair_up(values):
    if len(values) % 2:
        values = values + values[-1:]
    return [jnp.concatenate(values[i : i + 2], axis=1) for i in range(0, len(values), 2)]


def transfers(scale, frames, patches, tb_ref, tc1_ref, tc2_ref, cols_ref, focal_ref, rows_ref, transfer_ref):
    items = frames * patches

    def focal_stage(p, inside):
        cols = []
        for f in inside:
            rows = pl.ds(f * patches + p, BOX, stride=items)
            cols.append(jnp.concatenate([cols_ref[0, rows, :], cols_ref[1, rows, :]], axis=0))
        focal = left(tb_ref, pair_up(cols)[0])
        for k, f in enumerate(inside):
            focal_ref[f * patches + p] = focal[:, k * LANES : (k + 1) * LANES]
        real, imag = focal[:PATCH], focal[PATCH:]
        return scale * (real * real + imag * imag)

    def half_stage(p, inside, pair):
        half_rows(pair, inside, patches, p, tc1_ref, rows_ref)

    staggered(frames, patches, focal_stage, half_stage)
    transfer_ref[...] = right(rows_ref[...], tc2_ref)


def estimate_of(data, transfer):
    pairs = [(d[:, :LANES], d[:, LANES:], t[:, :LANES], t[:, LANES:]) for d, t in zip(data, transfer)]
    cross_real = sum(dr * tr + di * ti for dr, di, tr, ti in pairs)
    cross_imag = sum(di * tr - dr * ti for dr, di, tr, ti in pairs)
    power = sum(tr * tr + ti * ti for dr, di, tr, ti in pairs) + damping
    return cross_real / power, cross_imag / power


def gradient_of(data, transfer, est, weight):
    er, ei = est
    double = -2.0 * weight
    grads = []
    for d, t in zip(data, transfer):
        tr, ti = t[:, :LANES], t[:, LANES:]
        mr = d[:, :LANES] - (er * tr - ei * ti)
        mi = d[:, LANES:] - (er * ti + ei * tr)
        grads.append(
            jnp.concatenate([double * (er * mr + ei * mi), double * (er * mi - ei * mr)], axis=1)
        )
    return grads


def back_to_pupil(scale, frames, patches, tc2_ref, tf2_ref, tg1_ref, tg2_ref, grads_ref, focal_ref, rows_ref, back_ref, work_ref):
    items = frames * patches
    rows_ref[...] = right_t(grads_ref[...], tc2_ref)

    def spread_stage(p, inside):
        cols = []
        for f in inside:
            rows = item_rows(f * patches + p)
            cols.append(jnp.concatenate([rows_ref[rows, :LANES], rows_ref[rows, LANES:]], axis=0))
        spread = left_rows(tf2_ref, pair_up(cols)[0]) * (2.0 * scale)
        fields = []
        for k, f in enumerate(inside):
            one = spread[:, k * LANES : (k + 1) * LANES]
            fields.append(focal_ref[f * patches + p] * jnp.concatenate([one, one], axis=0))
        return pair_up(fields)[0]

    def pupil_stage(p, inside, field):
        pupil = left_rows(tg1_ref, field)
        for k, f in enumerate(inside):
            lanes = slice(k * LANES, (k + 1) * LANES)
            rows = item_rows(f * patches + p)
            work_ref[rows, :LANES] = pupil[:BOX, lanes]
            work_ref[rows, LANES:] = pupil[BOX:, lanes]

    staggered(frames, patches, spread_stage, pupil_stage)
    high, low = split(work_ref[...])
    first = mm(high, tg2_ref[...])
    back = first[:, :LANES] + first[:, LANES:] + mm(low, tg2_ref[:, :LANES])
    for item in range(items):
        back_ref[pl.ds(item, BOX, stride=items), :] = back[item * BOX : (item + 1) * BOX]


def coefficient_gradient(items, z_ref, pupil_ref, back_ref):
    lower = lax.broadcasted_iota(jnp.int32, (items, LANES), 1) < 64

    def two_rows(i, total):
        sides = []
        for k in range(2):
            rows = pl.ds(pl.multiple_of((2 * i + k) * items, 8), items)
            product = pupil_ref[rows, :] * back_ref[rows, :]
            sides.append(product + pltpu.roll(product, 64, 1))
        high, low = split(jnp.where(lower, sides[0], sides[1]))
        return total + mm_t(jnp.concatenate([high, low], axis=0), z_ref[i])

    total = lax.fori_loop(
        0, BOX // 2, two_rows, jnp.zeros((2 * items, 2 * MPAD), f32), unroll=4
    )
    total = total[:items] + total[items:]
    total = jnp.concatenate([total, jnp.zeros((items, LANES - 2 * MPAD), f32)], axis=1)
    total = total + pltpu.roll(total, LANES - MPAD, 1)
    lane = lax.broadcasted_iota(jnp.int32, total.shape, 1)
    return jnp.where(lane < MPAD, total, 0.0)


def unpack_pixels(packed):
    lane = lax.broadcasted_iota(jnp.int32, (PACK - 40, LANES), 1)
    third = jnp.concatenate(
        [pltpu.roll(packed[48:56], LANES - 8 - 8 * t, 1) for t in range(3)], axis=0
    )
    rest = jnp.where(
        lane < 40,
        pltpu.roll(packed[:24], 40, 1),
        jnp.where(lane < 80, pltpu.roll(packed[24:48], 80, 1), third),
    )
    return jnp.concatenate([packed, rest], axis=0)


def padded(patches):
    return -(-patches // 8) * 8


def starting_values(start, chunk, patches):
    rows = pl.ds(pl.multiple_of(chunk * padded(patches), 8), padded(patches))
    current = jnp.concatenate([s[rows, :][:patches] for s in start], axis=0)
    lane = lax.broadcasted_iota(jnp.int32, current.shape, 1)
    return jnp.where(lane < MPAD, current, 0.0)


def first_kernel(scale, frames, patches, chunk, *refs):
    start = refs[:frames]
    z_ref, mask_ref, ta_ref, tb_ref, tc1_ref, tc2_ref = refs[frames : frames + 6]
    pupil_ref, focal_ref, transfer_ref, cols_ref, rows_ref = refs[frames + 6 :]
    pupils([starting_values(start, chunk, patches)], z_ref, mask_ref, [pupil_ref])
    columns(pupil_ref, ta_ref, cols_ref)
    transfers(
        scale, frames, patches, tb_ref, tc1_ref, tc2_ref, cols_ref, focal_ref, rows_ref, transfer_ref
    )


def middle_kernel(scale, frames, patches, chunk_ref, *refs):
    chunk = chunk_ref[0]
    start = refs[:frames]
    pixels = refs[frames : 2 * frames]
    pupil_ref, focal_ref, transfer_ref = refs[2 * frames : 2 * frames + 3]
    (
        z_ref,
        mask_ref,
        ta_ref,
        tb_ref,
        tc1_ref,
        tc2_ref,
        tf2_ref,
        tg1_ref,
        tg2_ref,
        window_ref,
        weight_ref,
        freq_ref,
    ) = refs[2 * frames + 3 : 2 * frames + 15]
    (
        estimate_out,
        current_out,
        energy_out,
        pupil_out,
        focal_out,
        grads_out,
        data_ref,
        cols_ref,
        back_ref,
        ramp_ref,
        rows_ref,
    ) = refs[2 * frames + 15 :]
    items = frames * patches
    for f in range(frames):
        s = start[f][pl.ds(0, 1), :]
        angle = freq_ref[0] * s[:, MPAD : MPAD + 1] + freq_ref[1] * s[:, MPAD + 1 : MPAD + 2]
        ramp_ref[f, :, :LANES] = sine(angle, 0.5)
        ramp_ref[f, :, LANES:] = sine(angle, 0.0)
    back_args = (tc2_ref, tf2_ref, tg1_ref, tg2_ref)

    def pixel_rows(p, carry):
        window = window_ref[...]
        for inside in frame_pairs(frames):
            planes = [unpack_pixels(pixels[f][p]) * window for f in inside]
            half_rows(pair_up(planes)[0], inside, patches, p, tc1_ref, rows_ref)
        return carry

    lax.fori_loop(0, patches, pixel_rows, 0)
    data_ref[...] = right(rows_ref[...], tc2_ref)

    def first_gradient(p, carry):
        weight = weight_ref[...]
        data = []
        total = None
        for f in range(frames):
            rows = item_rows(f * patches + p)
            real, imag = data_ref[rows, :LANES], data_ref[rows, LANES:]
            cr, ci = ramp_ref[f, :, :LANES], ramp_ref[f, :, LANES:]
            dr, di = real * cr - imag * ci, real * ci + imag * cr
            both = jnp.concatenate([dr, di], axis=1)
            data.append(both)
            data_ref[rows, :] = both
            part = weight * (dr * dr + di * di)
            total = part if total is None else total + part
        energy = jnp.sum(jnp.sum(total, axis=0, keepdims=True), axis=1, keepdims=True)
        for f in range(frames):
            energy_out[pl.ds(f * patches + p, 1), :] = jnp.broadcast_to(energy, (1, LANES))
        transfer = [transfer_ref[item_rows(f * patches + p), :] for f in range(frames)]
        grads = gradient_of(data, transfer, estimate_of(data, transfer), weight)
        for f in range(frames):
            grads_out[item_rows(f * patches + p), :] = grads[f]
        return carry

    lax.fori_loop(0, patches, first_gradient, 0)
    back_to_pupil(scale, frames, patches, *back_args, grads_out, focal_ref, rows_ref, back_ref, grads_out)
    grad = coefficient_gradient(items, z_ref, pupil_ref, back_ref)
    current = starting_values(start, chunk, patches)
    current = current - step_size * frames * grad / energy_out[...]
    current_out[...] = current
    pupils([current], z_ref, mask_ref, [pupil_out])
    columns(pupil_out, ta_ref, cols_ref)
    transfers(
        scale, frames, patches, tb_ref, tc1_ref, tc2_ref, cols_ref, focal_out, rows_ref, grads_out
    )

    def next_gradient(p, carry):
        rows = [item_rows(f * patches + p) for f in range(frames)]
        transfer = [grads_out[r, :] for r in rows]
        data = [data_ref[r, :] for r in rows]
        est = estimate_of(data, transfer)
        estimate_out[p, 0] = est[0] * (1.0 / PATCH)
        estimate_out[p, 1] = est[1] * (1.0 / PATCH)
        grads = gradient_of(data, transfer, est, weight_ref[...])
        for f in range(frames):
            grads_out[rows[f], :] = grads[f]
        return carry

    lax.fori_loop(0, patches, next_gradient, 0)


def last_kernel(scale, frames, patches, chunks, order_ref, *refs):
    states = [refs[5 * c : 5 * c + 5] for c in range(chunks)]
    z_ref, tc2_ref, tf2_ref, tg1_ref, tg2_ref = refs[5 * chunks : 5 * chunks + 5]
    outs = refs[5 * chunks + 5 : 5 * chunks + 5 + frames]
    back_ref, rows_ref, work_ref, final_ref = refs[5 * chunks + 5 + frames :]
    items = frames * patches

    for f in range(frames):
        outs[f][...] = jnp.zeros(outs[f].shape, f32)
    for c in range(chunks):
        current_ref, energy_ref, pupil_ref, focal_ref, grads_ref = states[c]
        back_to_pupil(
            scale, frames, patches, tc2_ref, tf2_ref, tg1_ref, tg2_ref, grads_ref, focal_ref, rows_ref, back_ref, work_ref
        )
        grad = coefficient_gradient(items, z_ref, pupil_ref, back_ref)
        final_ref[...] = current_ref[...] - step_size * frames * grad / energy_ref[...]
        for j in range(patches):
            p = order_ref[c * patches + j]
            for f in range(frames):
                row = f * patches + j
                outs[f][pl.ds(p, 1), :] = final_ref[row : row + 1, :]


def slot_of(axes, me, strip, group, rank):
    frames, strips = axes
    chunks = strips // frames
    owner = lax.div(group, chunks)
    chunk = lax.rem(group + strip, chunks)
    relative = lax.rem(owner - me + frames, frames)
    return relative * chunks + chunk, rank


def prepare_kernel(axes, count, assign_ref, shifts_ref, coefs_ref, *refs):
    frames = axes[0]
    outs = refs[:frames]
    order_ref, sorted_ref, counts_ref = refs[frames:]
    modes = coefs_ref.shape[-1]
    per = count // axes[1]
    room = padded(per)
    me = lax.axis_index("frm")
    strip = lax.axis_index("pat")
    for g in range(axes[1]):
        counts_ref[g] = 0

    def one(p, carry):
        group = assign_ref[p]
        rank = counts_ref[group]
        counts_ref[group] = rank + 1
        piece, place = slot_of(axes, me, strip, group, rank)
        order_ref[piece * per + place] = p
        sorted_ref[pl.ds(piece * room + place, 1), :modes] = coefs_ref[pl.ds(p, 1), :]
        return carry

    sorted_ref[...] = jnp.zeros(sorted_ref.shape, f32)
    lax.fori_loop(0, count, one, 0)
    rows_each = sorted_ref.shape[0] // frames
    lane = lax.broadcasted_iota(jnp.int32, (rows_each, LANES), 1)
    for f in range(frames):
        rows = sorted_ref[f * rows_each : (f + 1) * rows_each, :]
        rows = jnp.where(lane == MPAD, shifts_ref[0, 0], rows)
        outs[f][...] = jnp.where(lane == MPAD + 1, shifts_ref[0, 1], rows)


def cut_kernel(axes, count, chunk, order_ref, anchors_ref, strip_ref, below_ref, *refs):
    frames, strips = axes
    outs, (tall_ref,) = refs[:frames], refs[frames:]
    patches = count // strips
    chunks = strips // frames
    height, width = strip_ref.shape
    tall_ref[:height, :width] = strip_ref[...]
    tall_ref[height : height + PATCH, :width] = below_ref[...]
    first = lax.axis_index("pat") * height

    lane = lax.broadcasted_iota(jnp.int32, (24, LANES), 1)
    for f in range(frames):

        def one(j, carry):
            p = order_ref[(f * chunks + chunk) * patches + j]
            row = anchors_ref[p, 0] - first
            col = anchors_ref[p, 1]
            tile = lax.div(col, LANES)
            base = pl.multiple_of(tile * LANES, LANES)
            above = pl.multiple_of(lax.div(row, 8) * 8, 8)
            block = tall_ref[pl.ds(above, FULL), pl.ds(base, 2 * LANES)]
            back = lax.rem(2 * LANES - (col - base), 2 * LANES)
            block = pltpu.roll(block, back, 1)[:, :LANES]
            block = pltpu.roll(block, lax.rem(FULL - (row - above), FULL), 0)[:PATCH]
            rest = block[PACK:]
            outs[f][j, 0:24, :] = jnp.where(lane < 88, block[0:24], pltpu.roll(rest, 88, 1))
            outs[f][j, 24:48, :] = jnp.where(lane < 88, block[24:48], pltpu.roll(rest, 48, 1))
            third = jnp.where(
                lane[:8] < 96,
                pltpu.roll(rest[:8], 8, 1),
                jnp.where(
                    lane[:8] < 104, pltpu.roll(rest[8:16], 16, 1), pltpu.roll(rest[16:24], 24, 1)
                ),
            )
            outs[f][j, 48:56, :] = jnp.where(lane[:8] < 88, block[48:56], third)
            outs[f][j, 56:64, :] = block[56:64]
            return carry

        lax.fori_loop(0, patches, one, 0, unroll=2)


def call(body, outs, scratch, operands, smem=0, micros=1, after=(), order=0):
    vmem = pl.BlockSpec(memory_space=pltpu.VMEM)
    scalar = pl.BlockSpec(memory_space=pltpu.SMEM)
    whole = pl.BlockSpec(memory_space=pl.ANY)

    def ordered(*refs):
        body(*refs[: len(operands)], *refs[len(operands) + len(after) :])

    return pl.pallas_call(
        ordered,
        out_shape=[jax.ShapeDtypeStruct(s, f32) for s in outs]
        + [jax.ShapeDtypeStruct((order,), jnp.int32)] * bool(order),
        in_specs=[scalar] * smem + [vmem] * (len(operands) - smem) + [whole] * len(after),
        out_specs=[vmem] * len(outs) + [scalar] * bool(order),
        scratch_shapes=scratch,
        cost_estimate=pl.CostEstimate(
            flops=int(micros * 1e9), bytes_accessed=1 << 20, transcendentals=0
        ),
        compiler_params=pltpu.CompilerParams(vmem_limit_bytes=VMEM_LIMIT),
    )(*operands, *after)


def around(value, axis, steps):
    count = lax.axis_size(axis)
    return lax.ppermute(value, axis, [(s, (s + steps) % count) for s in range(count)])


def assemble(half):
    mid = PATCH // 2
    top = half[:, :, : mid + 1, :PATCH]
    nyquist = half[:, :, 1:mid, PATCH : PATCH + 1]
    low = jnp.flip(half[:, :, 1:mid, :PATCH], axis=2)
    low_nyquist = jnp.flip(nyquist, axis=2)
    low = jnp.concatenate(
        [low[..., :1], jnp.flip(low[..., mid + 1 :], axis=3), low_nyquist, jnp.flip(low[..., 1:mid], axis=3)],
        axis=3,
    )
    low = low * jnp.array([1.0, -1.0], f32)[None, :, None, None]
    spectra = jnp.concatenate([top, low], axis=2)
    return spectra.reshape(spectra.shape[0], 2, PATCH * PATCH)


def shards(frames, shifts, coefficients, anchors, assign):
    t = tables()
    scale = t["scale"]
    c = {k: jnp.asarray(v) for k, v in t.items() if k != "scale"}
    height = frames.shape[1]
    width = frames.shape[2]
    count = assign.shape[0]
    n_frm = lax.axis_size("frm")
    n_pat = lax.axis_size("pat")
    axes = (n_frm, n_pat)
    chunks = n_pat // n_frm
    per = count // n_pat
    items = n_frm * per

    upper = frames[0, :PATCH, :]
    below = lax.ppermute(upper, "pat", [(s, s - 1) for s in range(1, n_pat)])
    ready = call(
        functools.partial(prepare_kernel, axes, count),
        [(chunks * padded(per), LANES)] * n_frm,
        [pltpu.VMEM((n_pat * padded(per), LANES), f32), pltpu.SMEM((n_pat,), jnp.int32)],
        [assign, shifts, coefficients[0]],
        smem=2,
        order=count,
        after=[upper],
    )
    order = ready[n_frm]
    start = [ready[0]] + [around(ready[r], "frm", r) for r in range(1, n_frm)]

    state = [(BOX * items, LANES), (items, 2 * PATCH, LANES), (items * HALF, 2 * LANES)]
    wide = pltpu.VMEM((items * HALF, 2 * LANES), f32)

    def cut(k, after):
        pieces = call(
            functools.partial(cut_kernel, axes, count, k),
            [(per, PACK, LANES)] * n_frm,
            [pltpu.VMEM((height + PATCH, width + LANES), f32)],
            [order, anchors, frames[0], below],
            smem=2,
            micros=3,
            after=after,
        )
        sent = [pieces[0]]
        for r in range(1, n_frm):
            sent.append(around(pieces[r], "frm", r))
        return pieces, sent

    def first_pass(k, after):
        return call(
            functools.partial(first_kernel, scale, n_frm, per, k),
            state,
            [pltpu.VMEM((2, BOX * items, LANES), f32), wide],
            start + [c[name] for name in ("z", "mask", "ta", "tb", "tc1", "tc2")],
            micros=4,
            after=after,
        )

    first = first_pass(0, [])
    pixels = []
    for k in range(chunks):
        pieces, sent = cut(k, [first[3 * k + 2]])
        pixels.append(sent)
        if k + 1 < chunks:
            first += first_pass(k + 1, [pieces[0]])

    halves = []
    states = []
    after = []
    for k in range(chunks):
        result = call(
            functools.partial(middle_kernel, scale, n_frm, per),
            [(per, 2, HALF, LANES), (items, LANES), (items, LANES)] + state,
            [
                wide,
                pltpu.VMEM((2, BOX * items, LANES), f32),
                pltpu.VMEM((BOX * items, LANES), f32),
                pltpu.VMEM((n_frm, HALF, 2 * LANES), f32),
                wide,
            ],
            [jnp.full((1,), k, jnp.int32)]
            + start
            + pixels[k]
            + list(first[3 * k : 3 * k + 3])
            + [
                c[name]
                for name in (
                    "z", "mask", "ta", "tb", "tc1", "tc2", "tf2", "tg1", "tg2",
                    "window", "weight", "freq",
                )
            ],
            smem=1,
            micros=12,
            after=after,
        )
        after = [result[2]]
        states += list(result[1:])
        halves.append(send_estimates(axes, k, result[0]))
    finals = call(
        functools.partial(last_kernel, scale, n_frm, per, chunks),
        [(count, LANES)] * n_frm,
        [pltpu.VMEM((BOX * items, LANES), f32), wide, wide, pltpu.VMEM((items, LANES), f32)],
        [order] + states + [c[k] for k in ("z", "tc2", "tf2", "tg1", "tg2")],
        smem=1,
        micros=9,
    )
    parts = [finals[0]]
    for r in range(1, n_frm):
        parts.append(around(finals[r], "frm", -r))
    new_coefficients = sum(parts)[None, :, : coefficients.shape[2]]
    object_spectra = assemble(in_order(axes, halves))
    return (new_coefficients, object_spectra)


def send_estimates(axes, k, estimate):
    n_frm, n_pat = axes
    chunks = n_pat // n_frm
    pairs = []
    for f in range(n_frm):
        for s in range(n_pat):
            group = chunks * f + (s + k) % chunks
            pairs.append((f * n_pat + s, (s // chunks) * n_pat + group))
    return lax.ppermute(estimate, ("frm", "pat"), pairs)


def in_order(axes, halves):
    n_frm, n_pat = axes
    chunks = n_pat // n_frm
    side = lax.rem(lax.axis_index("pat"), chunks)
    begin = lax.rem(2 * chunks - 1 - side, chunks)
    stacked = jnp.stack(halves[::-1] * 2)
    ordered = lax.dynamic_slice_in_dim(stacked, begin, chunks, 0)
    return ordered.reshape((-1,) + halves[0].shape[1:])


def solution(mesh):
    in_specs = (
        P("frm", "pat", None),
        P("frm", None),
        P("frm", "pat", None),
        P("pat", None),
        P("pat"),
    )
    out_specs = (P("frm", "pat", None), P(("pat", "frm"), None, None))

    return jax.shard_map(shards, mesh=mesh, in_specs=in_specs, out_specs=out_specs, check_vma=False)
```
